32 devices in a mesh: fsdp: 2 (over x), ctx: 4 (over y, core), tp: 4 (over z).
Axes of the slice: x: 2, y: 2, z: 4, core: 2. Of those that a mesh axis runs over, the one named last changes fastest.
Arguments:
- tokens: bfloat16 [8, 512, 768], P(('fsdp', 'tp'), 'ctx'), may hold values from -6 to 6
- seg_ids: int32 [8, 512], P(('fsdp', 'tp')), may hold values from 0 to 2, never falling along the last dimension, each value on 1 to 384 neighbouring positions
- routes: int32 [8, 512, 2], P(('fsdp', 'tp'), 'ctx'), may hold values from 0 to 3, all different within a row; in each aligned block of 128 rows (0 to 127, 128 to 255, ..., all dimensions but the last counted through in order) at most 80 rows name the same one
- norm_attn: bfloat16 [768], P('fsdp'), may hold values from 0.5 to 1.5
- weight_qkv: bfloat16 [768, 2304], P('fsdp'), may hold values from -0.21875 to 0.21875
- weight_proj: bfloat16 [768, 768], P(None, 'fsdp'), may hold values from -0.875 to 0.875
- rel_table: float32 [12, 32], replicated, may hold values from -4 to 4
- norm_ffn: bfloat16 [768], P('fsdp'), may hold values from 0.5 to 1.5
- weight_router: bfloat16 [768, 4], P('fsdp'), may hold values from -0.21875 to 0.21875
- expert_up: bfloat16 [4, 768, 3072], P(None, 'fsdp', ('ctx', 'tp')), may hold values from -0.21875 to 0.21875
- expert_down: bfloat16 [4, 3072, 768], P(None, ('ctx', 'tp'), 'fsdp'), may hold values from -0.109375 to 0.109375
- cotangent: bfloat16 [8, 512, 768], P(('fsdp', 'tp'), 'ctx'), may hold values from -6 to 6
Outputs:
- output: bfloat16 [8, 512, 768], P(('fsdp', 'tp'), 'ctx')
- grad_tokens: float32 [8, 512, 768], P(('fsdp', 'tp'), 'ctx')
- grad_norm_attn: float32 [768], P('fsdp')
- grad_weight_qkv: float32 [768, 2304], P('fsdp')
- grad_weight_proj: float32 [768, 768], P(None, 'fsdp')
- grad_rel_table: float32 [12, 32], replicated
- grad_norm_ffn: float32 [768], P('fsdp')
- grad_weight_router: float32 [768, 4], P('fsdp')
- grad_expert_up: float32 [4, 768, 3072], P(None, 'fsdp', ('ctx', 'tp'))
- grad_expert_down: float32 [4, 3072, 768], P(None, ('ctx', 'tp'), 'fsdp')
The draws below stay inside these ranges and needn't reach their ends.
Inputs may be any that keep to these rules, and one draw needn't show every extreme that they name: `seg_ids`: each group's 512 positions fall into at most 3 sequences whose numbers never fall along the positions; the longest has exactly 384 positions. `routes`: each token names two different experts. In each aligned block of 128 rows (the rows of one device) no expert is named more than 80 times, and in every draw some expert is named exactly 80 times in some block.
All inputs are finite; a program needn't handle non-finite values.
Results may differ from the reference program's by a relative error of at most 0.012.
Values may be sent and summed in bfloat16 or wider, within the bound.
A program may use at most 192 MiB of HBM per device.

```python
import math
from functools import partial
import jax
import jax.numpy as jnp
import numpy as np
from jax import lax

D = 768
HEADS = 12
HD = 64
FF = 3072
EXPERTS = 4
TOP = 2
BUCKETS = 32
MAX_DISTANCE = 128
SEGS = 3
TOK_DEV = 128
MOST = 80
GROUP_LEN = 512
SEG_MOST = 384
GROUPS = 8


def spiked(entries, stream_key, source, target, parts, factor):
    def block_of(dim):
        return (jnp.arange(entries.shape[dim]) // (entries.shape[dim] // parts)).reshape((-1,) + (1,) * (entries.ndim - 1 - dim))

    first = jax.random.permutation(stream_key, parts)[block_of(target)]
    second = (block_of(target) + parts // 2) % parts
    return jnp.where((block_of(source) == first) | (block_of(source) == second), factor * entries, entries)


def shard_levels(rng, shape, cuts, smallest, largest):
    def one(dim, parts):
        steps = jax.random.uniform(jax.random.fold_in(jax.random.fold_in(rng, 6), dim), (parts,), jnp.float32, smallest / len(cuts), largest / len(cuts))
        return jnp.repeat(jnp.exp(steps), shape[dim] // parts).reshape((-1,) + (1,) * (len(shape) - dim - 1))

    level = one(*cuts[0])
    for cut in cuts[1:]:
        level = level * one(*cut)
    return level


def split_up(number_of, total, most, skew):
    portions = [(1 << 20) // math.isqrt(grade ** skew) + 1 for grade in range(2, number_of + 1)]
    spare, counts = total - most - (number_of - 1), [1] * (number_of - 1)
    while spare > 0:
        free = [i for i in range(number_of - 1) if counts[i] < most]
        whole, left = sum([portions[i] for i in free]), spare
        for i in free:
            extra = min(most - counts[i], max(1, left * portions[i] // whole), spare)
            counts[i] = counts[i] + extra
            spare = spare - extra
    return np.array([most] + counts)


def uneven(rng, count, total, bound, skew):
    if count == 2:
        one = jax.random.randint(rng, (), max(1, total - bound), min(bound, total - 1) + 1)
        return jnp.stack([one, total - one])
    tallies = jnp.asarray(split_up(count, total, bound, skew), jnp.int32)
    pairs = (count - 1) // 2
    donor, receiver = tallies[1:1 + 2 * pairs:2], tallies[2:2 + 2 * pairs:2]
    margin = jnp.minimum(donor - 1, bound - receiver)
    shifted = jax.random.randint(jax.random.fold_in(rng, 1), (pairs,), 0, 1 << 20) % (margin + 1)
    tallies = tallies.at[1:1 + 2 * pairs:2].set(donor - shifted).at[2:2 + 2 * pairs:2].set(receiver + shifted)
    return tallies[jax.random.permutation(jax.random.fold_in(rng, 2), count)]


def assign_block(stream_key, own, number, rows, amount, top, bound, skew):
    sequence = jax.random.permutation(stream_key, amount)
    heavy_load, usual = shares(amount, rows * top, bound, skew, True), shares(amount, rows * top, bound, skew, False)
    places = jnp.arange(amount)

    def named(lengths, rotation):
        used = int((lengths > 0).sum())
        fixed = max(1, used // 4)
        passed = fixed + (places - fixed + rotation * (used - fixed)) % max(1, amount - fixed)
        return jnp.zeros((amount,), jnp.int32).at[sequence[jnp.where(places < fixed, places, passed)]].set(jnp.asarray(lengths, jnp.int32))

    lengths = jnp.where(number % 4 == 0, named(heavy_load, number // 4), named(usual, number - number // 4 - 1))
    mixed = jax.random.permutation(jax.random.fold_in(own, 3), amount)
    donor, taker = mixed[0:amount // 2 * 2:2], mixed[1:amount // 2 * 2:2]
    margin = jnp.minimum(lengths[donor] - 1, bound - lengths[taker]) // 2
    margin = jnp.where((donor == sequence[0]) | (taker == sequence[0]) | (lengths[taker] == 0), 0, jnp.maximum(margin, 0))
    passed = jax.random.randint(jax.random.fold_in(own, 4), (amount // 2,), 0, 1 << 20) % (margin + 1)
    lengths = lengths.at[donor].add(-passed).at[taker].add(passed)
    items = jnp.searchsorted(jnp.cumsum(lengths), jnp.arange(rows * top), side="right").astype(jnp.int32)
    grid = items.reshape(top, rows).T
    grid = grid[jax.random.permutation(jax.random.fold_in(own, 1), rows)]
    rotation = jax.random.randint(jax.random.fold_in(own, 2), (rows, 1), 0, top)
    return jnp.take_along_axis(grid, (jnp.arange(top)[None, :] + rotation) % top, axis=1)


def shares(count, total, bound, skew, full):
    loads = [(1 << 20) // math.isqrt(rank ** skew) + 1 for rank in range(1, count + 1)]
    largest = bound if full else min(bound, max(-(-total // count), total * loads[0] // sum(loads)))
    least = 1 if total - largest >= count - 1 else 0
    given, spare = [largest] + [least] * (count - 1), total - largest - least * (count - 1)
    while spare > 0:
        candidates = [i for i in range(1, count) if given[i] < largest] or [i for i in range(1, count) if given[i] < bound]
        whole, budget = sum([loads[i] for i in candidates]), spare
        for i in candidates:
            extra = min(bound - given[i], max(1, budget * loads[i] // whole), spare)
            given[i] = given[i] + extra
            spare = spare - extra
    return np.array(given)


def noise(stream_key, dims, deviation, limit, split=(), kind=jnp.bfloat16):
    level = shard_levels(stream_key, dims, split, -0.22, 0.18) if split else 1.0
    values = jax.random.normal(stream_key, dims, jnp.float32) * deviation * level
    return jnp.minimum(jnp.maximum(values, -limit), limit).astype(kind)


def gaussian_with(key, extent, deviation, bound, split, heavy, held_as=jnp.bfloat16):
    entries = deviation * jax.random.normal(key, extent, jnp.float32)
    if split:
        entries = entries * shard_levels(key, extent, split, -0.22, 0.18)
    return jnp.clip(spiked(entries, jax.random.fold_in(key, 3), *heavy), -bound, bound).astype(held_as)


def setup_inputs(seed: int = 0) -> dict:
    keys = jax.random.split(jax.random.key(seed), 13)
    tokens = noise(keys[0], (GROUPS, GROUP_LEN, D), 1.0, 6.0, ((0, 8), (1, 4)))
    seg_ids = jax.vmap(lambda own: jnp.searchsorted(jnp.cumsum(uneven(own, SEGS, GROUP_LEN, SEG_MOST, 2)), jnp.arange(GROUP_LEN), side="right"))(jax.random.split(keys[1], GROUPS)).reshape((GROUPS, GROUP_LEN)).astype(jnp.int32)
    routes_keys = jax.random.split(jax.random.fold_in(keys[2], 1), GROUPS * GROUP_LEN // TOK_DEV)
    routes_turns = jax.random.permutation(jax.random.fold_in(keys[2], 3), GROUPS * GROUP_LEN // TOK_DEV)
    routes = jax.vmap(lambda own, number: assign_block(jax.random.fold_in(keys[2], 2), own, number, TOK_DEV, EXPERTS, TOP, MOST, 1))(routes_keys, routes_turns).reshape((GROUPS, GROUP_LEN, TOP))
    norm_attn = jnp.clip(1.0 + 0.1 * jax.random.normal(keys[3], (D,), jnp.float32), 0.5, 1.5).astype(jnp.bfloat16)
    weight_qkv = noise(keys[4], (D, 3 * D), D ** -0.5, 0.21875, ((0, 2),))
    weight_proj = noise(keys[5], (D, D), (D // 16) ** -0.5, 0.875, ((1, 2),))
    rel_table = noise(keys[6], (HEADS, BUCKETS), 1.0, 4.0, (), jnp.float32)
    norm_ffn = jnp.clip(1.0 + 0.1 * jax.random.normal(keys[7], (D,), jnp.float32), 0.5, 1.5).astype(jnp.bfloat16)
    weight_router = noise(keys[8], (D, EXPERTS), D ** -0.5, 0.21875, ((0, 2),))
    expert_up = noise(keys[9], (EXPERTS, D, FF), D ** -0.5, 0.21875, ((1, 2), (2, 16)))
    expert_down = noise(keys[10], (EXPERTS, FF, D), FF ** -0.5, 0.109375, ((1, 16), (2, 2)))
    cotangent = gaussian_with(keys[11], (GROUPS, GROUP_LEN, D), 1.0, 6.0, ((0, 8), (1, 4)), (0, 2, 8, 2.0))
    return {"tokens": tokens, "seg_ids": seg_ids, "routes": routes, "norm_attn": norm_attn, "weight_qkv": weight_qkv, "weight_proj": weight_proj, "rel_table": rel_table, "norm_ffn": norm_ffn, "weight_router": weight_router, "expert_up": expert_up, "expert_down": expert_down, "cotangent": cotangent}


EPSILON = 1e-06
MASK_FILL = -1e+30

@jax.custom_vjp
def low(v):
    return lax.optimization_barrier(v.astype(jnp.bfloat16)).astype(jnp.float32)

@jax.custom_vjp
def low_back(v):
    return v

def low_keep(v):
    return (low(v), None)

def low_pass(kept, grad):
    return (grad,)

def back_keep(v):
    return (v, None)

def back_low(kept, grad):
    return (low(grad),)
low.defvjp(low_keep, low_pass)
low_back.defvjp(back_keep, back_low)

def bucket_bounds(buckets, far_reach):
    exact_count = buckets // 2
    bounds = []
    for number in range(1, buckets):
        if number <= exact_count:
            bounds.append(number)
        else:
            exponent = (number - exact_count) / (buckets - exact_count)
            bounds.append(int(np.ceil(exact_count * (far_reach / exact_count) ** exponent)))
    return np.array(bounds, dtype=np.int32)

def slot_tables(route_ids, experts, capacity):
    flat_ids = route_ids.reshape(-1)
    assignments = flat_ids.shape[0]
    member = (flat_ids[:, None] == jnp.arange(experts, dtype=jnp.int32)[None, :]).astype(jnp.int32)
    before = jnp.cumsum(member, axis=0) - member
    slot_index = lax.optimization_barrier(jnp.sum(before * member, axis=1))
    position = slot_index * experts + flat_ids
    filler = jnp.full((capacity * experts,), assignments, jnp.int32).at[position].set(jnp.arange(assignments, dtype=jnp.int32))
    return (position, filler)

def take_rows(table_rows, indices):
    return table_rows[indices]

def rms_norm(values, gain):
    return values * lax.rsqrt(lax.optimization_barrier(jnp.mean(values * values, axis=-1, keepdims=True)) + EPSILON) * gain

def forward(tokens, norm_attn, weight_qkv, weight_proj, rel_table, norm_ffn, weight_router, expert_up, expert_down, seg_ids, routes):
    highest = lax.Precision.HIGHEST
    token_total = GROUPS * GROUP_LEN
    inputs = tokens.reshape(token_total, D)
    normed_one = low(rms_norm(inputs, norm_attn))
    projected = low_back(low(jnp.dot(normed_one, weight_qkv, precision=highest)))
    by_group = projected.reshape(GROUPS, GROUP_LEN, 3, HEADS, HD)
    positions = jnp.arange(GROUP_LEN, dtype=jnp.int32)
    distance = jnp.maximum(positions[:, None] - positions[None, :], 0)
    bounds = jnp.asarray(bucket_bounds(BUCKETS, MAX_DISTANCE))
    which_bucket = lax.optimization_barrier(jnp.sum((distance[:, :, None] >= bounds[None, None, :]).astype(jnp.int32), axis=2))

    def one_group(pieces):
        group_qkv, segment = pieces
        products = jnp.einsum('qhd,khd->hqk', group_qkv[:, 0], group_qkv[:, 1], precision=highest)
        scores = low_back(products * HD ** (-0.5) + rel_table[:, which_bucket])
        allowed = (segment[:, None] == segment[None, :]) & (positions[:, None] >= positions[None, :])
        probs = low(jax.nn.softmax(jnp.where(allowed[None], scores, MASK_FILL), axis=-1))
        return low_back(low(jnp.einsum('hqk,khd->qhd', probs, group_qkv[:, 2], precision=highest)))
    attended = lax.map(jax.checkpoint(one_group), (by_group, seg_ids))
    mixed_heads = attended.reshape(token_total, D)
    attention = low_back(jnp.dot(mixed_heads, weight_proj, precision=highest))
    middle = inputs + attention
    normed_two = low(rms_norm(middle, norm_ffn))
    logits = jnp.dot(normed_two, weight_router, precision=highest)
    route_rows = routes.reshape(token_total, TOP)
    gate_weights = jax.nn.softmax(jnp.take_along_axis(logits, route_rows, axis=1), axis=-1)
    block_count = token_total // TOK_DEV
    position, filler = jax.vmap(partial(slot_tables, experts=EXPERTS, capacity=MOST))(routes.reshape(block_count, TOK_DEV, TOP))
    offsets = (jnp.arange(block_count, dtype=jnp.int32) * TOK_DEV)[:, None]
    owner = jnp.where(filler < 2 * TOK_DEV, offsets + filler // 2, token_total)
    padded_rows = jnp.concatenate([normed_two, jnp.zeros((1, D), jnp.float32)], axis=0)
    dispatched = padded_rows[owner].reshape(block_count * MOST, EXPERTS, D)
    by_expert = jnp.transpose(dispatched, (1, 0, 2))

    def one_expert(pieces):
        expert_rows, up_matrix, down_matrix = pieces
        pre_act = low_back(jnp.dot(expert_rows, up_matrix, precision=highest))
        activated = low(jax.nn.gelu(pre_act))
        return low_back(jnp.dot(activated, down_matrix, precision=highest))
    expert_result = lax.map(jax.checkpoint(one_expert), (by_expert, expert_up, expert_down))
    slot_result = jnp.transpose(expert_result, (1, 0, 2)).reshape(block_count, MOST * EXPERTS, D)
    per_choice = jax.vmap(take_rows)(slot_result, position).reshape(token_total, TOP, D)
    result = middle + lax.optimization_barrier(jnp.sum(gate_weights[:, :, None] * per_choice, axis=1))
    return result.reshape(GROUPS, GROUP_LEN, D)

def reference(tokens, seg_ids, routes, norm_attn, weight_qkv, weight_proj, rel_table, norm_ffn, weight_router, expert_up, expert_down, cotangent):
    floats = (tokens.astype(jnp.float32), norm_attn.astype(jnp.float32), weight_qkv.astype(jnp.float32), weight_proj.astype(jnp.float32), rel_table.astype(jnp.float32), norm_ffn.astype(jnp.float32), weight_router.astype(jnp.float32), expert_up.astype(jnp.float32), expert_down.astype(jnp.float32))

    def closed(*arrays):
        return forward(*arrays, seg_ids, routes)
    result, pullback = jax.vjp(closed, *floats)
    gradients = pullback(cotangent.astype(jnp.float32))
    return (result.astype(jnp.bfloat16), gradients[0], gradients[1], gradients[2], gradients[3], gradients[4], gradients[5], gradients[6], gradients[7], gradients[8])
```

```python
import jax
import jax.numpy as jnp
import numpy as np
from jax import lax
from jax.experimental import pallas as pl
from jax.experimental.pallas import tpu as pltpu
from jax.sharding import PartitionSpec as P

BUCKETS = 32
MAX_DISTANCE = 128
EPSILON = 1e-06
MASK_FILL = -1e30
F32 = jnp.float32
BF16 = jnp.bfloat16


def bucket_bounds(buckets, far_reach):
    exact_count = buckets // 2
    bounds = []
    for number in range(1, buckets):
        if number <= exact_count:
            bounds.append(number)
        else:
            exponent = (number - exact_count) / (buckets - exact_count)
            bounds.append(int(np.ceil(exact_count * (far_reach / exact_count) ** exponent)))
    return bounds


BOUNDS = bucket_bounds(BUCKETS, MAX_DISTANCE)


def rms_scale(values):
    return lax.rsqrt(jnp.mean(values * values, axis=-1, keepdims=True) + EPSILON)


def dot(a, b, ca, cb):
    return lax.dot_general(a, b, (((ca,), (cb,)), ((), ())), preferred_element_type=F32)


def gather(shard, axis, dim):
    count = lax.axis_size(axis)
    size = shard.shape[dim]
    me = lax.axis_index(axis)
    pieces = [shard] + [
        lax.ppermute(shard, axis, [(i, (i + step) % count) for i in range(count)])
        for step in range(1, count)
    ]
    if count == 2:
        first = me == 0
        return jnp.concatenate(
            [jnp.where(first, pieces[0], pieces[1]), jnp.where(first, pieces[1], pieces[0])],
            axis=dim,
        )
    shape = list(shard.shape)
    shape[dim] = count * size
    whole = jnp.zeros(shape, shard.dtype)
    for step, piece in enumerate(pieces):
        source = lax.rem(me + count - step, count)
        whole = lax.dynamic_update_slice_in_dim(whole, piece, source * size, dim)
    return whole


def exchange_sum(part, axis, dim, kind=BF16):
    count = lax.axis_size(axis)
    size = part.shape[dim] // count
    me = lax.axis_index(axis)
    total = lax.dynamic_slice_in_dim(part, me * size, size, dim).astype(F32)
    for step in range(1, count):
        target = lax.rem(me + step, count)
        piece = lax.dynamic_slice_in_dim(part, target * size, size, dim).astype(kind)
        total = total + lax.ppermute(
            piece, axis, [(i, (i + step) % count) for i in range(count)]
        ).astype(F32)
    return total


MESH = pl.DeviceIdType.MESH
TILE = 256
SLAB = 32
LANES = 128


def flip(value, bit):
    return value + bit - 2 * bit * lax.rem(lax.div(value, bit), 2)


def xor(value, mask):
    for bit in (1, 2):
        if mask & bit:
            value = flip(value, bit)
    return value


def place():
    return lax.axis_index("fsdp"), lax.axis_index("ctx"), lax.axis_index("tp")


def remote(src, dst, send, recv, target):
    return pltpu.make_async_remote_copy(
        src_ref=src,
        dst_ref=dst,
        send_sem=send,
        recv_sem=recv,
        device_id=target,
        device_id_type=MESH,
    )


def greet(targets):
    barrier = pltpu.get_barrier_semaphore()
    for target in targets:
        pl.semaphore_signal(barrier, inc=1, device_id=target, device_id_type=MESH)
    pl.semaphore_wait(barrier, len(targets))


def tanh_gelu(u):
    first = 0.7978845608028654
    cubic = 0.044715 * first
    square = u * u
    wave = jnp.tanh(u * (first + cubic * square))
    half = 0.5 + 0.5 * wave
    slope = half + (0.5 * u) * (1.0 - wave * wave) * (first + 3.0 * cubic * square)
    return u * half, slope


def experts_kernel(
    normed,
    grads,
    up,
    down,
    router,
    wide,
    back_sum,
    forth_sum,
    dots_sum,
    nall,
    gpre,
    gated,
    pre,
    reach,
    gate,
    high,
    low,
    bufs,
    gsend,
    grecv,
    ssend,
    srecv,
):
    f, i, t = place()
    rows, width = normed.shape
    group = nall.shape[1]
    sibling = (f, flip(i, 1), t)
    across = (f, flip(i, 2), t)
    along = [None] + [(f, i, xor(t, k)) for k in (1, 2, 3)]

    def block(index):
        return pl.ds(pl.multiple_of(index * rows, rows), rows)

    def spread_copy(k, j):
        if j == 0:
            src, here, target = normed, nall.at[t, block(i), :], along[k]
            return remote(src, here, gsend.at[k, j], grecv.at[k, j], target)
        source = i if j < 3 else flip(i, 2)
        slot = nall.at[xor(t, k), block(source), :]
        target = across if j == 2 else sibling
        return remote(slot, slot, gsend.at[k, j], grecv.at[k, j], target)

    gather = {(k, j): spread_copy(k, j) for k in range(4) for j in range(4) if (k, j) != (0, 0)}

    greet([sibling, across] + along[1:])
    nall[t, block(i), :] = normed[...]
    gather[0, 2].start()
    gather[0, 1].start()
    for k in (1, 2, 3):
        gather[k, 0].start()

    pick = wide[pl.ds(0, SLAB), :]

    def compute(k):
        tk = xor(t, k)

        def tile(m, carry):
            base = pl.multiple_of(m * TILE, TILE)
            piece = pl.ds(base, TILE)
            pre[...] = dot(nall[tk, piece, :], up[...], 1, 1)
            logits = dot(nall[tk, piece, :], router[...], 1, 1)
            reach[...] = dot(grads[tk, piece, pl.ds(0, width)], down[...], 1, 1)
            chosen = grads[tk, piece, pl.ds(width, LANES)].astype(F32) > 0.5
            masked = jnp.where(chosen, logits, MASK_FILL)
            raw = jnp.where(
                chosen, jnp.exp(masked - jnp.max(masked, axis=1, keepdims=True)), 0.0
            )
            gates = raw / jnp.sum(raw, axis=1, keepdims=True)
            terms = []
            for _ in range(3):
                terms.append(gates.astype(BF16))
                gates = gates - terms[-1].astype(F32)
            gate[...] = dot(jnp.concatenate(terms, axis=1), wide[...], 1, 0)

            def slab(s, inner):
                at = pl.ds(pl.multiple_of(s * SLAB, SLAB), SLAB)
                to = pl.ds(pl.multiple_of(base + s * SLAB, SLAB), SLAB)
                for c in range(pre.shape[1] // LANES):
                    cols = pl.ds(c * LANES, LANES)
                    share = gate[at, cols]
                    act, slope = tanh_gelu(pre[at, cols])
                    act = act.astype(BF16).astype(F32)
                    pull = reach[at, cols]
                    gated[tk, to, cols] = (act * share).astype(BF16)
                    gpre[tk, to, cols] = (pull * share * slope).astype(BF16)
                    product = act * pull
                    coarse = product.astype(BF16)
                    high[at, cols] = coarse
                    low[at, cols] = (product - coarse.astype(F32)).astype(BF16)
                return inner

            lax.fori_loop(0, TILE // SLAB, slab, 0)
            dots = dot(pick, high[...], 1, 1) + dot(pick, low[...], 1, 1)
            for half in range(TILE // rows):
                bufs["dots"]["part"][k, m * (TILE // rows) + half] = dots[
                    :8, half * rows : (half + 1) * rows
                ]
            bufs["back"]["part"][k, piece, :] = dot(gpre[tk, piece, :], up[...], 1, 0).astype(BF16)
            bufs["forth"]["part"][k, piece, :] = dot(gated[tk, piece, :], down[...], 1, 0).astype(BF16)
            return carry

        lax.fori_loop(0, group // TILE, tile, 0)

    names = ("back", "dots", "forth")

    def part_of(name, k, index):
        part = bufs[name]["part"]
        if name == "dots":
            return part.at[k, index]
        return part.at[k, block(index), :]

    def scatter_copy(name, k, stage):
        b, n = bufs[name], names.index(name)
        send, recv = ssend.at[n, k, stage], srecv.at[n, k, stage]
        if stage < 2:
            src = part_of(name, k, xor(i, 1 if stage == 0 else 3))
            return remote(src, b["near"].at[k, stage], send, recv, sibling)
        if stage == 2:
            return remote(b["out"].at[k, 0], b["far"].at[k, 0], send, recv, across)
        return remote(b["out"].at[k, 1], b["far"].at[k, 1], send, recv, along[k])

    scatter = {
        (n, k, s): scatter_copy(n, k, s)
        for n in names
        for k in range(4)
        for s in range(4)
        if (k, s) != (0, 3)
    }

    def first(k, which):
        for n in which:
            scatter[n, k, 1].start()
            scatter[n, k, 0].start()

    def second(k, which):
        for n in which:
            b = bufs[n]
            scatter[n, k, 1].wait_recv()
            total = part_of(n, k, flip(i, 2))[...].astype(F32) + b["near"][k, 1].astype(F32)
            b["out"][k, 0] = total.astype(b["out"].dtype)
            scatter[n, k, 2].start()

    def third(k, which):
        for n in which:
            b = bufs[n]
            scatter[n, k, 0].wait_recv()
            scatter[n, k, 2].wait_recv()
            total = (
                part_of(n, k, i)[...].astype(F32)
                + b["near"][k, 0].astype(F32)
                + b["far"][k, 0].astype(F32)
            )
            if k == 0:
                b["sum"][...] = total
            else:
                b["out"][k, 1] = total.astype(b["out"].dtype)
                scatter[n, k, 3].start()

    def last(which):
        for n in which:
            b = bufs[n]
            for k in (1, 2, 3):
                scatter[n, k, 3].wait_recv()
                b["sum"][...] = b["sum"][...] + b["far"][k, 1].astype(F32)

    bufs["back"]["sum"], bufs["forth"]["sum"], bufs["dots"]["sum"] = back_sum, forth_sum, dots_sum
    early = ("dots", "back")

    gather[0, 2].wait_recv()
    gather[0, 3].start()
    gather[1, 0].wait_recv()
    gather[1, 2].start()
    gather[1, 1].start()
    gather[0, 1].wait_recv()
    gather[0, 3].wait_recv()
    compute(0)
    first(0, early)
    gather[1, 2].wait_recv()
    gather[1, 3].start()
    for k in (2, 3):
        gather[k, 0].wait_recv()
        gather[k, 2].start()
        gather[k, 1].start()
    second(0, early)
    gather[1, 1].wait_recv()
    gather[1, 3].wait_recv()
    compute(1)
    first(1, early)
    for k in (2, 3):
        gather[k, 2].wait_recv()
        gather[k, 3].start()
    third(0, early)
    second(1, early)
    gather[2, 1].wait_recv()
    gather[2, 3].wait_recv()
    compute(2)
    first(2, early)
    third(1, early)
    second(2, early)
    gather[3, 1].wait_recv()
    gather[3, 3].wait_recv()
    compute(3)
    first(3, early)
    third(2, early)
    second(3, early)
    for k in range(4):
        first(k, ("forth",))
    third(3, early)
    for k in (1, 2, 3, 0):
        second(k, ("forth",))
    last(early)
    for k in (1, 2, 3, 0):
        third(k, ("forth",))
    last(("forth",))
    for copy in list(gather.values()) + list(scatter.values()):
        copy.wait_send()


def experts_call(normed, grads, up, down, router, wide):
    rows, width = normed.shape
    spans, group, _ = grads.shape
    hidden = up.shape[0]
    vmem = pl.BlockSpec(memory_space=pltpu.VMEM)

    def stream(kind, shape):
        return {
            "part": pltpu.VMEM((spans, 4) + shape if kind == F32 else (spans, group, width), kind),
            "near": pltpu.VMEM((spans, 2) + shape, kind),
            "out": pltpu.VMEM((spans, 2) + shape, kind),
            "far": pltpu.VMEM((spans, 2) + shape, kind),
        }

    return pl.pallas_call(
        experts_kernel,
        out_shape=(
            jax.ShapeDtypeStruct((rows, width), F32),
            jax.ShapeDtypeStruct((rows, width), F32),
            jax.ShapeDtypeStruct((8, rows), F32),
            jax.ShapeDtypeStruct((spans, group, width), BF16),
            jax.ShapeDtypeStruct((spans, group, hidden), BF16),
            jax.ShapeDtypeStruct((spans, group, hidden), BF16),
        ),
        in_specs=[vmem] * 6,
        out_specs=[vmem] * 6,
        scratch_shapes=[
            pltpu.VMEM((TILE, hidden), F32),
            pltpu.VMEM((TILE, hidden), F32),
            pltpu.VMEM((TILE, hidden), F32),
            pltpu.VMEM((TILE, hidden), BF16),
            pltpu.VMEM((TILE, hidden), BF16),
            {
                "back": stream(BF16, (rows, width)),
                "forth": stream(BF16, (rows, width)),
                "dots": stream(F32, (8, rows)),
            },
            pltpu.SemaphoreType.DMA((4, 4)),
            pltpu.SemaphoreType.DMA((4, 4)),
            pltpu.SemaphoreType.DMA((3, 4, 4)),
            pltpu.SemaphoreType.DMA((3, 4, 4)),
        ],
        compiler_params=pltpu.CompilerParams(
            collective_id=0, has_side_effects=True, vmem_limit_bytes=56 * 1024 * 1024
        ),
    )(normed, grads, up, down, router, wide)


def local(
    tokens,
    seg_ids,
    routes,
    norm_attn,
    weight_qkv,
    weight_proj,
    rel_table,
    norm_ffn,
    weight_router,
    expert_up,
    expert_down,
    cotangent,
):
    rows = tokens.shape[1]
    width = tokens.shape[2]
    heads = rel_table.shape[0]
    head_size = width // heads
    ctx_count = lax.axis_size("ctx")
    heads_here = heads // ctx_count
    hw = heads_here * head_size
    experts = expert_up.shape[0]
    units = expert_up.shape[2]
    length = seg_ids.shape[1]
    score_scale = head_size ** (-0.5)
    ctx_index = lax.axis_index("ctx")
    fsdp_index = lax.axis_index("fsdp")
    own_width = norm_attn.shape[0]
    world = ("ctx", "tp")

    token_group = lax.all_gather(tokens[0], "ctx", axis=0, tiled=True)
    small = jnp.concatenate([norm_attn[None], norm_ffn[None], weight_router.T], axis=0)
    small = gather(small, "fsdp", 1)
    gain_one = small[0].astype(F32)
    gain_two = small[1].astype(F32)
    router_t = small[2:]
    qkv_part = jnp.concatenate(
        [
            lax.dynamic_slice_in_dim(weight_qkv, s * width + ctx_index * hw, hw, 1)
            for s in range(3)
        ],
        axis=1,
    )
    qkv_here = gather(qkv_part, "fsdp", 0)
    proj_full = gather(weight_proj, "fsdp", 1)
    up_t = gather(
        jnp.swapaxes(expert_up, 1, 2).reshape(experts * units, own_width), "fsdp", 1
    )
    down = gather(expert_down.reshape(experts * units, own_width), "fsdp", 1)
    expert_ids = jnp.arange(LANES, dtype=jnp.int32)[None, :]
    named = (routes[0][:, 0:1] == expert_ids) | (routes[0][:, 1:2] == expert_ids)
    packed_grad = jnp.concatenate([cotangent[0], named.astype(BF16)], axis=1)
    grad_routes = lax.all_gather(packed_grad, ("tp", "ctx"), axis=0, tiled=True)

    block = MAX_DISTANCE
    table_here = lax.dynamic_slice_in_dim(rel_table, ctx_index * heads_here, heads_here, 0)
    offset = (
        lax.broadcasted_iota(jnp.int32, (1, block, block), 1)
        - lax.broadcasted_iota(jnp.int32, (1, block, block), 2)
    )

    def bias_block(distance):
        value = jnp.broadcast_to(table_here[:, 0][:, None, None], (heads_here, block, block))
        for number, bound in enumerate(BOUNDS, 1):
            value = jnp.where(distance >= bound, table_here[:, number][:, None, None], value)
        return value

    near = bias_block(offset)
    next_near = bias_block(offset + block)
    far = jnp.broadcast_to(table_here[:, BUCKETS - 1][:, None, None], (heads_here, block, block))
    blocks = length // block
    picks = {0: near, 1: next_near}
    bias = jnp.concatenate(
        [
            jnp.concatenate(
                [picks.get(i - j, far) for j in range(blocks)],
                axis=2,
            )
            for i in range(blocks)
        ],
        axis=1,
    )
    positions = jnp.arange(length, dtype=jnp.int32)
    segment = seg_ids[0]
    allowed = (segment[:, None] == segment[None, :]) & (positions[:, None] >= positions[None, :])
    bias = jnp.where(allowed[None], bias, MASK_FILL)

    inputs_group = token_group.astype(F32)
    normed_group = (inputs_group * rms_scale(inputs_group) * gain_one).astype(BF16)
    projected = dot(normed_group, qkv_here, 1, 0).astype(BF16)
    by_head = projected.reshape(length, 3, heads_here, head_size)
    query, key, value = by_head[:, 0], by_head[:, 1], by_head[:, 2]

    scores = (
        jnp.einsum("qhd,khd->hqk", query, key, preferred_element_type=F32) * score_scale + bias
    )
    peak = jnp.max(scores, axis=-1, keepdims=True)
    weights = jnp.exp(scores - peak)
    probs = weights / jnp.sum(weights, axis=-1, keepdims=True)
    low_probs = probs.astype(BF16)
    attended = (
        jnp.einsum("hqk,khd->qhd", low_probs, value, preferred_element_type=F32)
        .astype(BF16)
        .reshape(length, hw)
    )
    mixed = lax.all_to_all(attended, "ctx", split_axis=0, concat_axis=1, tiled=True)
    inputs = tokens[0].astype(F32)
    scale_one = rms_scale(inputs)
    mixed, grad_routes, up_t, down = lax.optimization_barrier((mixed, grad_routes, up_t, down))
    middle = inputs + dot(mixed, proj_full, 1, 0)
    scale_two = rms_scale(middle)
    normed_two = (middle * scale_two * gain_two).astype(BF16)

    def gates_of(normed, route):
        logits = dot(normed, router_t, 1, 1)
        number = lax.broadcasted_iota(jnp.int32, (1, experts), 1)
        chosen = (route[:, 0:1] == number) | (route[:, 1:2] == number)
        masked = jnp.where(chosen, logits, MASK_FILL)
        raw = jnp.where(chosen, jnp.exp(masked - jnp.max(masked, axis=1, keepdims=True)), 0.0)
        return raw / jnp.sum(raw, axis=1, keepdims=True)

    hidden = experts * units
    wide = (
        jnp.arange(hidden, dtype=jnp.int32)[None, :] // units
        == jnp.arange(3 * LANES, dtype=jnp.int32)[:, None] % LANES
    ).astype(BF16)
    router_pad = jnp.pad(router_t, ((0, LANES - experts), (0, 0)))
    tp_count = lax.axis_size("tp")
    grad_normed_two, result, dots_own, normed_all, grad_pre, gated = experts_call(
        normed_two,
        grad_routes.reshape(tp_count, length, width + LANES),
        up_t,
        down,
        router_pad,
        wide,
    )
    gate_dots = dots_own[:experts].T
    total_rows = tp_count * length
    normed_all = normed_all.reshape(total_rows, width)
    grad_pre = grad_pre.reshape(total_rows, hidden)
    gated = gated.reshape(total_rows, hidden)
    grad_all = grad_routes[:, :width]
    grad_up = exchange_sum(dot(grad_pre, normed_all, 0, 0), "fsdp", 1)
    grad_up = jnp.swapaxes(grad_up.reshape(experts, units, own_width), 1, 2)
    grad_down = exchange_sum(dot(gated, grad_all, 0, 0), "fsdp", 1)
    grad_down = grad_down.reshape(experts, units, own_width)

    grad_out = cotangent[0].astype(F32)
    gates = gates_of(normed_two, routes[0])
    grad_logits = gates * (gate_dots - jnp.sum(gates * gate_dots, axis=1, keepdims=True))
    grad_normed_two = grad_normed_two + jnp.dot(
        grad_logits, router_t.astype(F32), precision=lax.Precision.HIGHEST
    )
    grad_router = lax.dot_general(
        grad_logits,
        normed_two.astype(F32),
        (((0,), (0,)), ((), ())),
        precision=lax.Precision.HIGHEST,
    )
    weighted_two = grad_normed_two * gain_two
    grad_gain_two = jnp.sum(grad_normed_two * middle * scale_two, axis=0)
    grad_middle = (
        grad_out
        + scale_two * weighted_two
        - middle * scale_two**3 * jnp.mean(weighted_two * middle, axis=1, keepdims=True)
    )
    grad_mid_group = lax.all_gather(grad_middle.astype(BF16), "ctx", axis=0, tiled=True)
    proj_rows = lax.dynamic_slice_in_dim(proj_full, ctx_index * hw, hw, 0)
    grad_attended = dot(grad_mid_group, proj_rows, 1, 1).astype(BF16)
    grad_heads = grad_attended.reshape(length, heads_here, head_size)
    grad_value = jnp.einsum("hqk,qhd->khd", low_probs, grad_heads, preferred_element_type=F32)
    grad_probs = jnp.einsum("qhd,khd->hqk", grad_heads, value, preferred_element_type=F32)
    grad_scores = (
        probs * (grad_probs - jnp.sum(probs * grad_probs, axis=-1, keepdims=True))
    ).astype(BF16)
    grad_query = (
        jnp.einsum("hqk,khd->qhd", grad_scores, key, preferred_element_type=F32) * score_scale
    )
    grad_key = (
        jnp.einsum("hqk,qhd->khd", grad_scores, query, preferred_element_type=F32) * score_scale
    )
    grad_qkv = jnp.concatenate(
        [
            grad_query.astype(BF16).reshape(length, hw),
            grad_key.astype(BF16).reshape(length, hw),
            grad_value.astype(BF16).reshape(length, hw),
        ],
        axis=1,
    )
    grad_normed_one = exchange_sum(dot(grad_qkv, qkv_here, 1, 1), "ctx", 0)

    weight_part = jnp.concatenate(
        [dot(normed_group, grad_qkv, 0, 0), dot(grad_mid_group, attended, 0, 0)], axis=1
    )
    weight_own = exchange_sum(weight_part, "fsdp", 0)
    grad_scores, weight_own = lax.optimization_barrier((grad_scores, weight_own))
    weight_own = exchange_sum(weight_own, "tp", 0).astype(BF16)
    def score_block(i, j):
        return grad_scores[
            :, i * block : (i + 1) * block, j * block : (j + 1) * block
        ].astype(F32)

    near_sum = sum(score_block(i, i) for i in range(blocks))
    next_sum = sum(score_block(i + 1, i) for i in range(blocks - 1))
    far_sum = sum(
        jnp.sum(score_block(i, j), axis=(1, 2)) for i in range(blocks) for j in range(i - 1)
    )
    lows = [0] + BOUNDS
    highs = BOUNDS + [2 * block]
    bucket_sums = [
        jnp.sum(jnp.where((offset >= lo) & (offset < hi), near_sum, 0.0), axis=(1, 2))
        + jnp.sum(
            jnp.where((offset + block >= lo) & (offset + block < hi), next_sum, 0.0), axis=(1, 2)
        )
        for lo, hi in zip(lows, highs)
    ]
    bucket_sums[-1] = bucket_sums[-1] + far_sum
    table_here_grad = jnp.stack(bucket_sums, axis=1)
    table_term = lax.dynamic_update_slice_in_dim(
        jnp.zeros((heads, BUCKETS), F32), table_here_grad, ctx_index * heads_here, 0
    )

    weighted_one = grad_normed_one * gain_one
    grad_gain_one = jnp.sum(grad_normed_one * inputs * scale_one, axis=0)
    grad_tokens = (
        grad_middle
        + scale_one * weighted_one
        - inputs * scale_one**3 * jnp.mean(weighted_one * inputs, axis=1, keepdims=True)
    )
    packed = jnp.concatenate(
        [
            grad_gain_one,
            grad_gain_two,
            grad_router.reshape(-1),
            table_term.reshape(-1),
        ]
    ).reshape(-1, 128)
    packed, weight_own = lax.optimization_barrier((packed, weight_own))
    packed = lax.psum(packed, ("fsdp", "ctx", "tp")).reshape(-1)
    packed, result = lax.optimization_barrier((packed, result))
    output = (middle + result).astype(BF16)[None]
    weight_all = lax.all_gather(weight_own, world, axis=0, tiled=True).astype(F32)
    weight_all = weight_all.reshape(ctx_count, own_width, 4 * hw)
    grad_weight_qkv = jnp.concatenate(
        [
            weight_all[c, :, s * hw : (s + 1) * hw]
            for s in range(3)
            for c in range(ctx_count)
        ],
        axis=1,
    )
    grad_weight_proj = jnp.swapaxes(weight_all[:, :, 3 * hw :], 1, 2).reshape(width, own_width)
    gains = packed[: (2 + experts) * width].reshape(2 + experts, width)
    gains = lax.dynamic_slice_in_dim(gains, fsdp_index * own_width, own_width, 1)
    table_grad = packed[(2 + experts) * width :].reshape(heads, BUCKETS)
    return (
        output,
        grad_tokens[None],
        gains[0],
        grad_weight_qkv,
        grad_weight_proj,
        table_grad,
        gains[1],
        gains[2:].T,
        grad_up,
        grad_down,
    )


def solution(mesh):
    rows = P(("fsdp", "tp"), "ctx", None)
    in_specs = (
        rows,
        P(("fsdp", "tp"), None),
        rows,
        P("fsdp"),
        P("fsdp", None),
        P(None, "fsdp"),
        P(),
        P("fsdp"),
        P("fsdp", None),
        P(None, "fsdp", ("ctx", "tp")),
        P(None, ("ctx", "tp"), "fsdp"),
        rows,
    )
    out_specs = (
        rows,
        rows,
        P("fsdp"),
        P("fsdp", None),
        P(None, "fsdp"),
        P(),
        P("fsdp"),
        P("fsdp", None),
        P(None, "fsdp", ("ctx", "tp")),
        P(None, ("ctx", "tp"), "fsdp"),
    )
    return jax.shard_map(local, mesh=mesh, in_specs=in_specs, out_specs=out_specs, check_vma=False)
```

```python
import functools

import jax
import jax.numpy as jnp
import numpy as np
from jax import lax
from jax.experimental import pallas as pl
from jax.experimental.pallas import tpu as pltpu
from jax.sharding import PartitionSpec as P

BUCKETS = 32
MAX_DISTANCE = 128
EPSILON = 1e-06
MASK_FILL = -1e30
F32 = jnp.float32
BF16 = jnp.bfloat16


def bucket_bounds(buckets, far_reach):
    exact_count = buckets // 2
    bounds = []
    for number in range(1, buckets):
        if number <= exact_count:
            bounds.append(number)
        else:
            exponent = (number - exact_count) / (buckets - exact_count)
            bounds.append(int(np.ceil(exact_count * (far_reach / exact_count) ** exponent)))
    return bounds


BOUNDS = bucket_bounds(BUCKETS, MAX_DISTANCE)


def rms_scale(values):
    return lax.rsqrt(jnp.mean(values * values, axis=-1, keepdims=True) + EPSILON)


def dot(a, b, ca, cb):
    return lax.dot_general(a, b, (((ca,), (cb,)), ((), ())), preferred_element_type=F32)


def gather(shard, axis, dim):
    count = lax.axis_size(axis)
    size = shard.shape[dim]
    me = lax.axis_index(axis)
    pieces = [shard] + [
        lax.ppermute(shard, axis, [(i, (i + step) % count) for i in range(count)])
        for step in range(1, count)
    ]
    if count == 2:
        first = me == 0
        return jnp.concatenate(
            [jnp.where(first, pieces[0], pieces[1]), jnp.where(first, pieces[1], pieces[0])],
            axis=dim,
        )
    shape = list(shard.shape)
    shape[dim] = count * size
    whole = jnp.zeros(shape, shard.dtype)
    for step, piece in enumerate(pieces):
        source = lax.rem(me + count - step, count)
        whole = lax.dynamic_update_slice_in_dim(whole, piece, source * size, dim)
    return whole


def exchange_sum(part, axis, dim, kind=BF16):
    count = lax.axis_size(axis)
    size = part.shape[dim] // count
    me = lax.axis_index(axis)
    total = lax.dynamic_slice_in_dim(part, me * size, size, dim).astype(F32)
    for step in range(1, count):
        target = lax.rem(me + step, count)
        piece = lax.dynamic_slice_in_dim(part, target * size, size, dim).astype(kind)
        total = total + lax.ppermute(
            piece, axis, [(i, (i + step) % count) for i in range(count)]
        ).astype(F32)
    return total


MESH = pl.DeviceIdType.MESH
TILE = 256
SLAB = 32
LANES = 128


def flip(value, bit):
    return value + bit - 2 * bit * lax.rem(lax.div(value, bit), 2)


def xor(value, mask):
    for bit in (1, 2):
        if mask & bit:
            value = flip(value, bit)
    return value


def place():
    return lax.axis_index("fsdp"), lax.axis_index("ctx"), lax.axis_index("tp")


def remote(src, dst, send, recv, target):
    return pltpu.make_async_remote_copy(
        src_ref=src,
        dst_ref=dst,
        send_sem=send,
        recv_sem=recv,
        device_id=target,
        device_id_type=MESH,
    )


def greet(targets):
    barrier = pltpu.get_barrier_semaphore()
    for target in targets:
        pl.semaphore_signal(barrier, inc=1, device_id=target, device_id_type=MESH)
    pl.semaphore_wait(barrier, len(targets))


def tanh_gelu(u):
    first = 0.7978845608028654
    cubic = 0.044715 * first
    square = u * u
    wave = jnp.tanh(u * (first + cubic * square))
    half = 0.5 + 0.5 * wave
    slope = half + (0.5 * u) * (1.0 - wave * wave) * (first + 3.0 * cubic * square)
    return u * half, slope


def gather_copies(spots, source, slot, send, recv, spans=4):
    f, i, t, sibling, across, along = spots

    def one(k, j):
        ends = send.at[k, j], recv.at[k, j]
        if j == 0:
            return remote(source, slot(t, i), *ends, along[k])
        here = slot(xor(t, k), i if j < 3 else flip(i, 2))
        origin = source if (k == 0 and j < 3) else here
        return remote(origin, here, *ends, across if j == 2 else sibling)

    return {(k, j): one(k, j) for k in range(spans) for j in range(4) if (k, j) != (0, 0)}


def neighbours():
    f, i, t = place()
    along = [None] + [(f, i, xor(t, k)) for k in (1, 2, 3)]
    return f, i, t, (f, flip(i, 1), t), (f, flip(i, 2), t), along


class Scatter:
    def __init__(self, spots, buf, part, send, recv):
        f, self.i, t, sibling, across, along = spots
        self.buf, self.part = buf, part
        self.copies = {}
        for k in range(buf["near"].shape[0]):
            for stage in range(4 if k else 3):
                ends = send.at[k, stage], recv.at[k, stage]
                if stage < 2:
                    src = part(k, xor(self.i, 1 if stage == 0 else 3))
                    copy = remote(src, buf["near"].at[k, stage], *ends, sibling)
                elif stage == 2:
                    copy = remote(buf["out"].at[k, 0], buf["far"].at[k, 0], *ends, across)
                else:
                    copy = remote(buf["out"].at[k, 1], buf["far"].at[k, 1], *ends, along[k])
                self.copies[k, stage] = copy

    def first(self, k):
        self.copies[k, 1].start()
        self.copies[k, 0].start()

    def second(self, k):
        b = self.buf
        self.copies[k, 1].wait_recv()
        total = self.part(k, flip(self.i, 2))[...].astype(F32) + b["near"][k, 1].astype(F32)
        b["out"][k, 0] = total.astype(b["out"].dtype)
        self.copies[k, 2].start()

    def third(self, k):
        b = self.buf
        self.copies[k, 0].wait_recv()
        self.copies[k, 2].wait_recv()
        total = (
            self.part(k, self.i)[...].astype(F32)
            + b["near"][k, 0].astype(F32)
            + b["far"][k, 0].astype(F32)
        )
        if k == 0:
            b["sum"][...] = total
        else:
            b["out"][k, 1] = total.astype(b["out"].dtype)
            self.copies[k, 3].start()

    def last(self):
        b = self.buf
        for k in (1, 2, 3):
            self.copies[k, 3].wait_recv()
            b["sum"][...] = b["sum"][...] + b["far"][k, 1].astype(F32)


def experts_kernel(
    forth,
    normed,
    grads,
    up,
    down,
    router,
    wide,
    back_sum,
    forth_sum,
    dots_sum,
    nall,
    gpre,
    gated,
    pre,
    reach,
    gate,
    high,
    low,
    bufs,
    gsend,
    grecv,
    ssend,
    srecv,
):
    spots = neighbours()
    f, i, t, sibling, across, along = spots
    rows, width = normed.shape
    group = nall.shape[1]

    def block(index):
        return pl.ds(pl.multiple_of(index * rows, rows), rows)

    gather = gather_copies(
        spots, normed, lambda tt, ii: nall.at[tt, block(ii), :], gsend, grecv
    )
    greet([sibling, across] + along[1:])
    nall[t, block(i), :] = normed[...]
    gather[0, 2].start()
    gather[0, 1].start()
    for k in (1, 2, 3):
        gather[k, 0].start()

    pick = wide[pl.ds(0, SLAB), :]

    def compute(k):
        tk = xor(t, k)

        def tile(m, carry):
            base = pl.multiple_of(m * TILE, TILE)
            piece = pl.ds(base, TILE)
            pre[...] = dot(nall[tk, piece, :], up[...], 1, 1)
            logits = dot(nall[tk, piece, :], router[...], 1, 1)
            reach[...] = dot(grads[tk, piece, pl.ds(0, width)], down[...], 1, 1)
            chosen = grads[tk, piece, pl.ds(width, LANES)].astype(F32) > 0.5
            masked = jnp.where(chosen, logits, MASK_FILL)
            raw = jnp.where(
                chosen, jnp.exp(masked - jnp.max(masked, axis=1, keepdims=True)), 0.0
            )
            gates = raw / jnp.sum(raw, axis=1, keepdims=True)
            terms = []
            for _ in range(3):
                terms.append(gates.astype(BF16))
                gates = gates - terms[-1].astype(F32)
            gate[...] = dot(jnp.concatenate(terms, axis=1), wide[...], 1, 0)

            def slab(s, inner):
                at = pl.ds(pl.multiple_of(s * SLAB, SLAB), SLAB)
                to = pl.ds(pl.multiple_of(base + s * SLAB, SLAB), SLAB)
                for c in range(pre.shape[1] // LANES):
                    cols = pl.ds(c * LANES, LANES)
                    share = gate[at, cols]
                    act, slope = tanh_gelu(pre[at, cols])
                    act = act.astype(BF16).astype(F32)
                    pull = reach[at, cols]
                    gated[tk, to, cols] = (act * share).astype(BF16)
                    gpre[tk, to, cols] = (pull * share * slope).astype(BF16)
                    product = act * pull
                    coarse = product.astype(BF16)
                    high[at, cols] = coarse
                    low[at, cols] = (product - coarse.astype(F32)).astype(BF16)
                return inner

            lax.fori_loop(0, TILE // SLAB, slab, 0)
            dots = dot(pick, high[...], 1, 1) + dot(pick, low[...], 1, 1)
            for half in range(TILE // rows):
                bufs["dots"]["part"][k, m * (TILE // rows) + half] = dots[
                    :8, half * rows : (half + 1) * rows
                ]
            bufs["back"]["part"][k, piece, :] = dot(gpre[tk, piece, :], up[...], 1, 0).astype(BF16)
            if forth:
                bufs["forth"]["part"][k, piece, :] = dot(
                    gated[tk, piece, :], down[...], 1, 0
                ).astype(BF16)
            return carry

        lax.fori_loop(0, group // TILE, tile, 0)

    bufs["back"]["sum"], bufs["forth"]["sum"], bufs["dots"]["sum"] = back_sum, forth_sum, dots_sum

    def part_of(name):
        part = bufs[name]["part"]
        if name == "dots":
            return lambda k, index: part.at[k, index]
        return lambda k, index: part.at[k, block(index), :]

    streams = {
        name: Scatter(spots, bufs[name], part_of(name), ssend.at[n], srecv.at[n])
        for n, name in enumerate(("back", "dots", "forth") if forth else ("back", "dots"))
    }

    def first(k, which):
        for name in which:
            streams[name].first(k)

    def second(k, which):
        for name in which:
            streams[name].second(k)

    def third(k, which):
        for name in which:
            streams[name].third(k)

    def last(which):
        for name in which:
            streams[name].last()

    early = ("dots", "back")
    gather[0, 2].wait_recv()
    gather[0, 3].start()
    gather[1, 0].wait_recv()
    gather[1, 2].start()
    gather[1, 1].start()
    gather[0, 1].wait_recv()
    gather[0, 3].wait_recv()
    compute(0)
    first(0, early)
    gather[1, 2].wait_recv()
    gather[1, 3].start()
    for k in (2, 3):
        gather[k, 0].wait_recv()
        gather[k, 2].start()
        gather[k, 1].start()
    second(0, early)
    gather[1, 1].wait_recv()
    gather[1, 3].wait_recv()
    compute(1)
    first(1, early)
    for k in (2, 3):
        gather[k, 2].wait_recv()
        gather[k, 3].start()
    third(0, early)
    second(1, early)
    gather[2, 1].wait_recv()
    gather[2, 3].wait_recv()
    compute(2)
    first(2, early)
    third(1, early)
    second(2, early)
    gather[3, 1].wait_recv()
    gather[3, 3].wait_recv()
    compute(3)
    first(3, early)
    third(2, early)
    second(3, early)
    late = ("forth",) if forth else ()
    for k in range(4):
        first(k, late)
    third(3, early)
    for k in (1, 2, 3, 0):
        second(k, late)
    last(early)
    for k in (1, 2, 3, 0):
        third(k, late)
    last(late)
    copies = list(gather.values())
    for stream in streams.values():
        copies += list(stream.copies.values())
    for copy in copies:
        copy.wait_send()


def scatter_scratch(spans, kind, shape, part):
    return {
        "part": pltpu.VMEM((spans,) + part, kind),
        "near": pltpu.VMEM((spans, 2) + shape, kind),
        "out": pltpu.VMEM((spans, 2) + shape, kind),
        "far": pltpu.VMEM((spans, 2) + shape, kind),
    }


def experts_call(forth, normed, grads, up, down, router, wide):
    rows, width = normed.shape
    spans, group, _ = grads.shape
    hidden = up.shape[0]
    vmem = pl.BlockSpec(memory_space=pltpu.VMEM)

    streams = {
        "back": scatter_scratch(spans, BF16, (rows, width), (group, width)),
        "dots": scatter_scratch(spans, F32, (8, rows), (4, 8, rows)),
        "forth": (
            scatter_scratch(spans, BF16, (rows, width), (group, width))
            if forth
            else {"sum": pltpu.SMEM((1,), F32)}
        ),
    }
    return pl.pallas_call(
        functools.partial(experts_kernel, forth),
        out_shape=(
            jax.ShapeDtypeStruct((rows, width), F32),
            jax.ShapeDtypeStruct((rows, width) if forth else (8, LANES), F32),
            jax.ShapeDtypeStruct((8, rows), F32),
            jax.ShapeDtypeStruct((spans, group, width), BF16),
            jax.ShapeDtypeStruct((spans, group, hidden), BF16),
            jax.ShapeDtypeStruct((spans, group, hidden), BF16),
        ),
        in_specs=[vmem] * 6,
        out_specs=[vmem] * 6,
        scratch_shapes=[
            pltpu.VMEM((TILE, hidden), F32),
            pltpu.VMEM((TILE, hidden), F32),
            pltpu.VMEM((TILE, hidden), F32),
            pltpu.VMEM((TILE, hidden), BF16),
            pltpu.VMEM((TILE, hidden), BF16),
            streams,
            pltpu.SemaphoreType.DMA((4, 4)),
            pltpu.SemaphoreType.DMA((4, 4)),
            pltpu.SemaphoreType.DMA((3, 4, 4)),
            pltpu.SemaphoreType.DMA((3, 4, 4)),
        ],
        compiler_params=pltpu.CompilerParams(
            collective_id=0, has_side_effects=True, vmem_limit_bytes=56 * 1024 * 1024
        ),
    )(normed, grads, up, down, router, wide)


def tail_kernel(
    scale,
    gmid_own,
    probs,
    qkv,
    attended,
    normed,
    wqkv,
    wproj,
    gated,
    gpre,
    nall,
    grads,
    down,
    xscaled,
    fixed,
    near_bucket,
    next_bucket,
    forth_sum,
    gone_sum,
    gup,
    gdown,
    wall,
    small,
    gmid,
    gatt,
    gqkv,
    gscore,
    wide_up,
    wide_down,
    half_send,
    half_recv,
    wfull,
    wsend,
    wrecv,
    wsum,
    zsend,
    zrecv,
    smalls,
    forth_buf,
    gone_buf,
    msend,
    mrecv,
    fsend,
    frecv,
    osend,
    orecv,
    xsend,
    xrecv,
    wgsend,
    wgrecv,
):
    spots = neighbours()
    f, i, t, sibling, across, along = spots
    peer = (1 - f, i, t)
    rows, width = gmid_own.shape
    spans, group, _ = nall.shape
    heads, head = probs.shape[0], wproj.shape[0] // probs.shape[0]
    hw = heads * head
    own = width // 2
    piece = own // spans
    blocks = group // rows

    def block(index):
        return pl.ds(pl.multiple_of(index * rows, rows), rows)

    def half(index):
        return pl.ds(pl.multiple_of(index * own, LANES), own)

    mids = gather_copies(spots, gmid_own, lambda tt, ii: gmid.at[block(ii), :], msend, mrecv, 1)
    forth_buf["sum"], gone_buf["sum"] = forth_sum, gone_sum
    forth = Scatter(
        spots, forth_buf, lambda k, index: forth_buf["part"].at[k, block(index), :], fsend, frecv
    )
    gone = Scatter(
        spots, gone_buf, lambda k, index: gone_buf["part"].at[k, block(index), :], osend, orecv
    )
    halves = [
        remote(half_send[n], half_recv[n], xsend.at[n], xrecv.at[n], peer) for n in range(2)
    ]
    wx = [
        remote(wsend.at[n], wrecv.at[n], xsend.at[2 + n], xrecv.at[2 + n], peer) for n in range(2)
    ]
    wz = [
        {
            k: remote(
                zsend.at[n, pl.ds(pl.multiple_of(xor(t, k) * piece, 16), piece), :],
                zrecv.at[n, k],
                xsend.at[4 + 3 * n + k - 1],
                xrecv.at[4 + 3 * n + k - 1],
                along[k],
            )
            for k in (1, 2, 3)
        }
        for n in range(2)
    ]
    wg = [
        gather_copies(
            spots,
            wall.at[n, t, i],
            lambda tt, ii, n=n: wall.at[n, tt, ii],
            wgsend.at[n],
            wgrecv.at[n],
        )
        for n in range(2)
    ]
    steps = [
        remote(smalls.at[n], smalls.at[3 + n], xsend.at[10 + n], xrecv.at[10 + n], target)
        for n, target in enumerate((sibling, across, peer))
    ]
    rounds = [
        remote(small, smalls.at[5 + k], xsend.at[12 + k], xrecv.at[12 + k], along[k])
        for k in (1, 2, 3)
    ]

    greet([sibling, across, peer] + along[1:])
    gmid[block(i), :] = gmid_own[...]
    mids[0, 2].start()
    mids[0, 1].start()

    def forth_part(k):
        tk = xor(t, k)

        def tile(m, carry):
            at = pl.ds(pl.multiple_of(m * TILE, TILE), TILE)
            forth_buf["part"][k, at, :] = dot(gated[tk, at, :], down[...], 1, 0).astype(BF16)
            return carry

        lax.fori_loop(0, group // TILE, tile, 0)
        forth.first(k)

    def up_half(which, out):
        out[...] = jnp.zeros_like(out)

        def step(c, carry):
            out[...] += dot(nall[c, :, half(which)], gpre[c], 0, 0)
            return carry

        lax.fori_loop(0, spans, step, 0)

    def down_half(which, out):
        out[...] = jnp.zeros_like(out)

        def step(c, carry):
            out[...] += dot(gated[c], grads[c, :, half(which)], 0, 0)
            return carry

        lax.fori_loop(0, spans, step, 0)

    forth_part(1)
    forth_part(2)
    mids[0, 2].wait_recv()
    mids[0, 3].start()
    down_half(1 - f, wide_down)
    half_send[0][...] = wide_down[...].astype(BF16)
    halves[0].start()
    forth.second(1)
    forth_part(3)
    forth_part(0)
    forth.second(2)
    mids[0, 1].wait_recv()
    mids[0, 3].wait_recv()

    gatt[...] = dot(gmid[...], wproj[...], 1, 1).astype(BF16)
    wfull[0, :, pl.ds(0, hw)] = dot(gmid[...], attended[...], 0, 0)
    for h in range(heads):
        cols = pl.ds(h * head, head)
        gqkv[:, pl.ds(2 * hw + h * head, head)] = dot(
            probs[h].astype(BF16), gatt[:, cols], 0, 0
        ).astype(BF16)
    wfull[0, :, pl.ds(hw, hw)] = dot(normed[...], gqkv[:, pl.ds(2 * hw, hw)], 0, 0)
    wsend[0] = wfull[0, half(1 - f), :].astype(BF16)
    wx[0].start()
    forth.second(3)
    forth.second(0)
    forth.third(1)

    table = small.at[pl.ds(0, heads * BUCKETS), :]
    for h in range(heads):
        cols = pl.ds(h * head, head)
        keys = pl.ds(hw + h * head, head)

        def rowtile(m, carry, h=h, cols=cols, keys=keys):
            at = block(m)
            grad_probs = dot(gatt[at, cols], qkv[:, pl.ds(2 * hw + h * head, head)], 1, 1)
            prob = probs[h, at, :]
            inner = jnp.sum(prob * grad_probs, axis=1, keepdims=True)
            score = (prob * (grad_probs - inner)).astype(BF16)
            gscore[h, at, :] = score
            gqkv[at, cols] = (dot(score, qkv[:, keys], 1, 0) * scale).astype(BF16)
            return carry

        lax.fori_loop(0, blocks, rowtile, 0)
        gqkv[:, keys] = (dot(gscore[h], qkv[:, cols], 0, 0) * scale).astype(BF16)
        if h == 0:
            forth.third(2)
        if h == 1:
            forth.third(3)

    def gone_tile(m, carry):
        at = block(m)
        gone_buf["part"][0, at, :] = dot(gqkv[at, :], wqkv[...], 1, 1).astype(BF16)
        return carry

    lax.fori_loop(0, blocks, gone_tile, 0)
    gone.first(0)
    wfull[1] = dot(normed[...], gqkv[:, pl.ds(0, 2 * hw)], 0, 0)
    wsend[1] = wfull[1, half(1 - f), :].astype(BF16)
    wx[1].start()
    gone.second(0)
    up_half(1 - f, wide_up)
    half_send[1][...] = wide_up[...].astype(BF16)
    halves[1].start()

    def reduce_along(n):
        wx[n].wait_recv()
        total = wfull[n, half(f), :] + wrecv[n].astype(F32)
        wsum[n] = total
        zsend[n] = total.astype(BF16)
        for k in (1, 2, 3):
            wz[n][k].start()

    def share(n):
        total = wsum[n, pl.ds(pl.multiple_of(t * piece, 16), piece), :]
        for k in (1, 2, 3):
            wz[n][k].wait_recv()
            total = total + zrecv[n, k].astype(F32)
        wall[n, t, i] = total.astype(BF16)
        wg[n][0, 2].start()
        wg[n][0, 1].start()
        for k in (1, 2, 3):
            wg[n][k, 0].start()

    def onward(n):
        for k in (1, 2, 3):
            wg[n][k, 0].wait_recv()
            wg[n][k, 2].start()
            wg[n][k, 1].start()

    def relay(n):
        for k in range(4):
            wg[n][k, 2].wait_recv()
            wg[n][k, 3].start()

    reduce_along(0)
    forth.third(0)

    def bucket_sums(h):
        near = jnp.zeros((rows, rows), F32)
        after = jnp.zeros((rows, rows), F32)
        far = jnp.zeros((rows, rows), F32)
        for a in range(blocks):
            for b in range(a + 1):
                score = gscore[h, pl.ds(a * rows, rows), pl.ds(b * rows, rows)].astype(F32)
                if a == b:
                    near = near + score
                elif a == b + 1:
                    after = after + score
                else:
                    far = far + score
        sums = []
        for b in range(BUCKETS):
            value = jnp.where(near_bucket[...] == b, near, 0.0) + jnp.where(
                next_bucket[...] == b, after, 0.0
            )
            if b == BUCKETS - 1:
                value = value + far
            sums.append(jnp.sum(value, axis=0, keepdims=True))
        sums = jnp.sum(jnp.concatenate(sums, axis=0), axis=1, keepdims=True)
        lane = lax.broadcasted_iota(jnp.int32, (BUCKETS, LANES), 1)
        smalls[0, pl.ds(h * BUCKETS, BUCKETS), :] = jnp.where(lane == i, sums, 0.0)

    for h in range(heads):
        bucket_sums(h)
    gone.third(0)
    gain = jnp.sum(gone_sum[...] * xscaled[...], axis=0, keepdims=True)
    base = heads * BUCKETS
    smalls[0, pl.ds(base, smalls.shape[1] - base), :] = fixed[...]
    for c in range(width // LANES):
        smalls[0, pl.ds(base + c, 1), :] = gain[:, c * LANES : (c + 1) * LANES]
    share(0)
    steps[0].start()
    down_half(f, gdown)
    reduce_along(1)
    up_half(f, gup)
    steps[0].wait_recv()
    smalls[1] = smalls[0] + smalls[3]
    steps[1].start()
    onward(0)
    share(1)
    steps[1].wait_recv()
    smalls[2] = smalls[1] + smalls[4]
    steps[2].start()
    relay(0)
    steps[2].wait_recv()
    small[...] = smalls[2] + smalls[5]
    for copy in rounds:
        copy.start()
    onward(1)
    forth.last()
    relay(1)
    for copy in rounds:
        copy.wait()
    small[...] = small[...] + smalls[6] + smalls[7] + smalls[8]
    halves[0].wait_recv()
    gdown[...] = gdown[...] + half_recv[0][...].astype(F32)
    halves[1].wait_recv()
    gup[...] = gup[...] + half_recv[1][...].astype(F32)
    for n in range(2):
        for k in range(4):
            wg[n][k, 1].wait_recv()
            wg[n][k, 3].wait_recv()
    copies = halves + wx + steps + list(mids.values())
    copies += list(forth.copies.values()) + list(gone.copies.values())
    for n in range(2):
        copies += list(wz[n].values()) + list(wg[n].values())
    for copy in copies:
        copy.wait_send()


def tail_call(scale, *operands):
    gmid, probs, qkv, attended, normed, wqkv, wproj, gated, gpre, nall = operands[:10]
    rows, width = gmid.shape
    spans, group, hidden = gpre.shape
    heads = probs.shape[0]
    hw = attended.shape[1]
    own = width // 2
    piece = own // spans
    extra = 8 * width // LANES
    vmem = pl.BlockSpec(memory_space=pltpu.VMEM)
    shape = jax.ShapeDtypeStruct
    dma = pltpu.SemaphoreType.DMA
    table = heads * BUCKETS + extra
    return pl.pallas_call(
        functools.partial(tail_kernel, scale),
        out_shape=(
            shape((rows, width), F32),
            shape((rows, width), F32),
            shape((own, hidden), F32),
            shape((hidden, own), F32),
            shape((2, spans, 4, piece, 2 * hw), BF16),
            shape((table, LANES), F32),
        ),
        in_specs=[vmem] * len(operands),
        out_specs=[vmem] * 6,
        scratch_shapes=[
            pltpu.VMEM((group, width), BF16),
            pltpu.VMEM((group, hw), BF16),
            pltpu.VMEM((group, 3 * hw), BF16),
            pltpu.VMEM((heads, group, group), BF16),
            pltpu.VMEM((own, hidden), F32),
            pltpu.VMEM((hidden, own), F32),
            [pltpu.VMEM((hidden, own), BF16), pltpu.VMEM((own, hidden), BF16)],
            [pltpu.VMEM((hidden, own), BF16), pltpu.VMEM((own, hidden), BF16)],
            pltpu.VMEM((2, width, 2 * hw), F32),
            pltpu.VMEM((2, own, 2 * hw), BF16),
            pltpu.VMEM((2, own, 2 * hw), BF16),
            pltpu.VMEM((2, own, 2 * hw), F32),
            pltpu.VMEM((2, own, 2 * hw), BF16),
            pltpu.VMEM((2, 4, piece, 2 * hw), BF16),
            pltpu.VMEM((9, table, LANES), F32),
            scatter_scratch(spans, BF16, (rows, width), (group, width)),
            scatter_scratch(1, BF16, (rows, width), (group, width)),
            dma((1, 4)),
            dma((1, 4)),
            dma((spans, 4)),
            dma((spans, 4)),
            dma((1, 4)),
            dma((1, 4)),
            dma((16,)),
            dma((16,)),
            dma((2, 4, 4)),
            dma((2, 4, 4)),
        ],
        compiler_params=pltpu.CompilerParams(
            collective_id=1, has_side_effects=True, vmem_limit_bytes=58 * 1024 * 1024
        ),
    )(*operands)


def local(
    tokens,
    seg_ids,
    routes,
    norm_attn,
    weight_qkv,
    weight_proj,
    rel_table,
    norm_ffn,
    weight_router,
    expert_up,
    expert_down,
    cotangent,
):
    rows = tokens.shape[1]
    width = tokens.shape[2]
    heads = rel_table.shape[0]
    head_size = width // heads
    ctx_count = lax.axis_size("ctx")
    heads_here = heads // ctx_count
    hw = heads_here * head_size
    experts = expert_up.shape[0]
    units = expert_up.shape[2]
    length = seg_ids.shape[1]
    score_scale = head_size ** (-0.5)
    ctx_index = lax.axis_index("ctx")
    fsdp_index = lax.axis_index("fsdp")
    own_width = norm_attn.shape[0]
    world = ("ctx", "tp")

    token_group = lax.all_gather(tokens[0], "ctx", axis=0, tiled=True)
    small = jnp.concatenate([norm_attn[None], norm_ffn[None], weight_router.T], axis=0)
    small = gather(small, "fsdp", 1)
    gain_one = small[0].astype(F32)
    gain_two = small[1].astype(F32)
    router_t = small[2:]
    qkv_part = jnp.concatenate(
        [
            lax.dynamic_slice_in_dim(weight_qkv, s * width + ctx_index * hw, hw, 1)
            for s in range(3)
        ],
        axis=1,
    )
    qkv_here = gather(qkv_part, "fsdp", 0)
    proj_full = gather(weight_proj, "fsdp", 1)
    up_t = gather(
        jnp.swapaxes(expert_up, 1, 2).reshape(experts * units, own_width), "fsdp", 1
    )
    down = gather(expert_down.reshape(experts * units, own_width), "fsdp", 1)
    expert_ids = jnp.arange(LANES, dtype=jnp.int32)[None, :]
    named = (routes[0][:, 0:1] == expert_ids) | (routes[0][:, 1:2] == expert_ids)
    packed_grad = jnp.concatenate([cotangent[0], named.astype(BF16)], axis=1)
    grad_routes = lax.all_gather(packed_grad, ("tp", "ctx"), axis=0, tiled=True)

    block = MAX_DISTANCE
    table_here = lax.dynamic_slice_in_dim(rel_table, ctx_index * heads_here, heads_here, 0)
    offset = (
        lax.broadcasted_iota(jnp.int32, (1, block, block), 1)
        - lax.broadcasted_iota(jnp.int32, (1, block, block), 2)
    )

    def bias_block(distance):
        value = jnp.broadcast_to(table_here[:, 0][:, None, None], (heads_here, block, block))
        for number, bound in enumerate(BOUNDS, 1):
            value = jnp.where(distance >= bound, table_here[:, number][:, None, None], value)
        return value

    near = bias_block(offset)
    next_near = bias_block(offset + block)
    far = jnp.broadcast_to(table_here[:, BUCKETS - 1][:, None, None], (heads_here, block, block))
    blocks = length // block
    picks = {0: near, 1: next_near}
    bias = jnp.concatenate(
        [
            jnp.concatenate(
                [picks.get(i - j, far) for j in range(blocks)],
                axis=2,
            )
            for i in range(blocks)
        ],
        axis=1,
    )
    positions = jnp.arange(length, dtype=jnp.int32)
    segment = seg_ids[0]
    allowed = (segment[:, None] == segment[None, :]) & (positions[:, None] >= positions[None, :])
    bias = jnp.where(allowed[None], bias, MASK_FILL)

    inputs_group = token_group.astype(F32)
    normed_group = (inputs_group * rms_scale(inputs_group) * gain_one).astype(BF16)
    projected = dot(normed_group, qkv_here, 1, 0).astype(BF16)
    by_head = projected.reshape(length, 3, heads_here, head_size)
    query, key, value = by_head[:, 0], by_head[:, 1], by_head[:, 2]

    scores = (
        jnp.einsum("qhd,khd->hqk", query, key, preferred_element_type=F32) * score_scale + bias
    )
    peak = jnp.max(scores, axis=-1, keepdims=True)
    weights = jnp.exp(scores - peak)
    probs = weights / jnp.sum(weights, axis=-1, keepdims=True)
    low_probs = probs.astype(BF16)
    attended = (
        jnp.einsum("hqk,khd->qhd", low_probs, value, preferred_element_type=F32)
        .astype(BF16)
        .reshape(length, hw)
    )
    mixed = lax.all_to_all(attended, "ctx", split_axis=0, concat_axis=1, tiled=True)
    inputs = tokens[0].astype(F32)
    scale_one = rms_scale(inputs)
    mixed, grad_routes, up_t, down = lax.optimization_barrier((mixed, grad_routes, up_t, down))
    middle = inputs + dot(mixed, proj_full, 1, 0)
    scale_two = rms_scale(middle)
    normed_two = (middle * scale_two * gain_two).astype(BF16)

    def gates_of(normed, route):
        logits = dot(normed, router_t, 1, 1)
        number = lax.broadcasted_iota(jnp.int32, (1, experts), 1)
        chosen = (route[:, 0:1] == number) | (route[:, 1:2] == number)
        masked = jnp.where(chosen, logits, MASK_FILL)
        raw = jnp.where(chosen, jnp.exp(masked - jnp.max(masked, axis=1, keepdims=True)), 0.0)
        return raw / jnp.sum(raw, axis=1, keepdims=True)

    hidden = experts * units
    wide = (
        jnp.arange(hidden, dtype=jnp.int32)[None, :] // units
        == jnp.arange(3 * LANES, dtype=jnp.int32)[:, None] % LANES
    ).astype(BF16)
    router_pad = jnp.pad(router_t, ((0, LANES - experts), (0, 0)))
    tp_count = lax.axis_size("tp")
    pair = lax.axis_size("fsdp") == 2
    grad_normed_two, result, dots_own, normed_all, grad_pre, gated = experts_call(
        not pair,
        normed_two,
        grad_routes.reshape(tp_count, length, width + LANES),
        up_t,
        down,
        router_pad,
        wide,
    )
    gate_dots = dots_own[:experts].T
    total_rows = tp_count * length
    grad_out = cotangent[0].astype(F32)
    gates = gates_of(normed_two, routes[0])
    grad_logits = gates * (gate_dots - jnp.sum(gates * gate_dots, axis=1, keepdims=True))
    grad_normed_two = grad_normed_two + jnp.dot(
        grad_logits, router_t.astype(F32), precision=lax.Precision.HIGHEST
    )
    grad_router = lax.dot_general(
        grad_logits,
        normed_two.astype(F32),
        (((0,), (0,)), ((), ())),
        precision=lax.Precision.HIGHEST,
    )
    weighted_two = grad_normed_two * gain_two
    grad_gain_two = jnp.sum(grad_normed_two * middle * scale_two, axis=0)
    grad_middle = (
        grad_out
        + scale_two * weighted_two
        - middle * scale_two**3 * jnp.mean(weighted_two * middle, axis=1, keepdims=True)
    )
    if pair:
        lows = jnp.asarray(np.array(BOUNDS, np.int32))[:, None, None]
        near_bucket = jnp.sum((offset >= lows).astype(jnp.int32), axis=0)
        near_bucket = jnp.where(offset[0] >= 0, near_bucket, -1)
        next_bucket = jnp.sum((offset + block >= lows).astype(jnp.int32), axis=0)
        proj_rows = lax.dynamic_slice_in_dim(proj_full, ctx_index * hw, hw, 0)
        fixed = jnp.concatenate(
            [
                jnp.zeros((width,), F32),
                grad_gain_two,
                grad_router.reshape(-1),
                jnp.zeros((2 * width,), F32),
            ]
        ).reshape(-1, LANES)
        result, grad_normed_one, grad_up, grad_down, weight_all, packed = tail_call(
            score_scale,
            grad_middle.astype(BF16),
            probs,
            projected,
            attended,
            normed_group,
            qkv_here,
            proj_rows,
            gated,
            grad_pre,
            normed_all,
            grad_routes.reshape(tp_count, length, width + LANES),
            down,
            inputs * scale_one,
            fixed,
            near_bucket,
            next_bucket,
        )
        output = (middle + result).astype(BF16)[None]
        weighted_one = grad_normed_one * gain_one
        grad_tokens = (
            grad_middle
            + scale_one * weighted_one
            - inputs * scale_one**3 * jnp.mean(weighted_one * inputs, axis=1, keepdims=True)
        )
        grad_up = jnp.stack([grad_up[:, e * units : (e + 1) * units] for e in range(experts)])
        grad_down = grad_down.reshape(experts, units, own_width)
        weights = jnp.transpose(weight_all, (0, 2, 1, 3, 4)).reshape(
            2, ctx_count, own_width, 2 * hw
        )
        parts = [
            weights[1, :, :, :hw],
            weights[1, :, :, hw:],
            weights[0, :, :, hw:],
        ]
        grad_weight_qkv = jnp.concatenate(
            [part[c] for part in parts for c in range(ctx_count)], axis=1
        ).astype(F32)
        grad_weight_proj = (
            jnp.swapaxes(weights[0, :, :, :hw], 1, 2).reshape(width, own_width).astype(F32)
        )
        edge = heads_here * BUCKETS
        table_grad = packed[:edge, :ctx_count].T.reshape(heads, BUCKETS)
        gains = packed[edge:].reshape(-1, width)
        gains = lax.dynamic_slice_in_dim(gains, fsdp_index * own_width, own_width, 1)
        return (
            output,
            grad_tokens[None],
            gains[0],
            grad_weight_qkv,
            grad_weight_proj,
            table_grad,
            gains[1],
            gains[2 : 2 + experts].T,
            grad_up,
            grad_down,
        )
    normed_all = normed_all.reshape(total_rows, width)
    grad_pre = grad_pre.reshape(total_rows, hidden)
    gated = gated.reshape(total_rows, hidden)
    grad_all = grad_routes[:, :width]
    grad_up = exchange_sum(dot(grad_pre, normed_all, 0, 0), "fsdp", 1)
    grad_up = jnp.swapaxes(grad_up.reshape(experts, units, own_width), 1, 2)
    grad_down = exchange_sum(dot(gated, grad_all, 0, 0), "fsdp", 1)
    grad_down = grad_down.reshape(experts, units, own_width)

    grad_mid_group = lax.all_gather(grad_middle.astype(BF16), "ctx", axis=0, tiled=True)
    proj_rows = lax.dynamic_slice_in_dim(proj_full, ctx_index * hw, hw, 0)
    grad_attended = dot(grad_mid_group, proj_rows, 1, 1).astype(BF16)
    grad_heads = grad_attended.reshape(length, heads_here, head_size)
    grad_value = jnp.einsum("hqk,qhd->khd", low_probs, grad_heads, preferred_element_type=F32)
    grad_probs = jnp.einsum("qhd,khd->hqk", grad_heads, value, preferred_element_type=F32)
    grad_scores = (
        probs * (grad_probs - jnp.sum(probs * grad_probs, axis=-1, keepdims=True))
    ).astype(BF16)
    grad_query = (
        jnp.einsum("hqk,khd->qhd", grad_scores, key, preferred_element_type=F32) * score_scale
    )
    grad_key = (
        jnp.einsum("hqk,qhd->khd", grad_scores, query, preferred_element_type=F32) * score_scale
    )
    grad_qkv = jnp.concatenate(
        [
            grad_query.astype(BF16).reshape(length, hw),
            grad_key.astype(BF16).reshape(length, hw),
            grad_value.astype(BF16).reshape(length, hw),
        ],
        axis=1,
    )
    grad_normed_one = exchange_sum(dot(grad_qkv, qkv_here, 1, 1), "ctx", 0)

    weight_part = jnp.concatenate(
        [dot(normed_group, grad_qkv, 0, 0), dot(grad_mid_group, attended, 0, 0)], axis=1
    )
    weight_own = exchange_sum(weight_part, "fsdp", 0)
    grad_scores, weight_own = lax.optimization_barrier((grad_scores, weight_own))
    weight_own = exchange_sum(weight_own, "tp", 0).astype(BF16)
    def score_block(i, j):
        return grad_scores[
            :, i * block : (i + 1) * block, j * block : (j + 1) * block
        ].astype(F32)

    near_sum = sum(score_block(i, i) for i in range(blocks))
    next_sum = sum(score_block(i + 1, i) for i in range(blocks - 1))
    far_sum = sum(
        jnp.sum(score_block(i, j), axis=(1, 2)) for i in range(blocks) for j in range(i - 1)
    )
    lows = [0] + BOUNDS
    highs = BOUNDS + [2 * block]
    bucket_sums = [
        jnp.sum(jnp.where((offset >= lo) & (offset < hi), near_sum, 0.0), axis=(1, 2))
        + jnp.sum(
            jnp.where((offset + block >= lo) & (offset + block < hi), next_sum, 0.0), axis=(1, 2)
        )
        for lo, hi in zip(lows, highs)
    ]
    bucket_sums[-1] = bucket_sums[-1] + far_sum
    table_here_grad = jnp.stack(bucket_sums, axis=1)
    table_term = lax.dynamic_update_slice_in_dim(
        jnp.zeros((heads, BUCKETS), F32), table_here_grad, ctx_index * heads_here, 0
    )

    weighted_one = grad_normed_one * gain_one
    grad_gain_one = jnp.sum(grad_normed_one * inputs * scale_one, axis=0)
    grad_tokens = (
        grad_middle
        + scale_one * weighted_one
        - inputs * scale_one**3 * jnp.mean(weighted_one * inputs, axis=1, keepdims=True)
    )
    packed = jnp.concatenate(
        [
            grad_gain_one,
            grad_gain_two,
            grad_router.reshape(-1),
            table_term.reshape(-1),
        ]
    ).reshape(-1, 128)
    packed, weight_own = lax.optimization_barrier((packed, weight_own))
    packed = lax.psum(packed, ("fsdp", "ctx", "tp")).reshape(-1)
    packed, result = lax.optimization_barrier((packed, result))
    output = (middle + result).astype(BF16)[None]
    weight_all = lax.all_gather(weight_own, world, axis=0, tiled=True).astype(F32)
    weight_all = weight_all.reshape(ctx_count, own_width, 4 * hw)
    grad_weight_qkv = jnp.concatenate(
        [
            weight_all[c, :, s * hw : (s + 1) * hw]
            for s in range(3)
            for c in range(ctx_count)
        ],
        axis=1,
    )
    grad_weight_proj = jnp.swapaxes(weight_all[:, :, 3 * hw :], 1, 2).reshape(width, own_width)
    gains = packed[: (2 + experts) * width].reshape(2 + experts, width)
    gains = lax.dynamic_slice_in_dim(gains, fsdp_index * own_width, own_width, 1)
    table_grad = packed[(2 + experts) * width :].reshape(heads, BUCKETS)
    return (
        output,
        grad_tokens[None],
        gains[0],
        grad_weight_qkv,
        grad_weight_proj,
        table_grad,
        gains[1],
        gains[2:].T,
        grad_up,
        grad_down,
    )


def solution(mesh):
    rows = P(("fsdp", "tp"), "ctx", None)
    in_specs = (
        rows,
        P(("fsdp", "tp"), None),
        rows,
        P("fsdp"),
        P("fsdp", None),
        P(None, "fsdp"),
        P(),
        P("fsdp"),
        P("fsdp", None),
        P(None, "fsdp", ("ctx", "tp")),
        P(None, ("ctx", "tp"), "fsdp"),
        rows,
    )
    out_specs = (
        rows,
        rows,
        P("fsdp"),
        P("fsdp", None),
        P(None, "fsdp"),
        P(),
        P("fsdp"),
        P("fsdp", None),
        P(None, "fsdp", ("ctx", "tp")),
        P(None, ("ctx", "tp"), "fsdp"),
    )
    return jax.shard_map(local, mesh=mesh, in_specs=in_specs, out_specs=out_specs, check_vma=False)
```

```python
import functools

import jax
import jax.numpy as jnp
import numpy as np
from jax import lax
from jax.experimental import pallas as pl
from jax.experimental.pallas import tpu as pltpu
from jax.sharding import PartitionSpec as P

BUCKETS = 32
MAX_DISTANCE = 128
EPSILON = 1e-06
MASK_FILL = -1e30
F32 = jnp.float32
BF16 = jnp.bfloat16


def bucket_bounds(buckets, far_reach):
    exact_count = buckets // 2
    bounds = []
    for number in range(1, buckets):
        if number <= exact_count:
            bounds.append(number)
        else:
            exponent = (number - exact_count) / (buckets - exact_count)
            bounds.append(int(np.ceil(exact_count * (far_reach / exact_count) ** exponent)))
    return bounds


BOUNDS = bucket_bounds(BUCKETS, MAX_DISTANCE)


def rms_scale(values):
    return lax.rsqrt(jnp.mean(values * values, axis=-1, keepdims=True) + EPSILON)


def dot(a, b, ca, cb):
    return lax.dot_general(a, b, (((ca,), (cb,)), ((), ())), preferred_element_type=F32)


def gather(shard, axis, dim):
    count = lax.axis_size(axis)
    size = shard.shape[dim]
    me = lax.axis_index(axis)
    pieces = [shard] + [
        lax.ppermute(shard, axis, [(i, (i + step) % count) for i in range(count)])
        for step in range(1, count)
    ]
    if count == 2:
        first = me == 0
        return jnp.concatenate(
            [jnp.where(first, pieces[0], pieces[1]), jnp.where(first, pieces[1], pieces[0])],
            axis=dim,
        )
    shape = list(shard.shape)
    shape[dim] = count * size
    whole = jnp.zeros(shape, shard.dtype)
    for step, piece in enumerate(pieces):
        source = lax.rem(me + count - step, count)
        whole = lax.dynamic_update_slice_in_dim(whole, piece, source * size, dim)
    return whole


def exchange_sum(part, axis, dim, kind=BF16):
    count = lax.axis_size(axis)
    size = part.shape[dim] // count
    me = lax.axis_index(axis)
    total = lax.dynamic_slice_in_dim(part, me * size, size, dim).astype(F32)
    for step in range(1, count):
        target = lax.rem(me + step, count)
        piece = lax.dynamic_slice_in_dim(part, target * size, size, dim).astype(kind)
        total = total + lax.ppermute(
            piece, axis, [(i, (i + step) % count) for i in range(count)]
        ).astype(F32)
    return total


MESH = pl.DeviceIdType.MESH
TILE = 256
SLAB = 32
LANES = 128


def flip(value, bit):
    return value + bit - 2 * bit * lax.rem(lax.div(value, bit), 2)


def xor(value, mask):
    for bit in (1, 2):
        if mask & bit:
            value = flip(value, bit)
    return value


def place():
    return lax.axis_index("fsdp"), lax.axis_index("ctx"), lax.axis_index("tp")


def remote(src, dst, send, recv, target):
    return pltpu.make_async_remote_copy(
        src_ref=src,
        dst_ref=dst,
        send_sem=send,
        recv_sem=recv,
        device_id=target,
        device_id_type=MESH,
    )


def greet(targets):
    barrier = pltpu.get_barrier_semaphore()
    for target in targets:
        pl.semaphore_signal(barrier, inc=1, device_id=target, device_id_type=MESH)
    pl.semaphore_wait(barrier, len(targets))


def tanh_gelu(u):
    first = 0.7978845608028654
    cubic = 0.044715 * first
    square = u * u
    wave = jnp.tanh(u * (first + cubic * square))
    half = 0.5 + 0.5 * wave
    slope = half + (0.5 * u) * (1.0 - wave * wave) * (first + 3.0 * cubic * square)
    return u * half, slope


def gather_copies(spots, source, slot, send, recv, spans=4):
    f, i, t, sibling, across, along = spots

    def one(k, j):
        ends = send.at[k, j], recv.at[k, j]
        if j == 0:
            return remote(source, slot(t, i), *ends, along[k])
        here = slot(xor(t, k), i if j < 3 else flip(i, 2))
        origin = source if (k == 0 and j < 3) else here
        return remote(origin, here, *ends, across if j == 2 else sibling)

    return {(k, j): one(k, j) for k in range(spans) for j in range(4) if (k, j) != (0, 0)}


def neighbours():
    f, i, t = place()
    along = [None] + [(f, i, xor(t, k)) for k in (1, 2, 3)]
    return f, i, t, (f, flip(i, 1), t), (f, flip(i, 2), t), along


class Scatter:
    def __init__(self, spots, buf, part, send, recv):
        f, self.i, t, sibling, across, along = spots
        self.buf, self.part = buf, part
        self.copies = {}
        for k in range(buf["near"].shape[0]):
            for stage in range(4 if k else 3):
                ends = send.at[k, stage], recv.at[k, stage]
                if stage < 2:
                    src = part(k, xor(self.i, 1 if stage == 0 else 3))
                    copy = remote(src, buf["near"].at[k, stage], *ends, sibling)
                elif stage == 2:
                    copy = remote(buf["out"].at[k, 0], buf["far"].at[k, 0], *ends, across)
                else:
                    copy = remote(buf["out"].at[k, 1], buf["far"].at[k, 1], *ends, along[k])
                self.copies[k, stage] = copy

    def first(self, k):
        self.copies[k, 1].start()
        self.copies[k, 0].start()

    def second(self, k):
        b = self.buf
        self.copies[k, 1].wait_recv()
        total = self.part(k, flip(self.i, 2))[...].astype(F32) + b["near"][k, 1].astype(F32)
        b["out"][k, 0] = total.astype(b["out"].dtype)
        self.copies[k, 2].start()

    def third(self, k):
        b = self.buf
        self.copies[k, 0].wait_recv()
        self.copies[k, 2].wait_recv()
        total = (
            self.part(k, self.i)[...].astype(F32)
            + b["near"][k, 0].astype(F32)
            + b["far"][k, 0].astype(F32)
        )
        if k == 0:
            b["sum"][...] = total
        else:
            b["out"][k, 1] = total.astype(b["out"].dtype)
            self.copies[k, 3].start()

    def last(self):
        b = self.buf
        for k in (1, 2, 3):
            self.copies[k, 3].wait_recv()
            b["sum"][...] = b["sum"][...] + b["far"][k, 1].astype(F32)


def experts_kernel(
    forth,
    normed,
    grads,
    up,
    down,
    router,
    wide,
    back_sum,
    forth_sum,
    dots_sum,
    nall,
    gpre,
    gated,
    pre,
    reach,
    gate,
    high,
    low,
    bufs,
    gsend,
    grecv,
    ssend,
    srecv,
    ready=None,
):
    spots = neighbours()
    f, i, t, sibling, across, along = spots
    rows, width = normed.shape
    group = nall.shape[1]

    def block(index):
        return pl.ds(pl.multiple_of(index * rows, rows), rows)

    if ready is None:
        greet([sibling, across] + along[1:])
    gather = gather_copies(
        spots, normed, lambda tt, ii: nall.at[tt, block(ii), :], gsend, grecv
    )
    nall[t, block(i), :] = normed[...]
    gather[0, 2].start()
    gather[0, 1].start()
    for k in (1, 2, 3):
        gather[k, 0].start()

    pick = wide[pl.ds(0, SLAB), :]

    def compute(k):
        tk = xor(t, k)
        if ready is not None:
            ready(k)

        def tile(m, carry):
            base = pl.multiple_of(m * TILE, TILE)
            piece = pl.ds(base, TILE)
            pre[...] = dot(nall[tk, piece, :], up[...], 1, 1)
            logits = dot(nall[tk, piece, :], router[...], 1, 1)
            reach[...] = dot(grads[tk, piece, pl.ds(0, width)], down[...], 1, 1)
            chosen = grads[tk, piece, pl.ds(width, LANES)].astype(F32) > 0.5
            masked = jnp.where(chosen, logits, MASK_FILL)
            raw = jnp.where(
                chosen, jnp.exp(masked - jnp.max(masked, axis=1, keepdims=True)), 0.0
            )
            gates = raw / jnp.sum(raw, axis=1, keepdims=True)
            terms = []
            for _ in range(3):
                terms.append(gates.astype(BF16))
                gates = gates - terms[-1].astype(F32)
            gate[...] = dot(jnp.concatenate(terms, axis=1), wide[...], 1, 0)

            def slab(s, inner):
                at = pl.ds(pl.multiple_of(s * SLAB, SLAB), SLAB)
                to = pl.ds(pl.multiple_of(base + s * SLAB, SLAB), SLAB)
                for c in range(pre.shape[1] // LANES):
                    cols = pl.ds(c * LANES, LANES)
                    share = gate[at, cols]
                    act, slope = tanh_gelu(pre[at, cols])
                    act = act.astype(BF16).astype(F32)
                    pull = reach[at, cols]
                    gated[tk, to, cols] = (act * share).astype(BF16)
                    gpre[tk, to, cols] = (pull * share * slope).astype(BF16)
                    product = act * pull
                    coarse = product.astype(BF16)
                    high[at, cols] = coarse
                    low[at, cols] = (product - coarse.astype(F32)).astype(BF16)
                return inner

            lax.fori_loop(0, TILE // SLAB, slab, 0)
            dots = dot(pick, high[...], 1, 1) + dot(pick, low[...], 1, 1)
            for half in range(TILE // rows):
                bufs["dots"]["part"][k, m * (TILE // rows) + half] = dots[
                    :8, half * rows : (half + 1) * rows
                ]
            bufs["back"]["part"][k, piece, :] = dot(gpre[tk, piece, :], up[...], 1, 0).astype(BF16)
            if forth:
                bufs["forth"]["part"][k, piece, :] = dot(
                    gated[tk, piece, :], down[...], 1, 0
                ).astype(BF16)
            return carry

        lax.fori_loop(0, group // TILE, tile, 0)

    bufs["back"]["sum"], bufs["forth"]["sum"], bufs["dots"]["sum"] = back_sum, forth_sum, dots_sum

    def part_of(name):
        part = bufs[name]["part"]
        if name == "dots":
            return lambda k, index: part.at[k, index]
        return lambda k, index: part.at[k, block(index), :]

    streams = {
        name: Scatter(spots, bufs[name], part_of(name), ssend.at[n], srecv.at[n])
        for n, name in enumerate(("back", "dots", "forth") if forth else ("back", "dots"))
    }

    def first(k, which):
        for name in which:
            streams[name].first(k)

    def second(k, which):
        for name in which:
            streams[name].second(k)

    def third(k, which):
        for name in which:
            streams[name].third(k)

    def last(which):
        for name in which:
            streams[name].last()

    early = ("dots", "back")
    gather[0, 2].wait_recv()
    gather[0, 3].start()
    gather[1, 0].wait_recv()
    gather[1, 2].start()
    gather[1, 1].start()
    gather[0, 1].wait_recv()
    gather[0, 3].wait_recv()
    compute(0)
    first(0, early)
    gather[1, 2].wait_recv()
    gather[1, 3].start()
    for k in (2, 3):
        gather[k, 0].wait_recv()
        gather[k, 2].start()
        gather[k, 1].start()
    second(0, early)
    gather[1, 1].wait_recv()
    gather[1, 3].wait_recv()
    compute(1)
    first(1, early)
    for k in (2, 3):
        gather[k, 2].wait_recv()
        gather[k, 3].start()
    third(0, early)
    second(1, early)
    gather[2, 1].wait_recv()
    gather[2, 3].wait_recv()
    compute(2)
    first(2, early)
    third(1, early)
    second(2, early)
    gather[3, 1].wait_recv()
    gather[3, 3].wait_recv()
    compute(3)
    first(3, early)
    third(2, early)
    second(3, early)
    late = ("forth",) if forth else ()
    for k in range(4):
        first(k, late)
    third(3, early)
    for k in (1, 2, 3, 0):
        second(k, late)
    last(early)
    for k in (1, 2, 3, 0):
        third(k, late)
    last(late)
    copies = list(gather.values())
    for stream in streams.values():
        copies += list(stream.copies.values())
    for copy in copies:
        copy.wait_send()


def scatter_scratch(spans, kind, shape, part):
    return {
        "part": pltpu.VMEM((spans,) + part, kind),
        "near": pltpu.VMEM((spans, 2) + shape, kind),
        "out": pltpu.VMEM((spans, 2) + shape, kind),
        "far": pltpu.VMEM((spans, 2) + shape, kind),
    }


def experts_call(forth, normed, grads, up, down, router, wide):
    rows, width = normed.shape
    spans, group, _ = grads.shape
    hidden = up.shape[0]
    vmem = pl.BlockSpec(memory_space=pltpu.VMEM)

    return pl.pallas_call(
        functools.partial(experts_kernel, forth),
        out_shape=(
            jax.ShapeDtypeStruct((rows, width), F32),
            jax.ShapeDtypeStruct((rows, width) if forth else (8, LANES), F32),
            jax.ShapeDtypeStruct((8, rows), F32),
            jax.ShapeDtypeStruct((spans, group, width), BF16),
            jax.ShapeDtypeStruct((spans, group, hidden), BF16),
            jax.ShapeDtypeStruct((spans, group, hidden), BF16),
        ),
        in_specs=[vmem] * 6,
        out_specs=[vmem] * 6,
        scratch_shapes=experts_scratch(forth, spans, rows, group, width, hidden),
        compiler_params=pltpu.CompilerParams(
            collective_id=0, has_side_effects=True, vmem_limit_bytes=56 * 1024 * 1024
        ),
    )(normed, grads, up, down, router, wide)


def front_kernel(
    scale,
    tokens,
    packed,
    seg_down,
    seg_across,
    table,
    qkv_part,
    proj_part,
    up_part,
    down_part,
    small_part,
    wide,
    normed_group,
    qkv,
    probs,
    attended,
    middle,
    normed,
    qkv_full,
    proj_full,
    down_full,
    small_full,
    grads,
    back_sum,
    dots_sum,
    nall,
    gpre,
    gated,
    inputs,
    up_full,
    bias,
    mixed,
    xsend,
    xrecv,
    wsend,
    wrecv,
    csend,
    crecv,
    asend,
    arecv,
    forth_sum,
    *rest,
):
    spots = neighbours()
    f, i, t, sibling, across, along = spots
    peer, diagonal = (1 - f, i, t), (f, xor(i, 3), t)
    rows, width = tokens.shape
    group, own = inputs.shape[0], width // 2
    heads, hw = probs.shape[0], attended.shape[1]
    head, blocks = hw // heads, group // rows

    def block(index):
        return pl.ds(pl.multiple_of(index * rows, rows), rows)

    def half(index):
        return pl.ds(pl.multiple_of(index * own, LANES), own)

    ins = gather_copies(spots, tokens, lambda tt, ii: inputs.at[block(ii), :], xsend, xrecv, 1)
    cots = gather_copies(spots, packed, lambda tt, ii: grads.at[tt, block(ii), :], csend, crecv)

    def give(n, src, dst, target=peer):
        return remote(src, dst, wsend.at[n], wrecv.at[n], target)

    side = half(lax.rem(i, 2))
    other = proj_full.at[side, half(1 - f)]
    w_qkv = give(0, qkv_part, qkv_full.at[half(f), :])
    w_small = give(1, small_part, small_full.at[pl.ds(0, 16), half(f)])
    w_proj = give(2, proj_part.at[side, :], proj_full.at[side, half(f)])
    w_down = give(3, down_part, down_full.at[:, half(f)])
    w_up = give(4, up_part, up_full.at[:, half(f)])
    w_proj_on = give(5, other, other, sibling)
    swaps = [
        remote(attended.at[block(xor(i, j)), :], mixed.at[i], asend.at[j], arecv.at[j], target)
        for j, target in ((1, sibling), (2, across), (3, diagonal))
    ]

    small_full[...] = jnp.zeros_like(small_full)
    greet([sibling, across, diagonal, peer] + along[1:])
    ins[0, 2].start()
    ins[0, 1].start()
    w_small.start()
    w_qkv.start()
    for k in (1, 2, 3):
        cots[k, 0].start()
    w_proj.start()
    w_down.start()
    w_up.start()
    inputs[block(i), :] = tokens[...]
    grads[t, block(i), :] = packed[...]
    qkv_full[half(f), :] = qkv_part[...]
    small_full[pl.ds(0, 16), half(f)] = small_part[...]
    proj_full[:, half(f)] = proj_part[...]
    down_full[:, half(f)] = down_part[...]
    up_full[:, half(f)] = up_part[...]

    apart = lax.broadcasted_iota(jnp.int32, (rows, rows), 0) - lax.broadcasted_iota(
        jnp.int32, (rows, rows), 1
    )
    for h in range(heads):
        for n in range(2):
            value = jnp.full((rows, rows), table[i * heads + h, 0], F32)
            for number, bound in enumerate(BOUNDS, 1):
                value = jnp.where(apart + n * rows >= bound, table[i * heads + h, number], value)
            bias[n, h] = value

    ins[0, 2].wait_recv()
    ins[0, 3].start()
    cots[0, 2].start()
    cots[0, 1].start()
    w_small.wait_recv()
    ins[0, 1].wait_recv()
    ins[0, 3].wait_recv()

    def norm_tile(m, carry):
        at = pl.ds(pl.multiple_of(m * 64, 64), 64)
        value = inputs[at, :].astype(F32)
        gain = small_full[pl.ds(4, 1), :].astype(F32)
        normed_group[at, :] = (value * rms_scale(value) * gain).astype(BF16)
        return carry

    lax.fori_loop(0, group // 64, norm_tile, 0)
    w_qkv.wait_recv()
    for m in range(2):
        at = pl.ds(m * (group // 2), group // 2)
        qkv[at, :] = dot(normed_group[at, :], qkv_full[...], 1, 0).astype(BF16)

    def pass_on(k):
        cots[k, 0].wait_recv()
        cots[k, 2].start()
        cots[k, 1].start()

    def relay(k):
        cots[k, 2].wait_recv()
        cots[k, 3].start()

    pass_on(1)
    relay(0)
    for h in range(heads):
        cols = pl.ds(h * head, head)
        far = table[i * heads + h, BUCKETS - 1]
        for m in range(blocks):
            at, reach = pl.ds(m * rows, rows), (m + 1) * rows
            scores = dot(qkv[at, cols], qkv[pl.ds(0, reach), pl.ds(hw + h * head, head)], 1, 1)
            pieces = []
            for j in range(m + 1):
                allowed = seg_down[at, :] == seg_across[:, pl.ds(j * rows, rows)]
                if j == m:
                    allowed = allowed & (apart >= 0)
                add = bias[m - j, h] if m - j < 2 else far
                score = scores[:, j * rows : (j + 1) * rows] * scale + add
                pieces.append(jnp.where(allowed, score, MASK_FILL))
            scores = jnp.concatenate(pieces, axis=1)
            weights = jnp.exp(scores - jnp.max(scores, axis=1, keepdims=True))
            prob = weights / jnp.sum(weights, axis=1, keepdims=True)
            probs[h, at, pl.ds(0, reach)] = prob
            if reach < group:
                probs[h, at, pl.ds(reach, group - reach)] = jnp.zeros((rows, group - reach), F32)
            attended[at, cols] = dot(
                prob.astype(BF16), qkv[pl.ds(0, reach), pl.ds(2 * hw + h * head, head)], 1, 0
            ).astype(BF16)
        if h < 2:
            pass_on(2 + h)
            relay(1 + h)
    for swap in swaps:
        swap.start()
    mixed[i] = attended[block(i), :]
    w_proj.wait_recv()
    w_proj_on.start()
    relay(3)
    for swap in swaps:
        swap.wait_recv()
    w_proj_on.wait_recv()
    value = tokens[...].astype(F32)
    for j in range(blocks):
        value = value + dot(mixed[j], proj_full[pl.ds(j * hw, hw), :], 1, 0)
    middle[...] = value
    gain = small_full[pl.ds(5, 1), :].astype(F32)
    normed[...] = (value * rms_scale(value) * gain).astype(BF16)

    def ready(k):
        if k == 0:
            w_down.wait_recv()
            w_up.wait_recv()
        else:
            cots[k, 1].wait_recv()
            cots[k, 3].wait_recv()
        if k == 0:
            cots[0, 1].wait_recv()
            cots[0, 3].wait_recv()

    experts_kernel(
        False,
        normed,
        grads,
        up_full,
        down_full,
        small_full,
        wide,
        back_sum,
        forth_sum,
        dots_sum,
        nall,
        gpre,
        gated,
        *rest,
        ready=ready,
    )
    copies = list(ins.values()) + list(cots.values()) + swaps
    copies += [w_qkv, w_small, w_proj, w_down, w_up, w_proj_on]
    for copy in copies:
        copy.wait_send()


def front_call(scale, heads, hw, *operands):
    tokens, packed, seg_down = operands[:3]
    rows, width = tokens.shape
    group = seg_down.shape[0]
    spans, hidden = 4, operands[7].shape[0]
    vmem = pl.BlockSpec(memory_space=pltpu.VMEM)
    smem = pl.BlockSpec(memory_space=pltpu.SMEM)
    shape = jax.ShapeDtypeStruct
    dma = pltpu.SemaphoreType.DMA
    outs = (
        shape((group, width), BF16),
        shape((group, 3 * hw), BF16),
        shape((heads, group, group), F32),
        shape((group, hw), BF16),
        shape((rows, width), F32),
        shape((rows, width), BF16),
        shape((width, 3 * hw), BF16),
        shape((width, width), BF16),
        shape((hidden, width), BF16),
        shape((LANES, width), BF16),
        shape((spans, group, packed.shape[1]), BF16),
        shape((rows, width), F32),
        shape((8, rows), F32),
        shape((spans, group, width), BF16),
        shape((spans, group, hidden), BF16),
        shape((spans, group, hidden), BF16),
    )
    return pl.pallas_call(
        functools.partial(front_kernel, scale),
        out_shape=outs,
        in_specs=[smem if n == 4 else vmem for n in range(len(operands))],
        out_specs=[vmem] * len(outs),
        scratch_shapes=[
            pltpu.VMEM((group, width), BF16),
            pltpu.VMEM((hidden, width), BF16),
            pltpu.VMEM((2, heads, rows, rows), F32),
            pltpu.VMEM((4, rows, hw), BF16),
            dma((1, 4)),
            dma((1, 4)),
            dma((6,)),
            dma((6,)),
            dma((4, 4)),
            dma((4, 4)),
            dma((4,)),
            dma((4,)),
            pltpu.VMEM((8, LANES), F32),
        ]
        + experts_scratch(False, spans, rows, group, width, hidden),
        compiler_params=pltpu.CompilerParams(
            collective_id=2, has_side_effects=True, vmem_limit_bytes=60 * 1024 * 1024
        ),
    )(*operands)


def experts_scratch(forth, spans, rows, group, width, hidden):
    streams = {
        "back": scatter_scratch(spans, BF16, (rows, width), (group, width)),
        "dots": scatter_scratch(spans, F32, (8, rows), (4, 8, rows)),
        "forth": (
            scatter_scratch(spans, BF16, (rows, width), (group, width))
            if forth
            else {"sum": pltpu.SMEM((1,), F32)}
        ),
    }
    return [
        pltpu.VMEM((TILE, hidden), F32),
        pltpu.VMEM((TILE, hidden), F32),
        pltpu.VMEM((TILE, hidden), F32),
        pltpu.VMEM((TILE, hidden), BF16),
        pltpu.VMEM((TILE, hidden), BF16),
        streams,
        pltpu.SemaphoreType.DMA((4, 4)),
        pltpu.SemaphoreType.DMA((4, 4)),
        pltpu.SemaphoreType.DMA((3, 4, 4)),
        pltpu.SemaphoreType.DMA((3, 4, 4)),
    ]


def tail_kernel(
    scale,
    gmid_own,
    probs,
    qkv,
    attended,
    normed,
    wqkv,
    wproj,
    gated,
    gpre,
    nall,
    grads,
    down,
    xscaled,
    fixed,
    near_bucket,
    next_bucket,
    forth_sum,
    gone_sum,
    gup,
    gdown,
    wall,
    small,
    gmid,
    gatt,
    gqkv,
    gscore,
    wide_up,
    wide_down,
    half_send,
    half_recv,
    wfull,
    wsend,
    wrecv,
    wsum,
    zsend,
    zrecv,
    smalls,
    forth_buf,
    gone_buf,
    msend,
    mrecv,
    fsend,
    frecv,
    osend,
    orecv,
    xsend,
    xrecv,
    wgsend,
    wgrecv,
):
    spots = neighbours()
    f, i, t, sibling, across, along = spots
    peer = (1 - f, i, t)
    rows, width = gmid_own.shape
    spans, group, _ = nall.shape
    heads, hw = probs.shape[0], attended.shape[1]
    head = hw // heads
    own = width // 2
    piece = own // spans
    blocks = group // rows

    def block(index):
        return pl.ds(pl.multiple_of(index * rows, rows), rows)

    def half(index):
        return pl.ds(pl.multiple_of(index * own, LANES), own)

    mids = gather_copies(spots, gmid_own, lambda tt, ii: gmid.at[block(ii), :], msend, mrecv, 1)
    forth_buf["sum"], gone_buf["sum"] = forth_sum, gone_sum
    forth = Scatter(
        spots, forth_buf, lambda k, index: forth_buf["part"].at[k, block(index), :], fsend, frecv
    )
    gone = Scatter(
        spots, gone_buf, lambda k, index: gone_buf["part"].at[k, block(index), :], osend, orecv
    )
    halves = [
        remote(half_send[n], half_recv[n], xsend.at[n], xrecv.at[n], peer) for n in range(2)
    ]
    wx = [
        remote(wsend.at[n], wrecv.at[n], xsend.at[2 + n], xrecv.at[2 + n], peer) for n in range(2)
    ]
    wz = [
        {
            k: remote(
                zsend.at[n, pl.ds(pl.multiple_of(xor(t, k) * piece, 16), piece), :],
                zrecv.at[n, k],
                xsend.at[4 + 3 * n + k - 1],
                xrecv.at[4 + 3 * n + k - 1],
                along[k],
            )
            for k in (1, 2, 3)
        }
        for n in range(2)
    ]
    wg = [
        gather_copies(
            spots,
            wall.at[n, t, i],
            lambda tt, ii, n=n: wall.at[n, tt, ii],
            wgsend.at[n],
            wgrecv.at[n],
        )
        for n in range(2)
    ]
    steps = [
        remote(smalls.at[n], smalls.at[3 + n], xsend.at[10 + n], xrecv.at[10 + n], target)
        for n, target in enumerate((sibling, across, peer))
    ]
    rounds = [
        remote(small, smalls.at[5 + k], xsend.at[12 + k], xrecv.at[12 + k], along[k])
        for k in (1, 2, 3)
    ]

    greet([sibling, across, peer] + along[1:])
    gmid[block(i), :] = gmid_own[...]
    mids[0, 2].start()
    mids[0, 1].start()

    def forth_part(k):
        tk = xor(t, k)

        def tile(m, carry):
            at = pl.ds(pl.multiple_of(m * TILE, TILE), TILE)
            forth_buf["part"][k, at, :] = dot(gated[tk, at, :], down[...], 1, 0).astype(BF16)
            return carry

        lax.fori_loop(0, group // TILE, tile, 0)
        forth.first(k)

    def up_half(which, out):
        out[...] = jnp.zeros_like(out)

        def step(c, carry):
            out[...] += dot(nall[c, :, half(which)], gpre[c], 0, 0)
            return carry

        lax.fori_loop(0, spans, step, 0)

    def down_half(which, out):
        out[...] = jnp.zeros_like(out)

        def step(c, carry):
            out[...] += dot(gated[c], grads[c, :, half(which)], 0, 0)
            return carry

        lax.fori_loop(0, spans, step, 0)

    forth_part(1)
    forth_part(2)
    mids[0, 2].wait_recv()
    mids[0, 3].start()
    down_half(1 - f, wide_down)
    half_send[0][...] = wide_down[...].astype(BF16)
    halves[0].start()
    forth.second(1)
    forth_part(3)
    forth_part(0)
    forth.second(2)
    mids[0, 1].wait_recv()
    mids[0, 3].wait_recv()

    here = wproj[pl.ds(pl.multiple_of(i * hw, 16), hw), :]
    gatt[...] = dot(gmid[...], here, 1, 1).astype(BF16)
    wfull[0, :, pl.ds(0, hw)] = dot(gmid[...], attended[...], 0, 0)
    for h in range(heads):
        cols = pl.ds(h * head, head)
        gqkv[:, pl.ds(2 * hw + h * head, head)] = dot(
            probs[h].astype(BF16), gatt[:, cols], 0, 0
        ).astype(BF16)
    wfull[0, :, pl.ds(hw, hw)] = dot(normed[...], gqkv[:, pl.ds(2 * hw, hw)], 0, 0)
    wsend[0] = wfull[0, half(1 - f), :].astype(BF16)
    wx[0].start()
    forth.second(3)
    forth.second(0)
    forth.third(1)

    table = small.at[pl.ds(0, heads * BUCKETS), :]
    for h in range(heads):
        cols = pl.ds(h * head, head)
        keys = pl.ds(hw + h * head, head)

        def rowtile(m, carry, h=h, cols=cols, keys=keys):
            at = block(m)
            grad_probs = dot(gatt[at, cols], qkv[:, pl.ds(2 * hw + h * head, head)], 1, 1)
            prob = probs[h, at, :]
            inner = jnp.sum(prob * grad_probs, axis=1, keepdims=True)
            score = (prob * (grad_probs - inner)).astype(BF16)
            gscore[h, at, :] = score
            gqkv[at, cols] = (dot(score, qkv[:, keys], 1, 0) * scale).astype(BF16)
            return carry

        lax.fori_loop(0, blocks, rowtile, 0)
        gqkv[:, keys] = (dot(gscore[h], qkv[:, cols], 0, 0) * scale).astype(BF16)
        if h == 0:
            forth.third(2)
        if h == 1:
            forth.third(3)

    def gone_tile(m, carry):
        at = block(m)
        gone_buf["part"][0, at, :] = dot(gqkv[at, :], wqkv[...], 1, 1).astype(BF16)
        return carry

    lax.fori_loop(0, blocks, gone_tile, 0)
    gone.first(0)
    wfull[1] = dot(normed[...], gqkv[:, pl.ds(0, 2 * hw)], 0, 0)
    wsend[1] = wfull[1, half(1 - f), :].astype(BF16)
    wx[1].start()
    gone.second(0)
    up_half(1 - f, wide_up)
    half_send[1][...] = wide_up[...].astype(BF16)
    halves[1].start()

    def reduce_along(n):
        wx[n].wait_recv()
        total = wfull[n, half(f), :] + wrecv[n].astype(F32)
        wsum[n] = total
        zsend[n] = total.astype(BF16)
        for k in (1, 2, 3):
            wz[n][k].start()

    def share(n):
        total = wsum[n, pl.ds(pl.multiple_of(t * piece, 16), piece), :]
        for k in (1, 2, 3):
            wz[n][k].wait_recv()
            total = total + zrecv[n, k].astype(F32)
        wall[n, t, i] = total.astype(BF16)
        wg[n][0, 2].start()
        wg[n][0, 1].start()
        for k in (1, 2, 3):
            wg[n][k, 0].start()

    def onward(n):
        for k in (1, 2, 3):
            wg[n][k, 0].wait_recv()
            wg[n][k, 2].start()
            wg[n][k, 1].start()

    def relay(n):
        for k in range(4):
            wg[n][k, 2].wait_recv()
            wg[n][k, 3].start()

    reduce_along(0)
    forth.third(0)

    def bucket_sums(h):
        near = jnp.zeros((rows, rows), F32)
        after = jnp.zeros((rows, rows), F32)
        far = jnp.zeros((rows, rows), F32)
        for a in range(blocks):
            for b in range(a + 1):
                score = gscore[h, pl.ds(a * rows, rows), pl.ds(b * rows, rows)].astype(F32)
                if a == b:
                    near = near + score
                elif a == b + 1:
                    after = after + score
                else:
                    far = far + score
        sums = []
        for b in range(BUCKETS):
            value = jnp.where(near_bucket[...] == b, near, 0.0) + jnp.where(
                next_bucket[...] == b, after, 0.0
            )
            if b == BUCKETS - 1:
                value = value + far
            sums.append(jnp.sum(value, axis=0, keepdims=True))
        sums = jnp.sum(jnp.concatenate(sums, axis=0), axis=1, keepdims=True)
        lane = lax.broadcasted_iota(jnp.int32, (BUCKETS, LANES), 1)
        smalls[0, pl.ds(h * BUCKETS, BUCKETS), :] = jnp.where(lane == i, sums, 0.0)

    for h in range(heads):
        bucket_sums(h)
    gone.third(0)
    gain = jnp.sum(gone_sum[...] * xscaled[...], axis=0, keepdims=True)
    base = heads * BUCKETS
    smalls[0, pl.ds(base, smalls.shape[1] - base), :] = fixed[...]
    for c in range(width // LANES):
        smalls[0, pl.ds(base + c, 1), :] = gain[:, c * LANES : (c + 1) * LANES]
    share(0)
    steps[0].start()
    down_half(f, gdown)
    reduce_along(1)
    up_half(f, gup)
    steps[0].wait_recv()
    smalls[1] = smalls[0] + smalls[3]
    steps[1].start()
    onward(0)
    share(1)
    steps[1].wait_recv()
    smalls[2] = smalls[1] + smalls[4]
    steps[2].start()
    relay(0)
    steps[2].wait_recv()
    small[...] = smalls[2] + smalls[5]
    for copy in rounds:
        copy.start()
    onward(1)
    forth.last()
    relay(1)
    for copy in rounds:
        copy.wait()
    small[...] = small[...] + smalls[6] + smalls[7] + smalls[8]
    halves[0].wait_recv()
    gdown[...] = gdown[...] + half_recv[0][...].astype(F32)
    halves[1].wait_recv()
    gup[...] = gup[...] + half_recv[1][...].astype(F32)
    for n in range(2):
        for k in range(4):
            wg[n][k, 1].wait_recv()
            wg[n][k, 3].wait_recv()
    copies = halves + wx + steps + list(mids.values())
    copies += list(forth.copies.values()) + list(gone.copies.values())
    for n in range(2):
        copies += list(wz[n].values()) + list(wg[n].values())
    for copy in copies:
        copy.wait_send()


def tail_call(scale, *operands):
    gmid, probs, qkv, attended, normed, wqkv, wproj, gated, gpre, nall = operands[:10]
    rows, width = gmid.shape
    spans, group, hidden = gpre.shape
    heads = probs.shape[0]
    hw = attended.shape[1]
    own = width // 2
    piece = own // spans
    extra = 8 * width // LANES
    vmem = pl.BlockSpec(memory_space=pltpu.VMEM)
    shape = jax.ShapeDtypeStruct
    dma = pltpu.SemaphoreType.DMA
    table = heads * BUCKETS + extra
    return pl.pallas_call(
        functools.partial(tail_kernel, scale),
        out_shape=(
            shape((rows, width), F32),
            shape((rows, width), F32),
            shape((own, hidden), F32),
            shape((hidden, own), F32),
            shape((2, spans, 4, piece, 2 * hw), BF16),
            shape((table, LANES), F32),
        ),
        in_specs=[vmem] * len(operands),
        out_specs=[vmem] * 6,
        scratch_shapes=[
            pltpu.VMEM((group, width), BF16),
            pltpu.VMEM((group, hw), BF16),
            pltpu.VMEM((group, 3 * hw), BF16),
            pltpu.VMEM((heads, group, group), BF16),
            pltpu.VMEM((own, hidden), F32),
            pltpu.VMEM((hidden, own), F32),
            [pltpu.VMEM((hidden, own), BF16), pltpu.VMEM((own, hidden), BF16)],
            [pltpu.VMEM((hidden, own), BF16), pltpu.VMEM((own, hidden), BF16)],
            pltpu.VMEM((2, width, 2 * hw), F32),
            pltpu.VMEM((2, own, 2 * hw), BF16),
            pltpu.VMEM((2, own, 2 * hw), BF16),
            pltpu.VMEM((2, own, 2 * hw), F32),
            pltpu.VMEM((2, own, 2 * hw), BF16),
            pltpu.VMEM((2, 4, piece, 2 * hw), BF16),
            pltpu.VMEM((9, table, LANES), F32),
            scatter_scratch(spans, BF16, (rows, width), (group, width)),
            scatter_scratch(1, BF16, (rows, width), (group, width)),
            dma((1, 4)),
            dma((1, 4)),
            dma((spans, 4)),
            dma((spans, 4)),
            dma((1, 4)),
            dma((1, 4)),
            dma((16,)),
            dma((16,)),
            dma((2, 4, 4)),
            dma((2, 4, 4)),
        ],
        compiler_params=pltpu.CompilerParams(
            collective_id=1, has_side_effects=True, vmem_limit_bytes=58 * 1024 * 1024
        ),
    )(*operands)


def local(
    tokens,
    seg_ids,
    routes,
    norm_attn,
    weight_qkv,
    weight_proj,
    rel_table,
    norm_ffn,
    weight_router,
    expert_up,
    expert_down,
    cotangent,
):
    rows = tokens.shape[1]
    width = tokens.shape[2]
    heads = rel_table.shape[0]
    head_size = width // heads
    ctx_count = lax.axis_size("ctx")
    heads_here = heads // ctx_count
    hw = heads_here * head_size
    experts = expert_up.shape[0]
    units = expert_up.shape[2]
    length = seg_ids.shape[1]
    score_scale = head_size ** (-0.5)
    ctx_index = lax.axis_index("ctx")
    fsdp_index = lax.axis_index("fsdp")
    own_width = norm_attn.shape[0]
    world = ("ctx", "tp")

    tp_count = lax.axis_size("tp")
    pair = lax.axis_size("fsdp") == 2
    segment = seg_ids[0]
    inputs = tokens[0].astype(F32)
    scale_one = rms_scale(inputs)
    qkv_part = jnp.concatenate(
        [
            lax.dynamic_slice_in_dim(weight_qkv, s * width + ctx_index * hw, hw, 1)
            for s in range(3)
        ],
        axis=1,
    )
    expert_ids = jnp.arange(LANES, dtype=jnp.int32)[None, :]
    named = (routes[0][:, 0:1] == expert_ids) | (routes[0][:, 1:2] == expert_ids)
    packed_grad = jnp.concatenate([cotangent[0], named.astype(BF16)], axis=1)
    block = MAX_DISTANCE
    offset = (
        lax.broadcasted_iota(jnp.int32, (1, block, block), 1)
        - lax.broadcasted_iota(jnp.int32, (1, block, block), 2)
    )

    hidden = experts * units
    wide = (
        jnp.arange(hidden, dtype=jnp.int32)[None, :] // units
        == jnp.arange(3 * LANES, dtype=jnp.int32)[:, None] % LANES
    ).astype(BF16)
    if pair:
        up_part = jnp.swapaxes(expert_up, 1, 2).reshape(hidden, own_width)
        small_part = jnp.concatenate(
            [
                weight_router.T,
                norm_attn[None],
                norm_ffn[None],
                jnp.zeros((14 - experts, own_width), BF16),
            ],
            axis=0,
        )
        (
            normed_group,
            projected,
            probs,
            attended,
            middle,
            normed_two,
            qkv_here,
            proj_full,
            down,
            small,
            grads_all,
            grad_normed_two,
            dots_own,
            normed_all,
            grad_pre,
            gated,
        ) = front_call(
            score_scale,
            heads_here,
            hw,
            tokens[0],
            packed_grad,
            jnp.broadcast_to(segment[:, None], (length, LANES)),
            seg_ids,
            rel_table,
            qkv_part,
            weight_proj,
            up_part,
            expert_down.reshape(hidden, own_width),
            small_part,
            wide,
        )
        gain_one = small[experts].astype(F32)
        gain_two = small[experts + 1].astype(F32)
        router_t = small[:experts]
        scale_two = rms_scale(middle)
    else:
        token_group = lax.all_gather(tokens[0], "ctx", axis=0, tiled=True)
        small = jnp.concatenate([norm_attn[None], norm_ffn[None], weight_router.T], axis=0)
        small = gather(small, "fsdp", 1)
        gain_one = small[0].astype(F32)
        gain_two = small[1].astype(F32)
        router_t = small[2:]
        qkv_here = gather(qkv_part, "fsdp", 0)
        proj_full = gather(weight_proj, "fsdp", 1)
        up_t = gather(
            jnp.swapaxes(expert_up, 1, 2).reshape(experts * units, own_width), "fsdp", 1
        )
        down = gather(expert_down.reshape(experts * units, own_width), "fsdp", 1)
        grad_routes = lax.all_gather(packed_grad, ("tp", "ctx"), axis=0, tiled=True)

        table_here = lax.dynamic_slice_in_dim(rel_table, ctx_index * heads_here, heads_here, 0)
        def bias_block(distance):
            value = jnp.broadcast_to(table_here[:, 0][:, None, None], (heads_here, block, block))
            for number, bound in enumerate(BOUNDS, 1):
                value = jnp.where(distance >= bound, table_here[:, number][:, None, None], value)
            return value

        near = bias_block(offset)
        next_near = bias_block(offset + block)
        far = jnp.broadcast_to(table_here[:, BUCKETS - 1][:, None, None], (heads_here, block, block))
        blocks = length // block
        picks = {0: near, 1: next_near}
        bias = jnp.concatenate(
            [
                jnp.concatenate(
                    [picks.get(i - j, far) for j in range(blocks)],
                    axis=2,
                )
                for i in range(blocks)
            ],
            axis=1,
        )
        positions = jnp.arange(length, dtype=jnp.int32)
        allowed = (segment[:, None] == segment[None, :]) & (positions[:, None] >= positions[None, :])
        bias = jnp.where(allowed[None], bias, MASK_FILL)

        inputs_group = token_group.astype(F32)
        normed_group = (inputs_group * rms_scale(inputs_group) * gain_one).astype(BF16)
        projected = dot(normed_group, qkv_here, 1, 0).astype(BF16)
        by_head = projected.reshape(length, 3, heads_here, head_size)
        query, key, value = by_head[:, 0], by_head[:, 1], by_head[:, 2]

        scores = (
            jnp.einsum("qhd,khd->hqk", query, key, preferred_element_type=F32) * score_scale + bias
        )
        peak = jnp.max(scores, axis=-1, keepdims=True)
        weights = jnp.exp(scores - peak)
        probs = weights / jnp.sum(weights, axis=-1, keepdims=True)
        low_probs = probs.astype(BF16)
        attended = (
            jnp.einsum("hqk,khd->qhd", low_probs, value, preferred_element_type=F32)
            .astype(BF16)
            .reshape(length, hw)
        )
        mixed = lax.all_to_all(attended, "ctx", split_axis=0, concat_axis=1, tiled=True)
        mixed, grad_routes, up_t, down = lax.optimization_barrier((mixed, grad_routes, up_t, down))
        middle = inputs + dot(mixed, proj_full, 1, 0)
        scale_two = rms_scale(middle)
        normed_two = (middle * scale_two * gain_two).astype(BF16)

        router_pad = jnp.pad(router_t, ((0, LANES - experts), (0, 0)))
        grad_normed_two, result, dots_own, normed_all, grad_pre, gated = experts_call(
            True,
            normed_two,
            grad_routes.reshape(tp_count, length, width + LANES),
            up_t,
            down,
            router_pad,
            wide,
        )
    def gates_of(normed, route):
        logits = dot(normed, router_t, 1, 1)
        number = lax.broadcasted_iota(jnp.int32, (1, experts), 1)
        chosen = (route[:, 0:1] == number) | (route[:, 1:2] == number)
        masked = jnp.where(chosen, logits, MASK_FILL)
        raw = jnp.where(chosen, jnp.exp(masked - jnp.max(masked, axis=1, keepdims=True)), 0.0)
        return raw / jnp.sum(raw, axis=1, keepdims=True)

    gate_dots = dots_own[:experts].T
    total_rows = tp_count * length
    grad_out = cotangent[0].astype(F32)
    gates = gates_of(normed_two, routes[0])
    grad_logits = gates * (gate_dots - jnp.sum(gates * gate_dots, axis=1, keepdims=True))
    grad_normed_two = grad_normed_two + jnp.dot(
        grad_logits, router_t.astype(F32), precision=lax.Precision.HIGHEST
    )
    grad_router = lax.dot_general(
        grad_logits,
        normed_two.astype(F32),
        (((0,), (0,)), ((), ())),
        precision=lax.Precision.HIGHEST,
    )
    weighted_two = grad_normed_two * gain_two
    grad_gain_two = jnp.sum(grad_normed_two * middle * scale_two, axis=0)
    grad_middle = (
        grad_out
        + scale_two * weighted_two
        - middle * scale_two**3 * jnp.mean(weighted_two * middle, axis=1, keepdims=True)
    )
    if pair:
        lows = jnp.asarray(np.array(BOUNDS, np.int32))[:, None, None]
        near_bucket = jnp.sum((offset >= lows).astype(jnp.int32), axis=0)
        near_bucket = jnp.where(offset[0] >= 0, near_bucket, -1)
        next_bucket = jnp.sum((offset + block >= lows).astype(jnp.int32), axis=0)
        fixed = jnp.concatenate(
            [
                jnp.zeros((width,), F32),
                grad_gain_two,
                grad_router.reshape(-1),
                jnp.zeros((2 * width,), F32),
            ]
        ).reshape(-1, LANES)
        result, grad_normed_one, grad_up, grad_down, weight_all, packed = tail_call(
            score_scale,
            grad_middle.astype(BF16),
            probs,
            projected,
            attended,
            normed_group,
            qkv_here,
            proj_full,
            gated,
            grad_pre,
            normed_all,
            grads_all,
            down,
            inputs * scale_one,
            fixed,
            near_bucket,
            next_bucket,
        )
        output = (middle + result).astype(BF16)[None]
        weighted_one = grad_normed_one * gain_one
        grad_tokens = (
            grad_middle
            + scale_one * weighted_one
            - inputs * scale_one**3 * jnp.mean(weighted_one * inputs, axis=1, keepdims=True)
        )
        grad_up = jnp.stack([grad_up[:, e * units : (e + 1) * units] for e in range(experts)])
        grad_down = grad_down.reshape(experts, units, own_width)
        weights = jnp.transpose(weight_all, (0, 2, 1, 3, 4)).reshape(
            2, ctx_count, own_width, 2 * hw
        )
        parts = [
            weights[1, :, :, :hw],
            weights[1, :, :, hw:],
            weights[0, :, :, hw:],
        ]
        grad_weight_qkv = jnp.concatenate(
            [part[c] for part in parts for c in range(ctx_count)], axis=1
        ).astype(F32)
        grad_weight_proj = (
            jnp.swapaxes(weights[0, :, :, :hw], 1, 2).reshape(width, own_width).astype(F32)
        )
        edge = heads_here * BUCKETS
        table_grad = packed[:edge, :ctx_count].T.reshape(heads, BUCKETS)
        gains = packed[edge:].reshape(-1, width)
        gains = lax.dynamic_slice_in_dim(gains, fsdp_index * own_width, own_width, 1)
        return (
            output,
            grad_tokens[None],
            gains[0],
            grad_weight_qkv,
            grad_weight_proj,
            table_grad,
            gains[1],
            gains[2 : 2 + experts].T,
            grad_up,
            grad_down,
        )
    normed_all = normed_all.reshape(total_rows, width)
    grad_pre = grad_pre.reshape(total_rows, hidden)
    gated = gated.reshape(total_rows, hidden)
    grad_all = grad_routes[:, :width]
    grad_up = exchange_sum(dot(grad_pre, normed_all, 0, 0), "fsdp", 1)
    grad_up = jnp.swapaxes(grad_up.reshape(experts, units, own_width), 1, 2)
    grad_down = exchange_sum(dot(gated, grad_all, 0, 0), "fsdp", 1)
    grad_down = grad_down.reshape(experts, units, own_width)

    grad_mid_group = lax.all_gather(grad_middle.astype(BF16), "ctx", axis=0, tiled=True)
    proj_rows = lax.dynamic_slice_in_dim(proj_full, ctx_index * hw, hw, 0)
    grad_attended = dot(grad_mid_group, proj_rows, 1, 1).astype(BF16)
    grad_heads = grad_attended.reshape(length, heads_here, head_size)
    grad_value = jnp.einsum("hqk,qhd->khd", low_probs, grad_heads, preferred_element_type=F32)
    grad_probs = jnp.einsum("qhd,khd->hqk", grad_heads, value, preferred_element_type=F32)
    grad_scores = (
        probs * (grad_probs - jnp.sum(probs * grad_probs, axis=-1, keepdims=True))
    ).astype(BF16)
    grad_query = (
        jnp.einsum("hqk,khd->qhd", grad_scores, key, preferred_element_type=F32) * score_scale
    )
    grad_key = (
        jnp.einsum("hqk,qhd->khd", grad_scores, query, preferred_element_type=F32) * score_scale
    )
    grad_qkv = jnp.concatenate(
        [
            grad_query.astype(BF16).reshape(length, hw),
            grad_key.astype(BF16).reshape(length, hw),
            grad_value.astype(BF16).reshape(length, hw),
        ],
        axis=1,
    )
    grad_normed_one = exchange_sum(dot(grad_qkv, qkv_here, 1, 1), "ctx", 0)

    weight_part = jnp.concatenate(
        [dot(normed_group, grad_qkv, 0, 0), dot(grad_mid_group, attended, 0, 0)], axis=1
    )
    weight_own = exchange_sum(weight_part, "fsdp", 0)
    grad_scores, weight_own = lax.optimization_barrier((grad_scores, weight_own))
    weight_own = exchange_sum(weight_own, "tp", 0).astype(BF16)
    def score_block(i, j):
        return grad_scores[
            :, i * block : (i + 1) * block, j * block : (j + 1) * block
        ].astype(F32)

    near_sum = sum(score_block(i, i) for i in range(blocks))
    next_sum = sum(score_block(i + 1, i) for i in range(blocks - 1))
    far_sum = sum(
        jnp.sum(score_block(i, j), axis=(1, 2)) for i in range(blocks) for j in range(i - 1)
    )
    lows = [0] + BOUNDS
    highs = BOUNDS + [2 * block]
    bucket_sums = [
        jnp.sum(jnp.where((offset >= lo) & (offset < hi), near_sum, 0.0), axis=(1, 2))
        + jnp.sum(
            jnp.where((offset + block >= lo) & (offset + block < hi), next_sum, 0.0), axis=(1, 2)
        )
        for lo, hi in zip(lows, highs)
    ]
    bucket_sums[-1] = bucket_sums[-1] + far_sum
    table_here_grad = jnp.stack(bucket_sums, axis=1)
    table_term = lax.dynamic_update_slice_in_dim(
        jnp.zeros((heads, BUCKETS), F32), table_here_grad, ctx_index * heads_here, 0
    )

    weighted_one = grad_normed_one * gain_one
    grad_gain_one = jnp.sum(grad_normed_one * inputs * scale_one, axis=0)
    grad_tokens = (
        grad_middle
        + scale_one * weighted_one
        - inputs * scale_one**3 * jnp.mean(weighted_one * inputs, axis=1, keepdims=True)
    )
    packed = jnp.concatenate(
        [
            grad_gain_one,
            grad_gain_two,
            grad_router.reshape(-1),
            table_term.reshape(-1),
        ]
    ).reshape(-1, 128)
    packed, weight_own = lax.optimization_barrier((packed, weight_own))
    packed = lax.psum(packed, ("fsdp", "ctx", "tp")).reshape(-1)
    packed, result = lax.optimization_barrier((packed, result))
    output = (middle + result).astype(BF16)[None]
    weight_all = lax.all_gather(weight_own, world, axis=0, tiled=True).astype(F32)
    weight_all = weight_all.reshape(ctx_count, own_width, 4 * hw)
    grad_weight_qkv = jnp.concatenate(
        [
            weight_all[c, :, s * hw : (s + 1) * hw]
            for s in range(3)
            for c in range(ctx_count)
        ],
        axis=1,
    )
    grad_weight_proj = jnp.swapaxes(weight_all[:, :, 3 * hw :], 1, 2).reshape(width, own_width)
    gains = packed[: (2 + experts) * width].reshape(2 + experts, width)
    gains = lax.dynamic_slice_in_dim(gains, fsdp_index * own_width, own_width, 1)
    table_grad = packed[(2 + experts) * width :].reshape(heads, BUCKETS)
    return (
        output,
        grad_tokens[None],
        gains[0],
        grad_weight_qkv,
        grad_weight_proj,
        table_grad,
        gains[1],
        gains[2:].T,
        grad_up,
        grad_down,
    )


def solution(mesh):
    rows = P(("fsdp", "tp"), "ctx", None)
    in_specs = (
        rows,
        P(("fsdp", "tp"), None),
        rows,
        P("fsdp"),
        P("fsdp", None),
        P(None, "fsdp"),
        P(),
        P("fsdp"),
        P("fsdp", None),
        P(None, "fsdp", ("ctx", "tp")),
        P(None, ("ctx", "tp"), "fsdp"),
        rows,
    )
    out_specs = (
        rows,
        rows,
        P("fsdp"),
        P("fsdp", None),
        P(None, "fsdp"),
        P(),
        P("fsdp"),
        P("fsdp", None),
        P(None, "fsdp", ("ctx", "tp")),
        P(None, ("ctx", "tp"), "fsdp"),
    )
    return jax.shard_map(local, mesh=mesh, in_specs=in_specs, out_specs=out_specs, check_vma=False)
```

```python
import functools

import jax
import jax.numpy as jnp
import numpy as np
from jax import lax
from jax.experimental import pallas as pl
from jax.experimental.pallas import tpu as pltpu
from jax.sharding import PartitionSpec as P

BUCKETS = 32
MAX_DISTANCE = 128
EPSILON = 1e-06
MASK_FILL = -1e30
F32 = jnp.float32
BF16 = jnp.bfloat16


def bucket_bounds(buckets, far_reach):
    exact_count = buckets // 2
    bounds = []
    for number in range(1, buckets):
        if number <= exact_count:
            bounds.append(number)
        else:
            exponent = (number - exact_count) / (buckets - exact_count)
            bounds.append(int(np.ceil(exact_count * (far_reach / exact_count) ** exponent)))
    return bounds


BOUNDS = bucket_bounds(BUCKETS, MAX_DISTANCE)


def rms_scale(values):
    return lax.rsqrt(jnp.mean(values * values, axis=-1, keepdims=True) + EPSILON)


def dot(a, b, ca, cb):
    return lax.dot_general(a, b, (((ca,), (cb,)), ((), ())), preferred_element_type=F32)


def gather(shard, axis, dim):
    count = lax.axis_size(axis)
    size = shard.shape[dim]
    me = lax.axis_index(axis)
    pieces = [shard] + [
        lax.ppermute(shard, axis, [(i, (i + step) % count) for i in range(count)])
        for step in range(1, count)
    ]
    if count == 2:
        first = me == 0
        return jnp.concatenate(
            [jnp.where(first, pieces[0], pieces[1]), jnp.where(first, pieces[1], pieces[0])],
            axis=dim,
        )
    shape = list(shard.shape)
    shape[dim] = count * size
    whole = jnp.zeros(shape, shard.dtype)
    for step, piece in enumerate(pieces):
        source = lax.rem(me + count - step, count)
        whole = lax.dynamic_update_slice_in_dim(whole, piece, source * size, dim)
    return whole


def exchange_sum(part, axis, dim, kind=BF16):
    count = lax.axis_size(axis)
    size = part.shape[dim] // count
    me = lax.axis_index(axis)
    total = lax.dynamic_slice_in_dim(part, me * size, size, dim).astype(F32)
    for step in range(1, count):
        target = lax.rem(me + step, count)
        piece = lax.dynamic_slice_in_dim(part, target * size, size, dim).astype(kind)
        total = total + lax.ppermute(
            piece, axis, [(i, (i + step) % count) for i in range(count)]
        ).astype(F32)
    return total


MESH = pl.DeviceIdType.MESH
TILE = 256
SLAB = 32
LANES = 128


def flip(value, bit):
    return value + bit - 2 * bit * lax.rem(lax.div(value, bit), 2)


def xor(value, mask):
    for bit in (1, 2):
        if mask & bit:
            value = flip(value, bit)
    return value


def place():
    return lax.axis_index("fsdp"), lax.axis_index("ctx"), lax.axis_index("tp")


def remote(src, dst, send, recv, target):
    return pltpu.make_async_remote_copy(
        src_ref=src,
        dst_ref=dst,
        send_sem=send,
        recv_sem=recv,
        device_id=target,
        device_id_type=MESH,
    )


def greet(targets):
    barrier = pltpu.get_barrier_semaphore()
    for target in targets:
        pl.semaphore_signal(barrier, inc=1, device_id=target, device_id_type=MESH)
    pl.semaphore_wait(barrier, len(targets))


def tanh_gelu(u):
    first = 0.7978845608028654
    cubic = 0.044715 * first
    square = u * u
    wave = jnp.tanh(u * (first + cubic * square))
    half = 0.5 + 0.5 * wave
    slope = half + (0.5 * u) * (1.0 - wave * wave) * (first + 3.0 * cubic * square)
    return u * half, slope


def gather_copies(spots, source, slot, send, recv, spans=4):
    f, i, t, sibling, across, along = spots

    def one(k, j):
        ends = send.at[k, j], recv.at[k, j]
        if j == 0:
            return remote(source, slot(t, i), *ends, along[k])
        here = slot(xor(t, k), i if j < 3 else flip(i, 2))
        origin = source if (k == 0 and j < 3) else here
        return remote(origin, here, *ends, across if j == 2 else sibling)

    return {(k, j): one(k, j) for k in range(spans) for j in range(4) if (k, j) != (0, 0)}


def neighbours():
    f, i, t = place()
    along = [None] + [(f, i, xor(t, k)) for k in (1, 2, 3)]
    return f, i, t, (f, flip(i, 1), t), (f, flip(i, 2), t), along


class Scatter:
    def __init__(self, spots, buf, part, send, recv):
        f, self.i, t, sibling, across, along = spots
        self.buf, self.part = buf, part
        self.copies = {}
        for k in range(buf["near"].shape[0]):
            for stage in range(4 if k else 3):
                ends = send.at[k, stage], recv.at[k, stage]
                if stage < 2:
                    src = part(k, xor(self.i, 1 if stage == 0 else 3))
                    copy = remote(src, buf["near"].at[k, stage], *ends, sibling)
                elif stage == 2:
                    copy = remote(buf["out"].at[k, 0], buf["far"].at[k, 0], *ends, across)
                else:
                    copy = remote(buf["out"].at[k, 1], buf["far"].at[k, 1], *ends, along[k])
                self.copies[k, stage] = copy

    def first(self, k):
        self.copies[k, 1].start()
        self.copies[k, 0].start()

    def second(self, k):
        b = self.buf
        self.copies[k, 1].wait_recv()
        total = self.part(k, flip(self.i, 2))[...].astype(F32) + b["near"][k, 1].astype(F32)
        b["out"][k, 0] = total.astype(b["out"].dtype)
        self.copies[k, 2].start()

    def third(self, k):
        b = self.buf
        self.copies[k, 0].wait_recv()
        self.copies[k, 2].wait_recv()
        total = (
            self.part(k, self.i)[...].astype(F32)
            + b["near"][k, 0].astype(F32)
            + b["far"][k, 0].astype(F32)
        )
        if k == 0:
            b["sum"][...] = total
        else:
            b["out"][k, 1] = total.astype(b["out"].dtype)
            self.copies[k, 3].start()

    def last(self):
        b = self.buf
        for k in (1, 2, 3):
            self.copies[k, 3].wait_recv()
            b["sum"][...] = b["sum"][...] + b["far"][k, 1].astype(F32)


def gates_of(logits, chosen):
    masked = jnp.where(chosen, logits, MASK_FILL)
    raw = jnp.where(chosen, jnp.exp(masked - jnp.max(masked, axis=1, keepdims=True)), 0.0)
    return raw / jnp.sum(raw, axis=1, keepdims=True)


def experts_kernel(
    forth,
    normed,
    grads,
    up,
    down,
    router,
    wide,
    back_sum,
    forth_sum,
    dots_sum,
    nall,
    gpre,
    gated,
    pre,
    reach,
    gate,
    high,
    low,
    bufs,
    gsend,
    grecv,
    ssend,
    srecv,
    ready=None,
):
    spots = neighbours()
    f, i, t, sibling, across, along = spots
    rows, width = normed.shape
    group = nall.shape[1]

    def block(index):
        return pl.ds(pl.multiple_of(index * rows, rows), rows)

    if ready is None:
        greet([sibling, across] + along[1:])
    gather = gather_copies(
        spots, normed, lambda tt, ii: nall.at[tt, block(ii), :], gsend, grecv
    )
    nall[t, block(i), :] = normed[...]
    gather[0, 2].start()
    gather[0, 1].start()
    for k in (1, 2, 3):
        gather[k, 0].start()

    pick = wide[pl.ds(0, SLAB), :]

    def compute(k):
        tk = xor(t, k)
        if ready is not None:
            ready(k)

        def tile(m, carry):
            base = pl.multiple_of(m * TILE, TILE)
            piece = pl.ds(base, TILE)
            pre[...] = dot(nall[tk, piece, :], up[...], 1, 1)
            logits = dot(nall[tk, piece, :], router[...], 1, 1)
            reach[...] = dot(grads[tk, piece, pl.ds(0, width)], down[...], 1, 1)
            chosen = grads[tk, piece, pl.ds(width, LANES)].astype(F32) > 0.5
            gates = gates_of(logits, chosen)
            terms = []
            for _ in range(3):
                terms.append(gates.astype(BF16))
                gates = gates - terms[-1].astype(F32)
            gate[...] = dot(jnp.concatenate(terms, axis=1), wide[...], 1, 0)

            def slab(s, inner):
                at = pl.ds(pl.multiple_of(s * SLAB, SLAB), SLAB)
                to = pl.ds(pl.multiple_of(base + s * SLAB, SLAB), SLAB)
                for c in range(pre.shape[1] // LANES):
                    cols = pl.ds(c * LANES, LANES)
                    share = gate[at, cols]
                    act, slope = tanh_gelu(pre[at, cols])
                    act = act.astype(BF16).astype(F32)
                    pull = reach[at, cols]
                    gated[tk, to, cols] = (act * share).astype(BF16)
                    gpre[tk, to, cols] = (pull * share * slope).astype(BF16)
                    product = act * pull
                    coarse = product.astype(BF16)
                    high[at, cols] = coarse
                    low[at, cols] = (product - coarse.astype(F32)).astype(BF16)
                return inner

            lax.fori_loop(0, TILE // SLAB, slab, 0)
            dots = dot(pick, high[...], 1, 1) + dot(pick, low[...], 1, 1)
            for half in range(TILE // rows):
                bufs["dots"]["part"][k, m * (TILE // rows) + half] = dots[
                    :8, half * rows : (half + 1) * rows
                ]
            bufs["back"]["part"][k, piece, :] = dot(gpre[tk, piece, :], up[...], 1, 0).astype(BF16)
            if forth:
                bufs["forth"]["part"][k, piece, :] = dot(
                    gated[tk, piece, :], down[...], 1, 0
                ).astype(BF16)
            return carry

        lax.fori_loop(0, group // TILE, tile, 0)

    bufs["back"]["sum"], bufs["forth"]["sum"], bufs["dots"]["sum"] = back_sum, forth_sum, dots_sum

    def part_of(name):
        part = bufs[name]["part"]
        if name == "dots":
            return lambda k, index: part.at[k, index]
        return lambda k, index: part.at[k, block(index), :]

    streams = {
        name: Scatter(spots, bufs[name], part_of(name), ssend.at[n], srecv.at[n])
        for n, name in enumerate(("back", "dots", "forth") if forth else ("back", "dots"))
    }

    def first(k, which):
        for name in which:
            streams[name].first(k)

    def second(k, which):
        for name in which:
            streams[name].second(k)

    def third(k, which):
        for name in which:
            streams[name].third(k)

    def last(which):
        for name in which:
            streams[name].last()

    early = ("dots", "back")
    gather[0, 2].wait_recv()
    gather[0, 3].start()
    gather[1, 0].wait_recv()
    gather[1, 2].start()
    gather[1, 1].start()
    gather[0, 1].wait_recv()
    gather[0, 3].wait_recv()
    compute(0)
    first(0, early)
    gather[1, 2].wait_recv()
    gather[1, 3].start()
    for k in (2, 3):
        gather[k, 0].wait_recv()
        gather[k, 2].start()
        gather[k, 1].start()
    second(0, early)
    gather[1, 1].wait_recv()
    gather[1, 3].wait_recv()
    compute(1)
    first(1, early)
    for k in (2, 3):
        gather[k, 2].wait_recv()
        gather[k, 3].start()
    third(0, early)
    second(1, early)
    gather[2, 1].wait_recv()
    gather[2, 3].wait_recv()
    compute(2)
    first(2, early)
    third(1, early)
    second(2, early)
    gather[3, 1].wait_recv()
    gather[3, 3].wait_recv()
    compute(3)
    first(3, early)
    third(2, early)
    second(3, early)
    late = ("forth",) if forth else ()
    for k in range(4):
        first(k, late)
    third(3, early)
    for k in (1, 2, 3, 0):
        second(k, late)
    last(early)
    for k in (1, 2, 3, 0):
        third(k, late)
    last(late)
    copies = list(gather.values())
    for stream in streams.values():
        copies += list(stream.copies.values())
    for copy in copies:
        copy.wait_send()


def scatter_scratch(spans, kind, shape, part):
    return {
        "part": pltpu.VMEM((spans,) + part, kind),
        "near": pltpu.VMEM((spans, 2) + shape, kind),
        "out": pltpu.VMEM((spans, 2) + shape, kind),
        "far": pltpu.VMEM((spans, 2) + shape, kind),
    }


def experts_call(forth, normed, grads, up, down, router, wide):
    rows, width = normed.shape
    spans, group, _ = grads.shape
    hidden = up.shape[0]
    vmem = pl.BlockSpec(memory_space=pltpu.VMEM)

    return pl.pallas_call(
        functools.partial(experts_kernel, forth),
        out_shape=(
            jax.ShapeDtypeStruct((rows, width), F32),
            jax.ShapeDtypeStruct((rows, width) if forth else (8, LANES), F32),
            jax.ShapeDtypeStruct((8, rows), F32),
            jax.ShapeDtypeStruct((spans, group, width), BF16),
            jax.ShapeDtypeStruct((spans, group, hidden), BF16),
            jax.ShapeDtypeStruct((spans, group, hidden), BF16),
        ),
        in_specs=[vmem] * 6,
        out_specs=[vmem] * 6,
        scratch_shapes=experts_scratch(forth, spans, rows, group, width, hidden),
        compiler_params=pltpu.CompilerParams(
            collective_id=0, has_side_effects=True, vmem_limit_bytes=56 * 1024 * 1024
        ),
    )(normed, grads, up, down, router, wide)


def front_kernel(
    scale,
    experts,
    tokens,
    packed,
    seg_down,
    seg_across,
    table,
    qkv_part,
    proj_part,
    up_part,
    down_part,
    small_part,
    wide,
    normed_group,
    qkv,
    probs,
    attended,
    middle,
    normed,
    qkv_full,
    proj_full,
    down_full,
    small_full,
    grads,
    gmiddle,
    gmid_low,
    fixed,
    nall,
    gpre,
    gated,
    back_sum,
    dots_sum,
    inputs,
    up_full,
    bias,
    mixed,
    xsend,
    xrecv,
    wsend,
    wrecv,
    csend,
    crecv,
    asend,
    arecv,
    forth_sum,
    *rest,
):
    spots = neighbours()
    f, i, t, sibling, across, along = spots
    peer, diagonal = (1 - f, i, t), (f, xor(i, 3), t)
    rows, width = tokens.shape
    group, own = inputs.shape[0], width // 2
    heads, hw = probs.shape[0], attended.shape[1]
    head, blocks = hw // heads, group // rows

    def block(index):
        return pl.ds(pl.multiple_of(index * rows, rows), rows)

    def half(index):
        return pl.ds(pl.multiple_of(index * own, LANES), own)

    ins = gather_copies(spots, tokens, lambda tt, ii: inputs.at[block(ii), :], xsend, xrecv, 1)
    cots = gather_copies(spots, packed, lambda tt, ii: grads.at[tt, block(ii), :], csend, crecv)

    def give(n, src, dst, target=peer):
        return remote(src, dst, wsend.at[n], wrecv.at[n], target)

    side = half(lax.rem(i, 2))
    other = proj_full.at[side, half(1 - f)]
    w_qkv = give(0, qkv_part, qkv_full.at[half(f), :])
    w_small = give(1, small_part, small_full.at[pl.ds(0, 16), half(f)])
    w_proj = give(2, proj_part.at[side, :], proj_full.at[side, half(f)])
    w_down = give(3, down_part, down_full.at[:, half(f)])
    w_up = give(4, up_part, up_full.at[:, half(f)])
    w_proj_on = give(5, other, other, sibling)
    swaps = [
        remote(attended.at[block(xor(i, j)), :], mixed.at[i], asend.at[j], arecv.at[j], target)
        for j, target in ((1, sibling), (2, across), (3, diagonal))
    ]

    small_full[...] = jnp.zeros_like(small_full)
    greet([sibling, across, diagonal, peer] + along[1:])
    ins[0, 2].start()
    ins[0, 1].start()
    w_small.start()
    w_qkv.start()
    for k in (1, 2, 3):
        cots[k, 0].start()
    w_proj.start()
    w_down.start()
    w_up.start()
    inputs[block(i), :] = tokens[...]
    grads[t, block(i), :] = packed[...]
    qkv_full[half(f), :] = qkv_part[...]
    small_full[pl.ds(0, 16), half(f)] = small_part[...]
    proj_full[:, half(f)] = proj_part[...]
    down_full[:, half(f)] = down_part[...]
    up_full[:, half(f)] = up_part[...]

    apart = lax.broadcasted_iota(jnp.int32, (rows, rows), 0) - lax.broadcasted_iota(
        jnp.int32, (rows, rows), 1
    )
    for h in range(heads):
        for n in range(2):
            value = jnp.full((rows, rows), table[i * heads + h, 0], F32)
            for number, bound in enumerate(BOUNDS, 1):
                value = jnp.where(apart + n * rows >= bound, table[i * heads + h, number], value)
            bias[n, h] = value

    ins[0, 2].wait_recv()
    ins[0, 3].start()
    cots[0, 2].start()
    cots[0, 1].start()
    w_small.wait_recv()
    ins[0, 1].wait_recv()
    ins[0, 3].wait_recv()

    def norm_tile(m, carry):
        at = pl.ds(pl.multiple_of(m * 64, 64), 64)
        value = inputs[at, :].astype(F32)
        gain = small_full[pl.ds(4, 1), :].astype(F32)
        normed_group[at, :] = (value * rms_scale(value) * gain).astype(BF16)
        return carry

    lax.fori_loop(0, group // 64, norm_tile, 0)
    w_qkv.wait_recv()
    for m in range(2):
        at = pl.ds(m * (group // 2), group // 2)
        qkv[at, :] = dot(normed_group[at, :], qkv_full[...], 1, 0).astype(BF16)

    def pass_on(k):
        cots[k, 0].wait_recv()
        cots[k, 2].start()
        cots[k, 1].start()

    def relay(k):
        cots[k, 2].wait_recv()
        cots[k, 3].start()

    pass_on(1)
    relay(0)
    for h in range(heads):
        cols = pl.ds(h * head, head)
        far = table[i * heads + h, BUCKETS - 1]
        for m in range(blocks):
            at, reach = pl.ds(m * rows, rows), (m + 1) * rows
            scores = dot(qkv[at, cols], qkv[pl.ds(0, reach), pl.ds(hw + h * head, head)], 1, 1)
            pieces = []
            for j in range(m + 1):
                allowed = seg_down[at, :] == seg_across[:, pl.ds(j * rows, rows)]
                if j == m:
                    allowed = allowed & (apart >= 0)
                add = bias[m - j, h] if m - j < 2 else far
                score = scores[:, j * rows : (j + 1) * rows] * scale + add
                pieces.append(jnp.where(allowed, score, MASK_FILL))
            scores = jnp.concatenate(pieces, axis=1)
            weights = jnp.exp(scores - jnp.max(scores, axis=1, keepdims=True))
            prob = weights / jnp.sum(weights, axis=1, keepdims=True)
            probs[h, at, pl.ds(0, reach)] = prob
            if reach < group:
                probs[h, at, pl.ds(reach, group - reach)] = jnp.zeros((rows, group - reach), F32)
            attended[at, cols] = dot(
                prob.astype(BF16), qkv[pl.ds(0, reach), pl.ds(2 * hw + h * head, head)], 1, 0
            ).astype(BF16)
        if h < 2:
            pass_on(2 + h)
            relay(1 + h)
    for swap in swaps:
        swap.start()
    mixed[i] = attended[block(i), :]
    w_proj.wait_recv()
    w_proj_on.start()
    relay(3)
    for swap in swaps:
        swap.wait_recv()
    w_proj_on.wait_recv()
    value = tokens[...].astype(F32)
    for j in range(blocks):
        value = value + dot(mixed[j], proj_full[pl.ds(j * hw, hw), :], 1, 0)
    middle[...] = value
    gain = small_full[pl.ds(5, 1), :].astype(F32)
    normed[...] = (value * rms_scale(value) * gain).astype(BF16)

    def ready(k):
        if k == 0:
            w_down.wait_recv()
            w_up.wait_recv()
        else:
            cots[k, 1].wait_recv()
            cots[k, 3].wait_recv()
        if k == 0:
            cots[0, 1].wait_recv()
            cots[0, 3].wait_recv()

    experts_kernel(
        False,
        normed,
        grads,
        up_full,
        down_full,
        small_full,
        wide,
        back_sum,
        forth_sum,
        dots_sum,
        nall,
        gpre,
        gated,
        *rest,
        ready=ready,
    )

    turned = jnp.transpose(
        jnp.concatenate([dots_sum[...], jnp.zeros((rows - 8, rows), F32)], axis=0)
    )
    chosen = packed[:, pl.ds(width, LANES)].astype(F32) > 0.5
    gates = gates_of(dot(normed[...], small_full[...], 1, 1), chosen)
    grad_logits = gates * (turned - jnp.sum(gates * turned, axis=1, keepdims=True))
    sums = [jnp.zeros((1, width), F32) for _ in range(experts + 1)]
    step = 32
    for m in range(rows // step):
        at = pl.ds(m * step, step)
        parts = [grad_logits[m * step : (m + 1) * step, e : e + 1] for e in range(experts)]
        grad = back_sum[at, :]
        seen = normed[at, :].astype(F32)
        for e in range(experts):
            grad = grad + parts[e] * small_full[pl.ds(e, 1), :].astype(F32)
            sums[e + 1] = sums[e + 1] + jnp.sum(parts[e] * seen, axis=0, keepdims=True)
        mid = middle[at, :]
        size = rms_scale(mid)
        weighted = grad * gain
        sums[0] = sums[0] + jnp.sum(grad * mid * size, axis=0, keepdims=True)
        value = (
            packed[at, pl.ds(0, width)].astype(F32)
            + size * weighted
            - mid * size**3 * jnp.mean(weighted * mid, axis=1, keepdims=True)
        )
        gmiddle[at, :] = value
        gmid_low[at, :] = value.astype(BF16)
    tiles = width // LANES
    fixed[...] = jnp.zeros_like(fixed)
    for n, total in enumerate(sums):
        for c in range(tiles):
            fixed[pl.ds((n + 1) * tiles + c, 1), :] = total[:, c * LANES : (c + 1) * LANES]
    copies = list(ins.values()) + list(cots.values()) + swaps
    copies += [w_qkv, w_small, w_proj, w_down, w_up, w_proj_on]
    for copy in copies:
        copy.wait_send()


def front_call(scale, experts, heads, hw, *operands):
    tokens, packed, seg_down = operands[:3]
    rows, width = tokens.shape
    group = seg_down.shape[0]
    spans, hidden = 4, operands[7].shape[0]
    vmem = pl.BlockSpec(memory_space=pltpu.VMEM)
    smem = pl.BlockSpec(memory_space=pltpu.SMEM)
    shape = jax.ShapeDtypeStruct
    dma = pltpu.SemaphoreType.DMA
    outs = (
        shape((group, width), BF16),
        shape((group, 3 * hw), BF16),
        shape((heads, group, group), F32),
        shape((group, hw), BF16),
        shape((rows, width), F32),
        shape((rows, width), BF16),
        shape((width, 3 * hw), BF16),
        shape((width, width), BF16),
        shape((hidden, width), BF16),
        shape((LANES, width), BF16),
        shape((spans, group, packed.shape[1]), BF16),
        shape((rows, width), F32),
        shape((rows, width), BF16),
        shape((8 * width // LANES, LANES), F32),
        shape((spans, group, width), BF16),
        shape((spans, group, hidden), BF16),
        shape((spans, group, hidden), BF16),
    )
    return pl.pallas_call(
        functools.partial(front_kernel, scale, experts),
        out_shape=outs,
        in_specs=[smem if n == 4 else vmem for n in range(len(operands))],
        out_specs=[vmem] * len(outs),
        scratch_shapes=[
            pltpu.VMEM((rows, width), F32),
            pltpu.VMEM((8, rows), F32),
            pltpu.VMEM((group, width), BF16),
            pltpu.VMEM((hidden, width), BF16),
            pltpu.VMEM((2, heads, rows, rows), F32),
            pltpu.VMEM((4, rows, hw), BF16),
            dma((1, 4)),
            dma((1, 4)),
            dma((6,)),
            dma((6,)),
            dma((4, 4)),
            dma((4, 4)),
            dma((4,)),
            dma((4,)),
            pltpu.VMEM((8, LANES), F32),
        ]
        + experts_scratch(False, spans, rows, group, width, hidden),
        compiler_params=pltpu.CompilerParams(
            collective_id=2, has_side_effects=True, vmem_limit_bytes=60 * 1024 * 1024
        ),
    )(*operands)


def experts_scratch(forth, spans, rows, group, width, hidden):
    streams = {
        "back": scatter_scratch(spans, BF16, (rows, width), (group, width)),
        "dots": scatter_scratch(spans, F32, (8, rows), (4, 8, rows)),
        "forth": (
            scatter_scratch(spans, BF16, (rows, width), (group, width))
            if forth
            else {"sum": pltpu.SMEM((1,), F32)}
        ),
    }
    return [
        pltpu.VMEM((TILE, hidden), F32),
        pltpu.VMEM((TILE, hidden), F32),
        pltpu.VMEM((TILE, hidden), F32),
        pltpu.VMEM((TILE, hidden), BF16),
        pltpu.VMEM((TILE, hidden), BF16),
        streams,
        pltpu.SemaphoreType.DMA((4, 4)),
        pltpu.SemaphoreType.DMA((4, 4)),
        pltpu.SemaphoreType.DMA((3, 4, 4)),
        pltpu.SemaphoreType.DMA((3, 4, 4)),
    ]


def tail_kernel(
    scale,
    gmid_own,
    probs,
    qkv,
    attended,
    normed,
    wqkv,
    wproj,
    gated,
    gpre,
    nall,
    grads,
    down,
    tokens,
    fixed,
    forth_sum,
    gone_sum,
    gup,
    gdown,
    gwq,
    gwp,
    small,
    wall,
    ptmp,
    vtmp,
    wtmp,
    buckets,
    gmid,
    gatt,
    gqkv,
    gscore,
    wide_up,
    wide_down,
    half_send,
    half_recv,
    wsend,
    wrecv,
    wsum,
    zsend,
    zrecv,
    smalls,
    forth_buf,
    gone_buf,
    msend,
    mrecv,
    fsend,
    frecv,
    osend,
    orecv,
    xsend,
    xrecv,
    wgsend,
    wgrecv,
):
    spots = neighbours()
    f, i, t, sibling, across, along = spots
    peer = (1 - f, i, t)
    rows, width = gmid_own.shape
    spans, group, _ = nall.shape
    heads, hw = probs.shape[0], attended.shape[1]
    head = hw // heads
    own = width // 2
    piece = own // spans
    blocks = group // rows

    def block(index):
        return pl.ds(pl.multiple_of(index * rows, rows), rows)

    def half(index):
        return pl.ds(pl.multiple_of(index * own, LANES), own)

    mids = gather_copies(spots, gmid_own, lambda tt, ii: gmid.at[block(ii), :], msend, mrecv, 1)
    forth_buf["sum"], gone_buf["sum"] = forth_sum, gone_sum
    forth = Scatter(
        spots, forth_buf, lambda k, index: forth_buf["part"].at[k, block(index), :], fsend, frecv
    )
    gone = Scatter(
        spots, gone_buf, lambda k, index: gone_buf["part"].at[k, block(index), :], osend, orecv
    )
    halves = [
        remote(half_send[n], half_recv[n], xsend.at[n], xrecv.at[n], peer) for n in range(2)
    ]
    wx = [
        remote(wsend.at[n], wrecv.at[n], xsend.at[2 + n], xrecv.at[2 + n], peer) for n in range(2)
    ]
    wz = [
        {
            k: remote(
                zsend.at[n, pl.ds(pl.multiple_of(xor(t, k) * piece, 16), piece), :],
                zrecv.at[n, k],
                xsend.at[4 + 3 * n + k - 1],
                xrecv.at[4 + 3 * n + k - 1],
                along[k],
            )
            for k in (1, 2, 3)
        }
        for n in range(2)
    ]
    wg = [
        gather_copies(
            spots,
            wall.at[n, t, i],
            lambda tt, ii, n=n: wall.at[n, tt, ii],
            wgsend.at[n],
            wgrecv.at[n],
        )
        for n in range(2)
    ]
    steps = [
        remote(smalls.at[n], smalls.at[3 + n], xsend.at[10 + n], xrecv.at[10 + n], target)
        for n, target in enumerate((sibling, across, peer))
    ]
    rounds = [
        remote(small, smalls.at[5 + k], xsend.at[12 + k], xrecv.at[12 + k], along[k])
        for k in (1, 2, 3)
    ]

    greet([sibling, across, peer] + along[1:])
    gmid[block(i), :] = gmid_own[...]
    mids[0, 2].start()
    mids[0, 1].start()
    apart = lax.broadcasted_iota(jnp.int32, (rows, rows), 0) - lax.broadcasted_iota(
        jnp.int32, (rows, rows), 1
    )
    for n in range(2):
        value = jnp.where(apart + n * rows >= 0, 0, -1)
        for bound in BOUNDS:
            value = value + jnp.where(apart + n * rows >= bound, 1, 0)
        buckets[n] = value

    def forth_part(k):
        tk = xor(t, k)

        def tile(m, carry):
            at = pl.ds(pl.multiple_of(m * TILE, TILE), TILE)
            forth_buf["part"][k, at, :] = dot(gated[tk, at, :], down[...], 1, 0).astype(BF16)
            return carry

        lax.fori_loop(0, group // TILE, tile, 0)
        forth.first(k)

    def up_half(which, out):
        out[...] = jnp.zeros_like(out)

        def step(c, carry):
            out[...] += dot(nall[c, :, half(which)], gpre[c], 0, 0)
            return carry

        lax.fori_loop(0, spans, step, 0)

    def down_half(which, out):
        out[...] = jnp.zeros_like(out)

        def step(c, carry):
            out[...] += dot(gated[c], grads[c, :, half(which)], 0, 0)
            return carry

        lax.fori_loop(0, spans, step, 0)

    forth_part(1)
    forth_part(2)
    mids[0, 2].wait_recv()
    mids[0, 3].start()
    down_half(1 - f, wide_down)
    half_send[0][...] = wide_down[...].astype(BF16)
    halves[0].start()
    forth.second(1)
    forth_part(3)
    forth_part(0)
    forth.second(2)
    mids[0, 1].wait_recv()
    mids[0, 3].wait_recv()

    here = wproj[pl.ds(pl.multiple_of(i * hw, 16), hw), :]
    gatt[...] = dot(gmid[...], here, 1, 1).astype(BF16)
    ptmp[...] = dot(attended[...], gmid[...], 0, 0)
    for h in range(heads):
        cols = pl.ds(h * head, head)
        gqkv[:, pl.ds(2 * hw + h * head, head)] = dot(
            probs[h].astype(BF16), gatt[:, cols], 0, 0
        ).astype(BF16)
    vtmp[...] = dot(normed[...], gqkv[:, pl.ds(2 * hw, hw)], 0, 0)
    low, part = piece // 2, hw // spans
    for side, out in ((1 - f, wsend), (f, wsum)):
        for n in range(spans):
            out[0, pl.ds(n * piece, part), :] = ptmp[pl.ds(n * part, part), half(side)].astype(
                out.dtype
            )
            for e in range(2):
                start = pl.multiple_of(side * own + n * piece + e * low, 16)
                out[0, pl.ds(n * piece + part, low), pl.ds(e * hw, hw)] = vtmp[
                    pl.ds(start, low), :
                ].astype(out.dtype)
    wx[0].start()
    forth.second(3)
    forth.second(0)
    forth.third(1)

    table = small.at[pl.ds(0, heads * BUCKETS), :]
    for h in range(heads):
        cols = pl.ds(h * head, head)
        keys = pl.ds(hw + h * head, head)

        def rowtile(m, carry, h=h, cols=cols, keys=keys):
            at = block(m)
            grad_probs = dot(gatt[at, cols], qkv[:, pl.ds(2 * hw + h * head, head)], 1, 1)
            prob = probs[h, at, :]
            inner = jnp.sum(prob * grad_probs, axis=1, keepdims=True)
            score = (prob * (grad_probs - inner)).astype(BF16)
            gscore[h, at, :] = score
            gqkv[at, cols] = (dot(score, qkv[:, keys], 1, 0) * scale).astype(BF16)
            return carry

        lax.fori_loop(0, blocks, rowtile, 0)
        gqkv[:, keys] = (dot(gscore[h], qkv[:, cols], 0, 0) * scale).astype(BF16)
        if h == 0:
            forth.third(2)
        if h == 1:
            forth.third(3)

    def gone_tile(m, carry):
        at = block(m)
        gone_buf["part"][0, at, :] = dot(gqkv[at, :], wqkv[...], 1, 1).astype(BF16)
        return carry

    lax.fori_loop(0, blocks, gone_tile, 0)
    gone.first(0)
    wtmp[...] = dot(normed[...], gqkv[:, pl.ds(0, 2 * hw)], 0, 0)
    wsend[1] = wtmp[half(1 - f), :].astype(BF16)
    wsum[1] = wtmp[half(f), :]
    wx[1].start()
    gone.second(0)
    up_half(1 - f, wide_up)
    half_send[1][...] = wide_up[...].astype(BF16)
    halves[1].start()

    def reduce_along(n):
        wx[n].wait_recv()
        total = wsum[n] + wrecv[n].astype(F32)
        wsum[n] = total
        zsend[n] = total.astype(BF16)
        for k in (1, 2, 3):
            wz[n][k].start()

    def share(n):
        total = wsum[n, pl.ds(pl.multiple_of(t * piece, 16), piece), :]
        for k in (1, 2, 3):
            wz[n][k].wait_recv()
            total = total + zrecv[n, k].astype(F32)
        wall[n, t, i] = total.astype(BF16)
        wg[n][0, 2].start()
        wg[n][0, 1].start()
        for k in (1, 2, 3):
            wg[n][k, 0].start()

    def onward(n):
        for k in (1, 2, 3):
            wg[n][k, 0].wait_recv()
            wg[n][k, 2].start()
            wg[n][k, 1].start()

    def relay(n):
        for k in range(4):
            wg[n][k, 2].wait_recv()
            wg[n][k, 3].start()

    reduce_along(0)
    forth.third(0)

    def bucket_sums(h):
        near = jnp.zeros((rows, rows), F32)
        after = jnp.zeros((rows, rows), F32)
        far = jnp.zeros((rows, rows), F32)
        for a in range(blocks):
            for b in range(a + 1):
                score = gscore[h, pl.ds(a * rows, rows), pl.ds(b * rows, rows)].astype(F32)
                if a == b:
                    near = near + score
                elif a == b + 1:
                    after = after + score
                else:
                    far = far + score
        sums = []
        for b in range(BUCKETS):
            value = jnp.where(buckets[0] == b, near, 0.0) + jnp.where(
                buckets[1] == b, after, 0.0
            )
            if b == BUCKETS - 1:
                value = value + far
            sums.append(jnp.sum(value, axis=0, keepdims=True))
        sums = jnp.sum(jnp.concatenate(sums, axis=0), axis=1, keepdims=True)
        lane = lax.broadcasted_iota(jnp.int32, (BUCKETS, LANES), 1)
        smalls[0, pl.ds(h * BUCKETS, BUCKETS), :] = jnp.where(lane == i, sums, 0.0)

    for h in range(heads):
        bucket_sums(h)
    gone.third(0)
    value = tokens[...].astype(F32)
    gain = jnp.sum(gone_sum[...] * (value * rms_scale(value)), axis=0, keepdims=True)
    base = heads * BUCKETS
    smalls[0, pl.ds(base, smalls.shape[1] - base), :] = fixed[...]
    for c in range(width // LANES):
        smalls[0, pl.ds(base + c, 1), :] = gain[:, c * LANES : (c + 1) * LANES]
    share(0)
    steps[0].start()
    down_half(f, gdown)
    reduce_along(1)
    up_half(f, wide_up)
    steps[0].wait_recv()
    smalls[1] = smalls[0] + smalls[3]
    steps[1].start()
    onward(0)
    share(1)
    steps[1].wait_recv()
    smalls[2] = smalls[1] + smalls[4]
    steps[2].start()
    relay(0)
    steps[2].wait_recv()
    small[...] = smalls[2] + smalls[5]
    for copy in rounds:
        copy.start()
    onward(1)
    forth.last()
    relay(1)
    for copy in rounds:
        copy.wait()
    small[...] = small[...] + smalls[6] + smalls[7] + smalls[8]
    halves[0].wait_recv()
    gdown[...] = gdown[...] + half_recv[0][...].astype(F32)
    halves[1].wait_recv()
    units = gup.shape[2]
    for e in range(gup.shape[0]):
        cols = pl.ds(e * units, units)
        gup[e] = wide_up[:, cols] + half_recv[1][:, cols].astype(F32)
    for n in range(2):
        for k in range(4):
            wg[n][k, 1].wait_recv()
            wg[n][k, 3].wait_recv()
    for n in range(spans):
        for c in range(blocks):
            gwp[pl.ds(c * hw + n * part, part), :] = wall[0, n, c, pl.ds(0, part), :]
            for e in range(2):
                gwq[pl.ds(n * piece + e * low, low), pl.ds(2 * width + c * hw, hw)] = wall[
                    0, n, c, pl.ds(part, low), pl.ds(e * hw, hw)
                ]
                gwq[pl.ds(n * piece, piece), pl.ds(e * width + c * hw, hw)] = wall[
                    1, n, c, :, pl.ds(e * hw, hw)
                ]
    copies = halves + wx + steps + list(mids.values())
    copies += list(forth.copies.values()) + list(gone.copies.values())
    for n in range(2):
        copies += list(wz[n].values()) + list(wg[n].values())
    for copy in copies:
        copy.wait_send()


def tail_call(scale, experts, *operands):
    gmid, probs, qkv, attended, normed, wqkv, wproj, gated, gpre, nall = operands[:10]
    rows, width = gmid.shape
    spans, group, hidden = gpre.shape
    heads = probs.shape[0]
    hw = attended.shape[1]
    own = width // 2
    piece = own // spans
    extra = 8 * width // LANES
    vmem = pl.BlockSpec(memory_space=pltpu.VMEM)
    shape = jax.ShapeDtypeStruct
    dma = pltpu.SemaphoreType.DMA
    table = heads * BUCKETS + extra
    return pl.pallas_call(
        functools.partial(tail_kernel, scale),
        out_shape=(
            shape((rows, width), F32),
            shape((rows, width), F32),
            shape((experts, own, hidden // experts), F32),
            shape((hidden, own), F32),
            shape((own, 3 * width), BF16),
            shape((width, own), BF16),
            shape((table, LANES), F32),
        ),
        in_specs=[vmem] * len(operands),
        out_specs=[vmem] * 7,
        scratch_shapes=[
            pltpu.VMEM((2, spans, 4, piece, 2 * hw), BF16),
            pltpu.VMEM((hw, width), F32),
            pltpu.VMEM((width, hw), F32),
            pltpu.VMEM((width, 2 * hw), F32),
            pltpu.VMEM((2, rows, rows), jnp.int32),
            pltpu.VMEM((group, width), BF16),
            pltpu.VMEM((group, hw), BF16),
            pltpu.VMEM((group, 3 * hw), BF16),
            pltpu.VMEM((heads, group, group), BF16),
            pltpu.VMEM((own, hidden), F32),
            pltpu.VMEM((hidden, own), F32),
            [pltpu.VMEM((hidden, own), BF16), pltpu.VMEM((own, hidden), BF16)],
            [pltpu.VMEM((hidden, own), BF16), pltpu.VMEM((own, hidden), BF16)],
            pltpu.VMEM((2, own, 2 * hw), BF16),
            pltpu.VMEM((2, own, 2 * hw), BF16),
            pltpu.VMEM((2, own, 2 * hw), F32),
            pltpu.VMEM((2, own, 2 * hw), BF16),
            pltpu.VMEM((2, 4, piece, 2 * hw), BF16),
            pltpu.VMEM((9, table, LANES), F32),
            scatter_scratch(spans, BF16, (rows, width), (group, width)),
            scatter_scratch(1, BF16, (rows, width), (group, width)),
            dma((1, 4)),
            dma((1, 4)),
            dma((spans, 4)),
            dma((spans, 4)),
            dma((1, 4)),
            dma((1, 4)),
            dma((16,)),
            dma((16,)),
            dma((2, 4, 4)),
            dma((2, 4, 4)),
        ],
        compiler_params=pltpu.CompilerParams(
            collective_id=1, has_side_effects=True, vmem_limit_bytes=58 * 1024 * 1024
        ),
    )(*operands)


def local(
    tokens,
    seg_ids,
    routes,
    norm_attn,
    weight_qkv,
    weight_proj,
    rel_table,
    norm_ffn,
    weight_router,
    expert_up,
    expert_down,
    cotangent,
):
    rows = tokens.shape[1]
    width = tokens.shape[2]
    heads = rel_table.shape[0]
    head_size = width // heads
    ctx_count = lax.axis_size("ctx")
    heads_here = heads // ctx_count
    hw = heads_here * head_size
    experts = expert_up.shape[0]
    units = expert_up.shape[2]
    length = seg_ids.shape[1]
    score_scale = head_size ** (-0.5)
    ctx_index = lax.axis_index("ctx")
    fsdp_index = lax.axis_index("fsdp")
    own_width = norm_attn.shape[0]
    world = ("ctx", "tp")

    tp_count = lax.axis_size("tp")
    pair = lax.axis_size("fsdp") == 2
    segment = seg_ids[0]
    inputs = tokens[0].astype(F32)
    scale_one = rms_scale(inputs)
    qkv_part = jnp.concatenate(
        [
            lax.dynamic_slice_in_dim(weight_qkv, s * width + ctx_index * hw, hw, 1)
            for s in range(3)
        ],
        axis=1,
    )
    expert_ids = jnp.arange(LANES, dtype=jnp.int32)[None, :]
    named = (routes[0][:, 0:1] == expert_ids) | (routes[0][:, 1:2] == expert_ids)
    packed_grad = jnp.concatenate([cotangent[0], named.astype(BF16)], axis=1)
    block = MAX_DISTANCE
    offset = (
        lax.broadcasted_iota(jnp.int32, (1, block, block), 1)
        - lax.broadcasted_iota(jnp.int32, (1, block, block), 2)
    )

    hidden = experts * units
    wide = (
        jnp.arange(hidden, dtype=jnp.int32)[None, :] // units
        == jnp.arange(3 * LANES, dtype=jnp.int32)[:, None] % LANES
    ).astype(BF16)
    if pair:
        up_part = jnp.swapaxes(expert_up, 1, 2).reshape(hidden, own_width)
        small_part = jnp.concatenate(
            [
                weight_router.T,
                norm_attn[None],
                norm_ffn[None],
                jnp.zeros((14 - experts, own_width), BF16),
            ],
            axis=0,
        )
        (
            normed_group,
            projected,
            probs,
            attended,
            middle,
            normed_two,
            qkv_here,
            proj_full,
            down,
            small,
            grads_all,
            grad_middle,
            grad_mid_low,
            fixed,
            normed_all,
            grad_pre,
            gated,
        ) = front_call(
            score_scale,
            experts,
            heads_here,
            hw,
            tokens[0],
            packed_grad,
            jnp.broadcast_to(segment[:, None], (length, LANES)),
            seg_ids,
            rel_table,
            qkv_part,
            weight_proj,
            up_part,
            expert_down.reshape(hidden, own_width),
            small_part,
            wide,
        )
        gain_one = small[experts].astype(F32)
    else:
        token_group = lax.all_gather(tokens[0], "ctx", axis=0, tiled=True)
        small = jnp.concatenate([norm_attn[None], norm_ffn[None], weight_router.T], axis=0)
        small = gather(small, "fsdp", 1)
        gain_one = small[0].astype(F32)
        gain_two = small[1].astype(F32)
        router_t = small[2:]
        qkv_here = gather(qkv_part, "fsdp", 0)
        proj_full = gather(weight_proj, "fsdp", 1)
        up_t = gather(
            jnp.swapaxes(expert_up, 1, 2).reshape(experts * units, own_width), "fsdp", 1
        )
        down = gather(expert_down.reshape(experts * units, own_width), "fsdp", 1)
        grad_routes = lax.all_gather(packed_grad, ("tp", "ctx"), axis=0, tiled=True)

        table_here = lax.dynamic_slice_in_dim(rel_table, ctx_index * heads_here, heads_here, 0)
        def bias_block(distance):
            value = jnp.broadcast_to(table_here[:, 0][:, None, None], (heads_here, block, block))
            for number, bound in enumerate(BOUNDS, 1):
                value = jnp.where(distance >= bound, table_here[:, number][:, None, None], value)
            return value

        near = bias_block(offset)
        next_near = bias_block(offset + block)
        far = jnp.broadcast_to(table_here[:, BUCKETS - 1][:, None, None], (heads_here, block, block))
        blocks = length // block
        picks = {0: near, 1: next_near}
        bias = jnp.concatenate(
            [
                jnp.concatenate(
                    [picks.get(i - j, far) for j in range(blocks)],
                    axis=2,
                )
                for i in range(blocks)
            ],
            axis=1,
        )
        positions = jnp.arange(length, dtype=jnp.int32)
        allowed = (segment[:, None] == segment[None, :]) & (positions[:, None] >= positions[None, :])
        bias = jnp.where(allowed[None], bias, MASK_FILL)

        inputs_group = token_group.astype(F32)
        normed_group = (inputs_group * rms_scale(inputs_group) * gain_one).astype(BF16)
        projected = dot(normed_group, qkv_here, 1, 0).astype(BF16)
        by_head = projected.reshape(length, 3, heads_here, head_size)
        query, key, value = by_head[:, 0], by_head[:, 1], by_head[:, 2]

        scores = (
            jnp.einsum("qhd,khd->hqk", query, key, preferred_element_type=F32) * score_scale + bias
        )
        peak = jnp.max(scores, axis=-1, keepdims=True)
        weights = jnp.exp(scores - peak)
        probs = weights / jnp.sum(weights, axis=-1, keepdims=True)
        low_probs = probs.astype(BF16)
        attended = (
            jnp.einsum("hqk,khd->qhd", low_probs, value, preferred_element_type=F32)
            .astype(BF16)
            .reshape(length, hw)
        )
        mixed = lax.all_to_all(attended, "ctx", split_axis=0, concat_axis=1, tiled=True)
        mixed, grad_routes, up_t, down = lax.optimization_barrier((mixed, grad_routes, up_t, down))
        middle = inputs + dot(mixed, proj_full, 1, 0)
        scale_two = rms_scale(middle)
        normed_two = (middle * scale_two * gain_two).astype(BF16)

        router_pad = jnp.pad(router_t, ((0, LANES - experts), (0, 0)))
        grad_normed_two, result, dots_own, normed_all, grad_pre, gated = experts_call(
            True,
            normed_two,
            grad_routes.reshape(tp_count, length, width + LANES),
            up_t,
            down,
            router_pad,
            wide,
        )
    if pair:
        result, grad_normed_one, grad_up, grad_down, grad_qkv, grad_proj, packed = tail_call(
            score_scale,
            experts,
            grad_mid_low,
            probs,
            projected,
            attended,
            normed_group,
            qkv_here,
            proj_full,
            gated,
            grad_pre,
            normed_all,
            grads_all,
            down,
            tokens[0],
            fixed,
        )
        output = (middle + result).astype(BF16)[None]
        weighted_one = grad_normed_one * gain_one
        grad_tokens = (
            grad_middle
            + scale_one * weighted_one
            - inputs * scale_one**3 * jnp.mean(weighted_one * inputs, axis=1, keepdims=True)
        )
        grad_down = grad_down.reshape(experts, units, own_width)
        edge = heads_here * BUCKETS
        table_grad = packed[:edge, :ctx_count].T.reshape(heads, BUCKETS)
        gains = packed[edge:].reshape(-1, width)
        gains = lax.dynamic_slice_in_dim(gains, fsdp_index * own_width, own_width, 1)
        return (
            output,
            grad_tokens[None],
            gains[0],
            grad_qkv.astype(F32),
            grad_proj.astype(F32),
            table_grad,
            gains[1],
            gains[2 : 2 + experts].T,
            grad_up,
            grad_down,
        )
    gate_dots = dots_own[:experts].T
    total_rows = tp_count * length
    grad_out = cotangent[0].astype(F32)
    number = jnp.arange(experts, dtype=jnp.int32)[None, :]
    chosen = (routes[0][:, 0:1] == number) | (routes[0][:, 1:2] == number)
    gates = gates_of(dot(normed_two, router_t, 1, 1), chosen)
    grad_logits = gates * (gate_dots - jnp.sum(gates * gate_dots, axis=1, keepdims=True))
    grad_normed_two = grad_normed_two + jnp.dot(
        grad_logits, router_t.astype(F32), precision=lax.Precision.HIGHEST
    )
    grad_router = lax.dot_general(
        grad_logits,
        normed_two.astype(F32),
        (((0,), (0,)), ((), ())),
        precision=lax.Precision.HIGHEST,
    )
    weighted_two = grad_normed_two * gain_two
    grad_gain_two = jnp.sum(grad_normed_two * middle * scale_two, axis=0)
    grad_middle = (
        grad_out
        + scale_two * weighted_two
        - middle * scale_two**3 * jnp.mean(weighted_two * middle, axis=1, keepdims=True)
    )
    normed_all = normed_all.reshape(total_rows, width)
    grad_pre = grad_pre.reshape(total_rows, hidden)
    gated = gated.reshape(total_rows, hidden)
    grad_all = grad_routes[:, :width]
    grad_up = exchange_sum(dot(grad_pre, normed_all, 0, 0), "fsdp", 1)
    grad_up = jnp.swapaxes(grad_up.reshape(experts, units, own_width), 1, 2)
    grad_down = exchange_sum(dot(gated, grad_all, 0, 0), "fsdp", 1)
    grad_down = grad_down.reshape(experts, units, own_width)

    grad_mid_group = lax.all_gather(grad_middle.astype(BF16), "ctx", axis=0, tiled=True)
    proj_rows = lax.dynamic_slice_in_dim(proj_full, ctx_index * hw, hw, 0)
    grad_attended = dot(grad_mid_group, proj_rows, 1, 1).astype(BF16)
    grad_heads = grad_attended.reshape(length, heads_here, head_size)
    grad_value = jnp.einsum("hqk,qhd->khd", low_probs, grad_heads, preferred_element_type=F32)
    grad_probs = jnp.einsum("qhd,khd->hqk", grad_heads, value, preferred_element_type=F32)
    grad_scores = (
        probs * (grad_probs - jnp.sum(probs * grad_probs, axis=-1, keepdims=True))
    ).astype(BF16)
    grad_query = (
        jnp.einsum("hqk,khd->qhd", grad_scores, key, preferred_element_type=F32) * score_scale
    )
    grad_key = (
        jnp.einsum("hqk,qhd->khd", grad_scores, query, preferred_element_type=F32) * score_scale
    )
    grad_qkv = jnp.concatenate(
        [
            grad_query.astype(BF16).reshape(length, hw),
            grad_key.astype(BF16).reshape(length, hw),
            grad_value.astype(BF16).reshape(length, hw),
        ],
        axis=1,
    )
    grad_normed_one = exchange_sum(dot(grad_qkv, qkv_here, 1, 1), "ctx", 0)

    weight_part = jnp.concatenate(
        [dot(normed_group, grad_qkv, 0, 0), dot(grad_mid_group, attended, 0, 0)], axis=1
    )
    weight_own = exchange_sum(weight_part, "fsdp", 0)
    grad_scores, weight_own = lax.optimization_barrier((grad_scores, weight_own))
    weight_own = exchange_sum(weight_own, "tp", 0).astype(BF16)
    def score_block(i, j):
        return grad_scores[
            :, i * block : (i + 1) * block, j * block : (j + 1) * block
        ].astype(F32)

    near_sum = sum(score_block(i, i) for i in range(blocks))
    next_sum = sum(score_block(i + 1, i) for i in range(blocks - 1))
    far_sum = sum(
        jnp.sum(score_block(i, j), axis=(1, 2)) for i in range(blocks) for j in range(i - 1)
    )
    lows = [0] + BOUNDS
    highs = BOUNDS + [2 * block]
    bucket_sums = [
        jnp.sum(jnp.where((offset >= lo) & (offset < hi), near_sum, 0.0), axis=(1, 2))
        + jnp.sum(
            jnp.where((offset + block >= lo) & (offset + block < hi), next_sum, 0.0), axis=(1, 2)
        )
        for lo, hi in zip(lows, highs)
    ]
    bucket_sums[-1] = bucket_sums[-1] + far_sum
    table_here_grad = jnp.stack(bucket_sums, axis=1)
    table_term = lax.dynamic_update_slice_in_dim(
        jnp.zeros((heads, BUCKETS), F32), table_here_grad, ctx_index * heads_here, 0
    )

    weighted_one = grad_normed_one * gain_one
    grad_gain_one = jnp.sum(grad_normed_one * inputs * scale_one, axis=0)
    grad_tokens = (
        grad_middle
        + scale_one * weighted_one
        - inputs * scale_one**3 * jnp.mean(weighted_one * inputs, axis=1, keepdims=True)
    )
    packed = jnp.concatenate(
        [
            grad_gain_one,
            grad_gain_two,
            grad_router.reshape(-1),
            table_term.reshape(-1),
        ]
    ).reshape(-1, 128)
    packed, weight_own = lax.optimization_barrier((packed, weight_own))
    packed = lax.psum(packed, ("fsdp", "ctx", "tp")).reshape(-1)
    packed, result = lax.optimization_barrier((packed, result))
    output = (middle + result).astype(BF16)[None]
    weight_all = lax.all_gather(weight_own, world, axis=0, tiled=True).astype(F32)
    weight_all = weight_all.reshape(ctx_count, own_width, 4 * hw)
    grad_weight_qkv = jnp.concatenate(
        [
            weight_all[c, :, s * hw : (s + 1) * hw]
            for s in range(3)
            for c in range(ctx_count)
        ],
        axis=1,
    )
    grad_weight_proj = jnp.swapaxes(weight_all[:, :, 3 * hw :], 1, 2).reshape(width, own_width)
    gains = packed[: (2 + experts) * width].reshape(2 + experts, width)
    gains = lax.dynamic_slice_in_dim(gains, fsdp_index * own_width, own_width, 1)
    table_grad = packed[(2 + experts) * width :].reshape(heads, BUCKETS)
    return (
        output,
        grad_tokens[None],
        gains[0],
        grad_weight_qkv,
        grad_weight_proj,
        table_grad,
        gains[1],
        gains[2:].T,
        grad_up,
        grad_down,
    )


def solution(mesh):
    rows = P(("fsdp", "tp"), "ctx", None)
    in_specs = (
        rows,
        P(("fsdp", "tp"), None),
        rows,
        P("fsdp"),
        P("fsdp", None),
        P(None, "fsdp"),
        P(),
        P("fsdp"),
        P("fsdp", None),
        P(None, "fsdp", ("ctx", "tp")),
        P(None, ("ctx", "tp"), "fsdp"),
        rows,
    )
    out_specs = (
        rows,
        rows,
        P("fsdp"),
        P("fsdp", None),
        P(None, "fsdp"),
        P(),
        P("fsdp"),
        P("fsdp", None),
        P(None, "fsdp", ("ctx", "tp")),
        P(None, ("ctx", "tp"), "fsdp"),
    )
    return jax.shard_map(local, mesh=mesh, in_specs=in_specs, out_specs=out_specs, check_vma=False)
```

```python
import functools

import jax
import jax.numpy as jnp
import numpy as np
from jax import lax
from jax.experimental import pallas as pl
from jax.experimental.pallas import tpu as pltpu
from jax.sharding import PartitionSpec as P

BUCKETS = 32
MAX_DISTANCE = 128
EPSILON = 1e-06
MASK_FILL = -1e30
F32 = jnp.float32
BF16 = jnp.bfloat16


def bucket_bounds(buckets, far_reach):
    exact_count = buckets // 2
    bounds = []
    for number in range(1, buckets):
        if number <= exact_count:
            bounds.append(number)
        else:
            exponent = (number - exact_count) / (buckets - exact_count)
            bounds.append(int(np.ceil(exact_count * (far_reach / exact_count) ** exponent)))
    return bounds


BOUNDS = bucket_bounds(BUCKETS, MAX_DISTANCE)


def rms_scale(values):
    return lax.rsqrt(jnp.mean(values * values, axis=-1, keepdims=True) + EPSILON)


def dot(a, b, ca, cb):
    return lax.dot_general(a, b, (((ca,), (cb,)), ((), ())), preferred_element_type=F32)


def gather(shard, axis, dim):
    count = lax.axis_size(axis)
    size = shard.shape[dim]
    me = lax.axis_index(axis)
    pieces = [shard] + [
        lax.ppermute(shard, axis, [(i, (i + step) % count) for i in range(count)])
        for step in range(1, count)
    ]
    if count == 2:
        first = me == 0
        return jnp.concatenate(
            [jnp.where(first, pieces[0], pieces[1]), jnp.where(first, pieces[1], pieces[0])],
            axis=dim,
        )
    shape = list(shard.shape)
    shape[dim] = count * size
    whole = jnp.zeros(shape, shard.dtype)
    for step, piece in enumerate(pieces):
        source = lax.rem(me + count - step, count)
        whole = lax.dynamic_update_slice_in_dim(whole, piece, source * size, dim)
    return whole


def exchange_sum(part, axis, dim, kind=BF16):
    count = lax.axis_size(axis)
    size = part.shape[dim] // count
    me = lax.axis_index(axis)
    total = lax.dynamic_slice_in_dim(part, me * size, size, dim).astype(F32)
    for step in range(1, count):
        target = lax.rem(me + step, count)
        piece = lax.dynamic_slice_in_dim(part, target * size, size, dim).astype(kind)
        total = total + lax.ppermute(
            piece, axis, [(i, (i + step) % count) for i in range(count)]
        ).astype(F32)
    return total


MESH = pl.DeviceIdType.MESH
TILE = 256
SLAB = 32
LANES = 128


def flip(value, bit):
    return value + bit - 2 * bit * lax.rem(lax.div(value, bit), 2)


def xor(value, mask):
    for bit in (1, 2):
        if mask & bit:
            value = flip(value, bit)
    return value


def place():
    return lax.axis_index("fsdp"), lax.axis_index("ctx"), lax.axis_index("tp")


def remote(src, dst, send, recv, target):
    return pltpu.make_async_remote_copy(
        src_ref=src,
        dst_ref=dst,
        send_sem=send,
        recv_sem=recv,
        device_id=target,
        device_id_type=MESH,
    )


def greet(targets):
    barrier = pltpu.get_barrier_semaphore()
    for target in targets:
        pl.semaphore_signal(barrier, inc=1, device_id=target, device_id_type=MESH)
    pl.semaphore_wait(barrier, len(targets))


def tanh_gelu(u):
    first = 0.7978845608028654
    cubic = 0.044715 * first
    square = u * u
    wave = jnp.tanh(u * (first + cubic * square))
    half = 0.5 + 0.5 * wave
    slope = half + (0.5 * u) * (1.0 - wave * wave) * (first + 3.0 * cubic * square)
    return u * half, slope


def gather_copies(spots, source, slot, send, recv, spans=4):
    f, i, t, sibling, across, along = spots

    def one(k, j):
        ends = send.at[k, j], recv.at[k, j]
        if j == 0:
            return remote(source, slot(t, i), *ends, along[k])
        here = slot(xor(t, k), i if j < 3 else flip(i, 2))
        origin = source if (k == 0 and j < 3) else here
        return remote(origin, here, *ends, across if j == 2 else sibling)

    return {(k, j): one(k, j) for k in range(spans) for j in range(4) if (k, j) != (0, 0)}


def neighbours():
    f, i, t = place()
    along = [None] + [(f, i, xor(t, k)) for k in (1, 2, 3)]
    return f, i, t, (f, flip(i, 1), t), (f, flip(i, 2), t), along


class Scatter:
    def __init__(self, spots, buf, part, send, recv):
        f, self.i, t, sibling, across, along = spots
        self.buf, self.part = buf, part
        self.copies = {}
        for k in range(buf["near"].shape[0]):
            for stage in range(4 if k else 3):
                ends = send.at[k, stage], recv.at[k, stage]
                if stage < 2:
                    src = part(k, xor(self.i, 1 if stage == 0 else 3))
                    copy = remote(src, buf["near"].at[k, stage], *ends, sibling)
                elif stage == 2:
                    copy = remote(buf["out"].at[k, 0], buf["far"].at[k, 0], *ends, across)
                else:
                    copy = remote(buf["out"].at[k, 1], buf["far"].at[k, 1], *ends, along[k])
                self.copies[k, stage] = copy

    def first(self, k):
        self.copies[k, 1].start()
        self.copies[k, 0].start()

    def second(self, k):
        b = self.buf
        self.copies[k, 1].wait_recv()
        total = self.part(k, flip(self.i, 2))[...].astype(F32) + b["near"][k, 1].astype(F32)
        b["out"][k, 0] = total.astype(b["out"].dtype)
        self.copies[k, 2].start()

    def third(self, k):
        b = self.buf
        self.copies[k, 0].wait_recv()
        self.copies[k, 2].wait_recv()
        total = (
            self.part(k, self.i)[...].astype(F32)
            + b["near"][k, 0].astype(F32)
            + b["far"][k, 0].astype(F32)
        )
        if k == 0:
            b["sum"][...] = total
        else:
            b["out"][k, 1] = total.astype(b["out"].dtype)
            self.copies[k, 3].start()

    def last(self):
        b = self.buf
        for k in (1, 2, 3):
            self.copies[k, 3].wait_recv()
            b["sum"][...] = b["sum"][...] + b["far"][k, 1].astype(F32)


def gates_of(logits, chosen):
    masked = jnp.where(chosen, logits, MASK_FILL)
    raw = jnp.where(chosen, jnp.exp(masked - jnp.max(masked, axis=1, keepdims=True)), 0.0)
    return raw / jnp.sum(raw, axis=1, keepdims=True)


def experts_kernel(
    forth,
    normed,
    grads,
    up,
    down,
    router,
    wide,
    back_sum,
    forth_sum,
    dots_sum,
    nall,
    gpre,
    gated,
    pre,
    reach,
    gate,
    high,
    low,
    bufs,
    gsend,
    grecv,
    ssend,
    srecv,
    ready=None,
):
    spots = neighbours()
    f, i, t, sibling, across, along = spots
    rows, width = normed.shape
    group = nall.shape[1]

    def block(index):
        return pl.ds(pl.multiple_of(index * rows, rows), rows)

    if ready is None:
        greet([sibling, across] + along[1:])
    gather = gather_copies(
        spots, normed, lambda tt, ii: nall.at[tt, block(ii), :], gsend, grecv
    )
    nall[t, block(i), :] = normed[...]
    gather[0, 2].start()
    gather[0, 1].start()
    gather[1, 0].start()
    gather[2, 0].start()

    pick = wide[pl.ds(0, SLAB), :]

    def compute(k):
        tk = xor(t, k)
        if ready is not None:
            ready(k)

        def tile(m, carry):
            base = pl.multiple_of(m * TILE, TILE)
            piece = pl.ds(base, TILE)
            pre[...] = dot(nall[tk, piece, :], up[...], 1, 1)
            logits = dot(nall[tk, piece, :], router[...], 1, 1)
            reach[...] = dot(grads[tk, piece, pl.ds(0, width)], down[...], 1, 1)
            chosen = grads[tk, piece, pl.ds(width, LANES)].astype(F32) > 0.5
            gates = gates_of(logits, chosen)
            terms = []
            for _ in range(3):
                terms.append(gates.astype(BF16))
                gates = gates - terms[-1].astype(F32)
            gate[...] = dot(jnp.concatenate(terms, axis=1), wide[...], 1, 0)

            def slab(s, inner):
                at = pl.ds(pl.multiple_of(s * SLAB, SLAB), SLAB)
                to = pl.ds(pl.multiple_of(base + s * SLAB, SLAB), SLAB)
                for c in range(pre.shape[1] // LANES):
                    cols = pl.ds(c * LANES, LANES)
                    share = gate[at, cols]
                    act, slope = tanh_gelu(pre[at, cols])
                    act = act.astype(BF16).astype(F32)
                    pull = reach[at, cols]
                    gated[tk, to, cols] = (act * share).astype(BF16)
                    gpre[tk, to, cols] = (pull * share * slope).astype(BF16)
                    product = act * pull
                    coarse = product.astype(BF16)
                    high[at, cols] = coarse
                    low[at, cols] = (product - coarse.astype(F32)).astype(BF16)
                return inner

            lax.fori_loop(0, TILE // SLAB, slab, 0)
            dots = dot(pick, high[...], 1, 1) + dot(pick, low[...], 1, 1)
            for half in range(TILE // rows):
                bufs["dots"]["part"][k, m * (TILE // rows) + half] = dots[
                    :8, half * rows : (half + 1) * rows
                ]
            bufs["back"]["part"][k, piece, :] = dot(gpre[tk, piece, :], up[...], 1, 0).astype(BF16)
            if forth:
                bufs["forth"]["part"][k, piece, :] = dot(
                    gated[tk, piece, :], down[...], 1, 0
                ).astype(BF16)
            return carry

        lax.fori_loop(0, group // TILE, tile, 0)

    bufs["back"]["sum"], bufs["forth"]["sum"], bufs["dots"]["sum"] = back_sum, forth_sum, dots_sum

    def part_of(name):
        part = bufs[name]["part"]
        if name == "dots":
            return lambda k, index: part.at[k, index]
        return lambda k, index: part.at[k, block(index), :]

    streams = {
        name: Scatter(spots, bufs[name], part_of(name), ssend.at[n], srecv.at[n])
        for n, name in enumerate(("back", "dots", "forth") if forth else ("back", "dots"))
    }

    def first(k, which):
        for name in which:
            streams[name].first(k)

    def second(k, which):
        for name in which:
            streams[name].second(k)

    def third(k, which):
        for name in which:
            streams[name].third(k)

    def last(which):
        for name in which:
            streams[name].last()

    early = ("dots", "back")
    gather[0, 2].wait_recv()
    gather[0, 3].start()
    gather[1, 0].wait_recv()
    gather[3, 0].start()
    gather[1, 2].start()
    gather[1, 1].start()
    gather[0, 1].wait_recv()
    gather[0, 3].wait_recv()
    compute(0)
    first(0, early)
    gather[1, 2].wait_recv()
    gather[1, 3].start()
    for k in (2, 3):
        gather[k, 0].wait_recv()
        gather[k, 2].start()
        gather[k, 1].start()
    second(0, early)
    gather[1, 1].wait_recv()
    gather[1, 3].wait_recv()
    compute(1)
    first(1, early)
    for k in (2, 3):
        gather[k, 2].wait_recv()
        gather[k, 3].start()
    third(0, early)
    second(1, early)
    gather[2, 1].wait_recv()
    gather[2, 3].wait_recv()
    compute(2)
    first(2, early)
    third(1, early)
    second(2, early)
    gather[3, 1].wait_recv()
    gather[3, 3].wait_recv()
    compute(3)
    first(3, early)
    third(2, early)
    second(3, early)
    late = ("forth",) if forth else ()
    for k in range(4):
        first(k, late)
    third(3, early)
    for k in (1, 2, 3, 0):
        second(k, late)
    last(early)
    for k in (1, 2, 3, 0):
        third(k, late)
    last(late)
    copies = list(gather.values())
    for stream in streams.values():
        copies += list(stream.copies.values())
    for copy in copies:
        copy.wait_send()


def scatter_scratch(spans, kind, shape, part):
    return {
        "part": pltpu.VMEM((spans,) + part, kind),
        "near": pltpu.VMEM((spans, 2) + shape, kind),
        "out": pltpu.VMEM((spans, 2) + shape, kind),
        "far": pltpu.VMEM((spans, 2) + shape, kind),
    }


def experts_call(forth, normed, grads, up, down, router, wide):
    rows, width = normed.shape
    spans, group, _ = grads.shape
    hidden = up.shape[0]
    vmem = pl.BlockSpec(memory_space=pltpu.VMEM)

    return pl.pallas_call(
        functools.partial(experts_kernel, forth),
        out_shape=(
            jax.ShapeDtypeStruct((rows, width), F32),
            jax.ShapeDtypeStruct((rows, width) if forth else (8, LANES), F32),
            jax.ShapeDtypeStruct((8, rows), F32),
            jax.ShapeDtypeStruct((spans, group, width), BF16),
            jax.ShapeDtypeStruct((spans, group, hidden), BF16),
            jax.ShapeDtypeStruct((spans, group, hidden), BF16),
        ),
        in_specs=[vmem] * 6,
        out_specs=[vmem] * 6,
        scratch_shapes=experts_scratch(forth, spans, rows, group, width, hidden),
        compiler_params=pltpu.CompilerParams(
            collective_id=0, has_side_effects=True, vmem_limit_bytes=56 * 1024 * 1024
        ),
    )(normed, grads, up, down, router, wide)


def front_kernel(
    scale,
    experts,
    tokens,
    cotangent,
    routes,
    seg_across,
    table,
    qkv_part,
    proj_part,
    up_part,
    down_part,
    small_part,
    normed_group,
    qkv,
    probs,
    attended,
    middle,
    normed,
    qkv_full,
    proj_full,
    down_full,
    small_full,
    grads,
    gmiddle,
    gmid_low,
    fixed,
    nall,
    gpre,
    gated,
    back_sum,
    dots_sum,
    inputs,
    up_full,
    bias,
    mixed,
    packed,
    seg_down,
    wide,
    xsend,
    xrecv,
    wsend,
    wrecv,
    csend,
    crecv,
    asend,
    arecv,
    forth_sum,
    *rest,
):
    spots = neighbours()
    f, i, t, sibling, across, along = spots
    peer, diagonal = (1 - f, i, t), (f, xor(i, 3), t)
    rows, width = tokens.shape
    group, own = inputs.shape[0], width // 2
    heads, hw = probs.shape[0], attended.shape[1]
    head, blocks = hw // heads, group // rows

    def block(index):
        return pl.ds(pl.multiple_of(index * rows, rows), rows)

    def half(index):
        return pl.ds(pl.multiple_of(index * own, LANES), own)

    ins = gather_copies(spots, tokens, lambda tt, ii: inputs.at[block(ii), :], xsend, xrecv, 1)
    cots = gather_copies(spots, packed, lambda tt, ii: grads.at[tt, block(ii), :], csend, crecv)

    def give(n, src, dst, target=peer):
        return remote(src, dst, wsend.at[n], wrecv.at[n], target)

    side = half(lax.rem(i, 2))
    other = proj_full.at[side, half(1 - f)]
    w_qkv = give(0, qkv_part, qkv_full.at[half(f), :])
    w_small = give(1, small_part, small_full.at[pl.ds(0, 16), half(f)])
    w_proj = give(2, proj_part.at[side, :], proj_full.at[side, half(f)])
    w_down = give(3, down_part, down_full.at[:, half(f)])
    w_up = give(4, up_part, up_full.at[:, half(f)])
    w_proj_on = give(5, other, other, sibling)
    swaps = [
        remote(attended.at[block(xor(i, j)), :], mixed.at[i], asend.at[j], arecv.at[j], target)
        for j, target in ((1, sibling), (2, across), (3, diagonal))
    ]

    small_full[...] = jnp.zeros_like(small_full)
    lane = lax.broadcasted_iota(jnp.int32, (rows, LANES), 1)
    named = (lane == routes[:, 0:1]) | (lane == routes[:, 1:2])
    packed[:, pl.ds(0, width)] = cotangent[...]
    packed[:, pl.ds(width, LANES)] = jnp.where(named, 1.0, 0.0).astype(BF16)
    greet([sibling, across, diagonal, peer] + along[1:])
    ins[0, 2].start()
    ins[0, 1].start()
    w_small.start()
    w_qkv.start()
    for k in (1, 2, 3):
        cots[k, 0].start()
    inputs[block(i), :] = tokens[...]
    grads[t, block(i), :] = packed[...]
    qkv_full[half(f), :] = qkv_part[...]
    small_full[pl.ds(0, 16), half(f)] = small_part[...]
    proj_full[:, half(f)] = proj_part[...]
    down_full[:, half(f)] = down_part[...]
    up_full[:, half(f)] = up_part[...]

    for m in range(blocks):
        seg = jnp.broadcast_to(seg_across[:, pl.ds(m * rows, rows)], (rows, rows))
        seg_down[pl.ds(m * rows, rows), :] = jnp.transpose(seg)
    units = wide.shape[1] // experts
    expert = lax.broadcasted_iota(jnp.int32, (LANES, wide.shape[1]), 0)
    unit = lax.broadcasted_iota(jnp.int32, (LANES, wide.shape[1]), 1)
    here = (unit >= expert * units) & (unit < (expert + 1) * units)
    spread = jnp.where(here, 1.0, 0.0).astype(BF16)
    for n in range(3):
        wide[pl.ds(n * LANES, LANES), :] = spread
    apart = lax.broadcasted_iota(jnp.int32, (rows, rows), 0) - lax.broadcasted_iota(
        jnp.int32, (rows, rows), 1
    )
    for h in range(heads):
        for n in range(2):
            value = jnp.full((rows, rows), table[i * heads + h, 0], F32)
            for number, bound in enumerate(BOUNDS, 1):
                value = jnp.where(apart + n * rows >= bound, table[i * heads + h, number], value)
            bias[n, h] = value

    ins[0, 2].wait_recv()
    ins[0, 3].start()
    cots[0, 2].start()
    cots[0, 1].start()
    w_small.wait_recv()
    ins[0, 1].wait_recv()
    ins[0, 3].wait_recv()

    def norm_tile(m, carry):
        at = pl.ds(pl.multiple_of(m * 64, 64), 64)
        value = inputs[at, :].astype(F32)
        gain = small_full[pl.ds(4, 1), :].astype(F32)
        normed_group[at, :] = (value * rms_scale(value) * gain).astype(BF16)
        return carry

    lax.fori_loop(0, group // 64, norm_tile, 0)
    w_qkv.wait_recv()
    w_proj.start()
    w_down.start()
    for m in range(2):
        at = pl.ds(m * (group // 2), group // 2)
        qkv[at, :] = dot(normed_group[at, :], qkv_full[...], 1, 0).astype(BF16)

    def pass_on(k):
        cots[k, 0].wait_recv()
        cots[k, 2].start()
        cots[k, 1].start()

    def relay(k):
        cots[k, 2].wait_recv()
        cots[k, 3].start()

    pass_on(1)
    relay(0)
    for h in range(heads):
        cols = pl.ds(h * head, head)
        far = table[i * heads + h, BUCKETS - 1]
        for m in range(blocks):
            at, reach = pl.ds(m * rows, rows), (m + 1) * rows
            scores = dot(qkv[at, cols], qkv[pl.ds(0, reach), pl.ds(hw + h * head, head)], 1, 1)
            pieces = []
            for j in range(m + 1):
                allowed = seg_down[at, :] == seg_across[:, pl.ds(j * rows, rows)]
                if j == m:
                    allowed = allowed & (apart >= 0)
                add = bias[m - j, h] if m - j < 2 else far
                score = scores[:, j * rows : (j + 1) * rows] * scale + add
                pieces.append(jnp.where(allowed, score, MASK_FILL))
            scores = jnp.concatenate(pieces, axis=1)
            weights = jnp.exp(scores - jnp.max(scores, axis=1, keepdims=True))
            prob = weights / jnp.sum(weights, axis=1, keepdims=True)
            probs[h, at, pl.ds(0, reach)] = prob
            if reach < group:
                probs[h, at, pl.ds(reach, group - reach)] = jnp.zeros((rows, group - reach), F32)
            attended[at, cols] = dot(
                prob.astype(BF16), qkv[pl.ds(0, reach), pl.ds(2 * hw + h * head, head)], 1, 0
            ).astype(BF16)
        if h == 0:
            w_up.start()
        if h < 2:
            pass_on(2 + h)
            relay(1 + h)
    for swap in swaps:
        swap.start()
    mixed[i] = attended[block(i), :]
    w_proj.wait_recv()
    w_proj_on.start()
    relay(3)
    for swap in swaps:
        swap.wait_recv()
    w_proj_on.wait_recv()
    value = tokens[...].astype(F32)
    for j in range(blocks):
        value = value + dot(mixed[j], proj_full[pl.ds(j * hw, hw), :], 1, 0)
    middle[...] = value
    gain = small_full[pl.ds(5, 1), :].astype(F32)
    normed[...] = (value * rms_scale(value) * gain).astype(BF16)

    def ready(k):
        if k == 0:
            w_down.wait_recv()
            w_up.wait_recv()
        else:
            cots[k, 1].wait_recv()
            cots[k, 3].wait_recv()
        if k == 0:
            cots[0, 1].wait_recv()
            cots[0, 3].wait_recv()

    experts_kernel(
        False,
        normed,
        grads,
        up_full,
        down_full,
        small_full,
        wide,
        back_sum,
        forth_sum,
        dots_sum,
        nall,
        gpre,
        gated,
        *rest,
        ready=ready,
    )

    turned = jnp.transpose(
        jnp.concatenate([dots_sum[...], jnp.zeros((rows - 8, rows), F32)], axis=0)
    )
    chosen = packed[:, pl.ds(width, LANES)].astype(F32) > 0.5
    gates = gates_of(dot(normed[...], small_full[...], 1, 1), chosen)
    grad_logits = gates * (turned - jnp.sum(gates * turned, axis=1, keepdims=True))
    sums = [jnp.zeros((1, width), F32) for _ in range(experts + 1)]
    step = 32
    for m in range(rows // step):
        at = pl.ds(m * step, step)
        parts = [grad_logits[m * step : (m + 1) * step, e : e + 1] for e in range(experts)]
        grad = back_sum[at, :]
        seen = normed[at, :].astype(F32)
        for e in range(experts):
            grad = grad + parts[e] * small_full[pl.ds(e, 1), :].astype(F32)
            sums[e + 1] = sums[e + 1] + jnp.sum(parts[e] * seen, axis=0, keepdims=True)
        mid = middle[at, :]
        size = rms_scale(mid)
        weighted = grad * gain
        sums[0] = sums[0] + jnp.sum(grad * mid * size, axis=0, keepdims=True)
        value = (
            packed[at, pl.ds(0, width)].astype(F32)
            + size * weighted
            - mid * size**3 * jnp.mean(weighted * mid, axis=1, keepdims=True)
        )
        gmiddle[at, :] = value
        gmid_low[at, :] = value.astype(BF16)
    tiles = width // LANES
    fixed[...] = jnp.zeros_like(fixed)
    for n, total in enumerate(sums):
        for c in range(tiles):
            fixed[pl.ds((n + 1) * tiles + c, 1), :] = total[:, c * LANES : (c + 1) * LANES]
    copies = list(ins.values()) + list(cots.values()) + swaps
    copies += [w_qkv, w_small, w_proj, w_down, w_up, w_proj_on]
    for copy in copies:
        copy.wait_send()


def front_call(scale, experts, heads, hw, *operands):
    tokens, seg_across = operands[0], operands[3]
    rows, width = tokens.shape
    group = seg_across.shape[1]
    spans, hidden = 4, operands[7].shape[0]
    vmem = pl.BlockSpec(memory_space=pltpu.VMEM)
    smem = pl.BlockSpec(memory_space=pltpu.SMEM)
    shape = jax.ShapeDtypeStruct
    dma = pltpu.SemaphoreType.DMA
    outs = (
        shape((group, width), BF16),
        shape((group, 3 * hw), BF16),
        shape((heads, group, group), F32),
        shape((group, hw), BF16),
        shape((rows, width), F32),
        shape((rows, width), BF16),
        shape((width, 3 * hw), BF16),
        shape((width, width), BF16),
        shape((hidden, width), BF16),
        shape((LANES, width), BF16),
        shape((spans, group, width + LANES), BF16),
        shape((rows, width), F32),
        shape((rows, width), BF16),
        shape((8 * width // LANES, LANES), F32),
        shape((spans, group, width), BF16),
        shape((spans, group, hidden), BF16),
        shape((spans, group, hidden), BF16),
    )
    return pl.pallas_call(
        functools.partial(front_kernel, scale, experts),
        out_shape=outs,
        in_specs=[smem if n == 4 else vmem for n in range(len(operands))],
        out_specs=[vmem] * len(outs),
        scratch_shapes=[
            pltpu.VMEM((rows, width), F32),
            pltpu.VMEM((8, rows), F32),
            pltpu.VMEM((group, width), BF16),
            pltpu.VMEM((hidden, width), BF16),
            pltpu.VMEM((2, heads, rows, rows), F32),
            pltpu.VMEM((4, rows, hw), BF16),
            pltpu.VMEM((rows, width + LANES), BF16),
            pltpu.VMEM((group, LANES), jnp.int32),
            pltpu.VMEM((3 * LANES, hidden), BF16),
            dma((1, 4)),
            dma((1, 4)),
            dma((6,)),
            dma((6,)),
            dma((4, 4)),
            dma((4, 4)),
            dma((4,)),
            dma((4,)),
            pltpu.VMEM((8, LANES), F32),
        ]
        + experts_scratch(False, spans, rows, group, width, hidden),
        compiler_params=pltpu.CompilerParams(
            collective_id=2, has_side_effects=True, vmem_limit_bytes=60 * 1024 * 1024
        ),
    )(*operands)


def experts_scratch(forth, spans, rows, group, width, hidden):
    streams = {
        "back": scatter_scratch(spans, BF16, (rows, width), (group, width)),
        "dots": scatter_scratch(spans, F32, (8, rows), (4, 8, rows)),
        "forth": (
            scatter_scratch(spans, BF16, (rows, width), (group, width))
            if forth
            else {"sum": pltpu.SMEM((1,), F32)}
        ),
    }
    return [
        pltpu.VMEM((TILE, hidden), F32),
        pltpu.VMEM((TILE, hidden), F32),
        pltpu.VMEM((TILE, hidden), F32),
        pltpu.VMEM((TILE, hidden), BF16),
        pltpu.VMEM((TILE, hidden), BF16),
        streams,
        pltpu.SemaphoreType.DMA((4, 4)),
        pltpu.SemaphoreType.DMA((4, 4)),
        pltpu.SemaphoreType.DMA((3, 4, 4)),
        pltpu.SemaphoreType.DMA((3, 4, 4)),
    ]


def tail_kernel(
    scale,
    gmid_own,
    probs,
    qkv,
    attended,
    normed,
    wqkv,
    wproj,
    gated,
    gpre,
    nall,
    grads,
    down,
    tokens,
    fixed,
    forth_sum,
    gone_sum,
    gup,
    gdown,
    gwq,
    gwp,
    small,
    wall,
    ptmp,
    vtmp,
    wtmp,
    buckets,
    gmid,
    gatt,
    gqkv,
    gscore,
    wide_up,
    wide_down,
    half_send,
    half_recv,
    wsend,
    wrecv,
    wsum,
    zsend,
    zrecv,
    smalls,
    forth_buf,
    gone_buf,
    msend,
    mrecv,
    fsend,
    frecv,
    osend,
    orecv,
    xsend,
    xrecv,
    wgsend,
    wgrecv,
):
    spots = neighbours()
    f, i, t, sibling, across, along = spots
    peer = (1 - f, i, t)
    rows, width = gmid_own.shape
    spans, group, _ = nall.shape
    heads, hw = probs.shape[0], attended.shape[1]
    head = hw // heads
    own = width // 2
    piece = own // spans
    blocks = group // rows

    def block(index):
        return pl.ds(pl.multiple_of(index * rows, rows), rows)

    def half(index):
        return pl.ds(pl.multiple_of(index * own, LANES), own)

    mids = gather_copies(spots, gmid_own, lambda tt, ii: gmid.at[block(ii), :], msend, mrecv, 1)
    forth_buf["sum"], gone_buf["sum"] = forth_sum, gone_sum
    forth = Scatter(
        spots, forth_buf, lambda k, index: forth_buf["part"].at[k, block(index), :], fsend, frecv
    )
    gone = Scatter(
        spots, gone_buf, lambda k, index: gone_buf["part"].at[k, block(index), :], osend, orecv
    )
    halves = [
        remote(half_send[n], half_recv[n], xsend.at[n], xrecv.at[n], peer) for n in range(2)
    ]
    wx = [
        remote(wsend.at[n], wrecv.at[n], xsend.at[2 + n], xrecv.at[2 + n], peer) for n in range(2)
    ]
    wz = [
        {
            k: remote(
                zsend.at[n, pl.ds(pl.multiple_of(xor(t, k) * piece, 16), piece), :],
                zrecv.at[n, k],
                xsend.at[4 + 3 * n + k - 1],
                xrecv.at[4 + 3 * n + k - 1],
                along[k],
            )
            for k in (1, 2, 3)
        }
        for n in range(2)
    ]
    wg = [
        gather_copies(
            spots,
            wall.at[n, t, i],
            lambda tt, ii, n=n: wall.at[n, tt, ii],
            wgsend.at[n],
            wgrecv.at[n],
        )
        for n in range(2)
    ]
    steps = [
        remote(smalls.at[n], smalls.at[3 + n], xsend.at[10 + n], xrecv.at[10 + n], target)
        for n, target in enumerate((sibling, across, peer))
    ]
    rounds = [
        remote(small, smalls.at[5 + k], xsend.at[12 + k], xrecv.at[12 + k], along[k])
        for k in (1, 2, 3)
    ]

    greet([sibling, across, peer] + along[1:])
    gmid[block(i), :] = gmid_own[...]
    mids[0, 2].start()
    mids[0, 1].start()
    apart = lax.broadcasted_iota(jnp.int32, (rows, rows), 0) - lax.broadcasted_iota(
        jnp.int32, (rows, rows), 1
    )
    for n in range(2):
        value = jnp.where(apart + n * rows >= 0, 0, -1)
        for bound in BOUNDS:
            value = value + jnp.where(apart + n * rows >= bound, 1, 0)
        buckets[n] = value

    def forth_part(k):
        tk = xor(t, k)

        def tile(m, carry):
            at = pl.ds(pl.multiple_of(m * TILE, TILE), TILE)
            forth_buf["part"][k, at, :] = dot(gated[tk, at, :], down[...], 1, 0).astype(BF16)
            return carry

        lax.fori_loop(0, group // TILE, tile, 0)
        forth.first(k)

    def up_half(which, out):
        out[...] = jnp.zeros_like(out)

        def step(c, carry):
            out[...] += dot(nall[c, :, half(which)], gpre[c], 0, 0)
            return carry

        lax.fori_loop(0, spans, step, 0)

    def down_half(which, out):
        out[...] = jnp.zeros_like(out)

        def step(c, carry):
            out[...] += dot(gated[c], grads[c, :, half(which)], 0, 0)
            return carry

        lax.fori_loop(0, spans, step, 0)

    forth_part(1)
    forth_part(2)
    mids[0, 2].wait_recv()
    mids[0, 3].start()
    down_half(1 - f, wide_down)
    half_send[0][...] = wide_down[...].astype(BF16)
    halves[0].start()
    forth.second(1)
    forth_part(3)
    forth_part(0)
    forth.second(2)
    mids[0, 1].wait_recv()
    mids[0, 3].wait_recv()

    here = wproj[pl.ds(pl.multiple_of(i * hw, 16), hw), :]
    gatt[...] = dot(gmid[...], here, 1, 1).astype(BF16)
    ptmp[...] = dot(attended[...], gmid[...], 0, 0)
    for h in range(heads):
        cols = pl.ds(h * head, head)
        gqkv[:, pl.ds(2 * hw + h * head, head)] = dot(
            probs[h].astype(BF16), gatt[:, cols], 0, 0
        ).astype(BF16)
    vtmp[...] = dot(normed[...], gqkv[:, pl.ds(2 * hw, hw)], 0, 0)
    low, part = piece // 2, hw // spans
    for side, out in ((1 - f, wsend), (f, wsum)):
        for n in range(spans):
            out[0, pl.ds(n * piece, part), :] = ptmp[pl.ds(n * part, part), half(side)].astype(
                out.dtype
            )
            for e in range(2):
                start = pl.multiple_of(side * own + n * piece + e * low, 16)
                out[0, pl.ds(n * piece + part, low), pl.ds(e * hw, hw)] = vtmp[
                    pl.ds(start, low), :
                ].astype(out.dtype)
    wx[0].start()
    forth.second(3)
    forth.second(0)
    forth.third(1)

    table = small.at[pl.ds(0, heads * BUCKETS), :]
    def reduce_along(n):
        wx[n].wait_recv()
        total = wsum[n] + wrecv[n].astype(F32)
        wsum[n] = total
        zsend[n] = total.astype(BF16)
        for k in (1, 2, 3):
            wz[n][k].start()

    def share(n):
        total = wsum[n, pl.ds(pl.multiple_of(t * piece, 16), piece), :]
        for k in (1, 2, 3):
            wz[n][k].wait_recv()
            total = total + zrecv[n, k].astype(F32)
        wall[n, t, i] = total.astype(BF16)
        wg[n][0, 2].start()
        wg[n][0, 1].start()
        for k in (1, 2, 3):
            wg[n][k, 0].start()

    def onward(n):
        for k in (1, 2, 3):
            wg[n][k, 0].wait_recv()
            wg[n][k, 2].start()
            wg[n][k, 1].start()

    def relay(n):
        for k in range(4):
            wg[n][k, 2].wait_recv()
            wg[n][k, 3].start()

    for h in range(heads):
        cols = pl.ds(h * head, head)
        keys = pl.ds(hw + h * head, head)

        def rowtile(m, carry, h=h, cols=cols, keys=keys):
            at = block(m)
            grad_probs = dot(gatt[at, cols], qkv[:, pl.ds(2 * hw + h * head, head)], 1, 1)
            prob = probs[h, at, :]
            inner = jnp.sum(prob * grad_probs, axis=1, keepdims=True)
            score = (prob * (grad_probs - inner)).astype(BF16)
            gscore[h, at, :] = score
            gqkv[at, cols] = (dot(score, qkv[:, keys], 1, 0) * scale).astype(BF16)
            return carry

        lax.fori_loop(0, blocks, rowtile, 0)
        gqkv[:, keys] = (dot(gscore[h], qkv[:, cols], 0, 0) * scale).astype(BF16)
        if h == 0:
            forth.third(2)
        if h == 1:
            forth.third(3)

    def gone_tile(m, carry):
        at = block(m)
        gone_buf["part"][0, at, :] = dot(gqkv[at, :], wqkv[...], 1, 1).astype(BF16)
        return carry

    lax.fori_loop(0, blocks, gone_tile, 0)
    gone.first(0)
    wtmp[...] = dot(normed[...], gqkv[:, pl.ds(0, 2 * hw)], 0, 0)
    wsend[1] = wtmp[half(1 - f), :].astype(BF16)
    wsum[1] = wtmp[half(f), :]
    wx[1].start()
    gone.second(0)
    up_half(1 - f, wide_up)
    half_send[1][...] = wide_up[...].astype(BF16)
    halves[1].start()
    reduce_along(0)
    forth.third(0)

    def bucket_sums(h):
        near = jnp.zeros((rows, rows), F32)
        after = jnp.zeros((rows, rows), F32)
        far = jnp.zeros((rows, rows), F32)
        for a in range(blocks):
            for b in range(a + 1):
                score = gscore[h, pl.ds(a * rows, rows), pl.ds(b * rows, rows)].astype(F32)
                if a == b:
                    near = near + score
                elif a == b + 1:
                    after = after + score
                else:
                    far = far + score
        sums = []
        for b in range(BUCKETS):
            value = jnp.where(buckets[0] == b, near, 0.0) + jnp.where(
                buckets[1] == b, after, 0.0
            )
            if b == BUCKETS - 1:
                value = value + far
            sums.append(jnp.sum(value, axis=0, keepdims=True))
        sums = jnp.sum(jnp.concatenate(sums, axis=0), axis=1, keepdims=True)
        lane = lax.broadcasted_iota(jnp.int32, (BUCKETS, LANES), 1)
        smalls[0, pl.ds(h * BUCKETS, BUCKETS), :] = jnp.where(lane == i, sums, 0.0)

    for h in range(heads):
        bucket_sums(h)
    gone.third(0)
    value = tokens[...].astype(F32)
    gain = jnp.sum(gone_sum[...] * (value * rms_scale(value)), axis=0, keepdims=True)
    base = heads * BUCKETS
    smalls[0, pl.ds(base, smalls.shape[1] - base), :] = fixed[...]
    for c in range(width // LANES):
        smalls[0, pl.ds(base + c, 1), :] = gain[:, c * LANES : (c + 1) * LANES]
    share(0)
    steps[0].start()
    down_half(f, gdown)
    reduce_along(1)
    up_half(f, wide_up)
    steps[0].wait_recv()
    smalls[1] = smalls[0] + smalls[3]
    steps[1].start()
    onward(0)
    share(1)
    steps[1].wait_recv()
    smalls[2] = smalls[1] + smalls[4]
    steps[2].start()
    relay(0)
    steps[2].wait_recv()
    small[...] = smalls[2] + smalls[5]
    for copy in rounds:
        copy.start()
    onward(1)
    forth.last()
    relay(1)
    for copy in rounds:
        copy.wait()
    small[...] = small[...] + smalls[6] + smalls[7] + smalls[8]
    halves[0].wait_recv()
    gdown[...] = gdown[...] + half_recv[0][...].astype(F32)
    halves[1].wait_recv()
    units = gup.shape[2]
    for e in range(gup.shape[0]):
        cols = pl.ds(e * units, units)
        gup[e] = wide_up[:, cols] + half_recv[1][:, cols].astype(F32)
    for n in range(2):
        for k in range(4):
            wg[n][k, 1].wait_recv()
            wg[n][k, 3].wait_recv()
    for n in range(spans):
        for c in range(blocks):
            gwp[pl.ds(c * hw + n * part, part), :] = wall[0, n, c, pl.ds(0, part), :]
            for e in range(2):
                gwq[pl.ds(n * piece + e * low, low), pl.ds(2 * width + c * hw, hw)] = wall[
                    0, n, c, pl.ds(part, low), pl.ds(e * hw, hw)
                ]
                gwq[pl.ds(n * piece, piece), pl.ds(e * width + c * hw, hw)] = wall[
                    1, n, c, :, pl.ds(e * hw, hw)
                ]
    copies = halves + wx + steps + list(mids.values())
    copies += list(forth.copies.values()) + list(gone.copies.values())
    for n in range(2):
        copies += list(wz[n].values()) + list(wg[n].values())
    for copy in copies:
        copy.wait_send()


def tail_call(scale, experts, *operands):
    gmid, probs, qkv, attended, normed, wqkv, wproj, gated, gpre, nall = operands[:10]
    rows, width = gmid.shape
    spans, group, hidden = gpre.shape
    heads = probs.shape[0]
    hw = attended.shape[1]
    own = width // 2
    piece = own // spans
    extra = 8 * width // LANES
    vmem = pl.BlockSpec(memory_space=pltpu.VMEM)
    shape = jax.ShapeDtypeStruct
    dma = pltpu.SemaphoreType.DMA
    table = heads * BUCKETS + extra
    return pl.pallas_call(
        functools.partial(tail_kernel, scale),
        out_shape=(
            shape((rows, width), F32),
            shape((rows, width), F32),
            shape((experts, own, hidden // experts), F32),
            shape((hidden, own), F32),
            shape((own, 3 * width), BF16),
            shape((width, own), BF16),
            shape((table, LANES), F32),
        ),
        in_specs=[vmem] * len(operands),
        out_specs=[vmem] * 7,
        scratch_shapes=[
            pltpu.VMEM((2, spans, 4, piece, 2 * hw), BF16),
            pltpu.VMEM((hw, width), F32),
            pltpu.VMEM((width, hw), F32),
            pltpu.VMEM((width, 2 * hw), F32),
            pltpu.VMEM((2, rows, rows), jnp.int32),
            pltpu.VMEM((group, width), BF16),
            pltpu.VMEM((group, hw), BF16),
            pltpu.VMEM((group, 3 * hw), BF16),
            pltpu.VMEM((heads, group, group), BF16),
            pltpu.VMEM((own, hidden), F32),
            pltpu.VMEM((hidden, own), F32),
            [pltpu.VMEM((hidden, own), BF16), pltpu.VMEM((own, hidden), BF16)],
            [pltpu.VMEM((hidden, own), BF16), pltpu.VMEM((own, hidden), BF16)],
            pltpu.VMEM((2, own, 2 * hw), BF16),
            pltpu.VMEM((2, own, 2 * hw), BF16),
            pltpu.VMEM((2, own, 2 * hw), F32),
            pltpu.VMEM((2, own, 2 * hw), BF16),
            pltpu.VMEM((2, 4, piece, 2 * hw), BF16),
            pltpu.VMEM((9, table, LANES), F32),
            scatter_scratch(spans, BF16, (rows, width), (group, width)),
            scatter_scratch(1, BF16, (rows, width), (group, width)),
            dma((1, 4)),
            dma((1, 4)),
            dma((spans, 4)),
            dma((spans, 4)),
            dma((1, 4)),
            dma((1, 4)),
            dma((16,)),
            dma((16,)),
            dma((2, 4, 4)),
            dma((2, 4, 4)),
        ],
        compiler_params=pltpu.CompilerParams(
            collective_id=1, has_side_effects=True, vmem_limit_bytes=58 * 1024 * 1024
        ),
    )(*operands)


def local(
    tokens,
    seg_ids,
    routes,
    norm_attn,
    weight_qkv,
    weight_proj,
    rel_table,
    norm_ffn,
    weight_router,
    expert_up,
    expert_down,
    cotangent,
):
    rows = tokens.shape[1]
    width = tokens.shape[2]
    heads = rel_table.shape[0]
    head_size = width // heads
    ctx_count = lax.axis_size("ctx")
    heads_here = heads // ctx_count
    hw = heads_here * head_size
    experts = expert_up.shape[0]
    units = expert_up.shape[2]
    length = seg_ids.shape[1]
    score_scale = head_size ** (-0.5)
    ctx_index = lax.axis_index("ctx")
    fsdp_index = lax.axis_index("fsdp")
    own_width = norm_attn.shape[0]
    world = ("ctx", "tp")

    tp_count = lax.axis_size("tp")
    pair = lax.axis_size("fsdp") == 2
    segment = seg_ids[0]
    inputs = tokens[0].astype(F32)
    scale_one = rms_scale(inputs)
    qkv_part = jnp.concatenate(
        [
            lax.dynamic_slice_in_dim(weight_qkv, s * width + ctx_index * hw, hw, 1)
            for s in range(3)
        ],
        axis=1,
    )
    expert_ids = jnp.arange(LANES, dtype=jnp.int32)[None, :]
    named = (routes[0][:, 0:1] == expert_ids) | (routes[0][:, 1:2] == expert_ids)
    packed_grad = jnp.concatenate([cotangent[0], named.astype(BF16)], axis=1)
    block = MAX_DISTANCE
    offset = (
        lax.broadcasted_iota(jnp.int32, (1, block, block), 1)
        - lax.broadcasted_iota(jnp.int32, (1, block, block), 2)
    )

    hidden = experts * units
    wide = (
        jnp.arange(hidden, dtype=jnp.int32)[None, :] // units
        == jnp.arange(3 * LANES, dtype=jnp.int32)[:, None] % LANES
    ).astype(BF16)
    if pair:
        up_part = jnp.swapaxes(expert_up, 1, 2).reshape(hidden, own_width)
        small_part = jnp.concatenate(
            [
                weight_router.T,
                norm_attn[None],
                norm_ffn[None],
                jnp.zeros((14 - experts, own_width), BF16),
            ],
            axis=0,
        )
        (
            normed_group,
            projected,
            probs,
            attended,
            middle,
            normed_two,
            qkv_here,
            proj_full,
            down,
            small,
            grads_all,
            grad_middle,
            grad_mid_low,
            fixed,
            normed_all,
            grad_pre,
            gated,
        ) = front_call(
            score_scale,
            experts,
            heads_here,
            hw,
            tokens[0],
            cotangent[0],
            routes[0],
            seg_ids,
            rel_table,
            qkv_part,
            weight_proj,
            up_part,
            expert_down.reshape(hidden, own_width),
            small_part,
        )
        gain_one = small[experts].astype(F32)
    else:
        token_group = lax.all_gather(tokens[0], "ctx", axis=0, tiled=True)
        small = jnp.concatenate([norm_attn[None], norm_ffn[None], weight_router.T], axis=0)
        small = gather(small, "fsdp", 1)
        gain_one = small[0].astype(F32)
        gain_two = small[1].astype(F32)
        router_t = small[2:]
        qkv_here = gather(qkv_part, "fsdp", 0)
        proj_full = gather(weight_proj, "fsdp", 1)
        up_t = gather(
            jnp.swapaxes(expert_up, 1, 2).reshape(experts * units, own_width), "fsdp", 1
        )
        down = gather(expert_down.reshape(experts * units, own_width), "fsdp", 1)
        grad_routes = lax.all_gather(packed_grad, ("tp", "ctx"), axis=0, tiled=True)

        table_here = lax.dynamic_slice_in_dim(rel_table, ctx_index * heads_here, heads_here, 0)
        def bias_block(distance):
            value = jnp.broadcast_to(table_here[:, 0][:, None, None], (heads_here, block, block))
            for number, bound in enumerate(BOUNDS, 1):
                value = jnp.where(distance >= bound, table_here[:, number][:, None, None], value)
            return value

        near = bias_block(offset)
        next_near = bias_block(offset + block)
        far = jnp.broadcast_to(table_here[:, BUCKETS - 1][:, None, None], (heads_here, block, block))
        blocks = length // block
        picks = {0: near, 1: next_near}
        bias = jnp.concatenate(
            [
                jnp.concatenate(
                    [picks.get(i - j, far) for j in range(blocks)],
                    axis=2,
                )
                for i in range(blocks)
            ],
            axis=1,
        )
        positions = jnp.arange(length, dtype=jnp.int32)
        allowed = (segment[:, None] == segment[None, :]) & (positions[:, None] >= positions[None, :])
        bias = jnp.where(allowed[None], bias, MASK_FILL)

        inputs_group = token_group.astype(F32)
        normed_group = (inputs_group * rms_scale(inputs_group) * gain_one).astype(BF16)
        projected = dot(normed_group, qkv_here, 1, 0).astype(BF16)
        by_head = projected.reshape(length, 3, heads_here, head_size)
        query, key, value = by_head[:, 0], by_head[:, 1], by_head[:, 2]

        scores = (
            jnp.einsum("qhd,khd->hqk", query, key, preferred_element_type=F32) * score_scale + bias
        )
        peak = jnp.max(scores, axis=-1, keepdims=True)
        weights = jnp.exp(scores - peak)
        probs = weights / jnp.sum(weights, axis=-1, keepdims=True)
        low_probs = probs.astype(BF16)
        attended = (
            jnp.einsum("hqk,khd->qhd", low_probs, value, preferred_element_type=F32)
            .astype(BF16)
            .reshape(length, hw)
        )
        mixed = lax.all_to_all(attended, "ctx", split_axis=0, concat_axis=1, tiled=True)
        mixed, grad_routes, up_t, down = lax.optimization_barrier((mixed, grad_routes, up_t, down))
        middle = inputs + dot(mixed, proj_full, 1, 0)
        scale_two = rms_scale(middle)
        normed_two = (middle * scale_two * gain_two).astype(BF16)

        router_pad = jnp.pad(router_t, ((0, LANES - experts), (0, 0)))
        grad_normed_two, result, dots_own, normed_all, grad_pre, gated = experts_call(
            True,
            normed_two,
            grad_routes.reshape(tp_count, length, width + LANES),
            up_t,
            down,
            router_pad,
            wide,
        )
    if pair:
        result, grad_normed_one, grad_up, grad_down, grad_qkv, grad_proj, packed = tail_call(
            score_scale,
            experts,
            grad_mid_low,
            probs,
            projected,
            attended,
            normed_group,
            qkv_here,
            proj_full,
            gated,
            grad_pre,
            normed_all,
            grads_all,
            down,
            tokens[0],
            fixed,
        )
        output = (middle + result).astype(BF16)[None]
        weighted_one = grad_normed_one * gain_one
        grad_tokens = (
            grad_middle
            + scale_one * weighted_one
            - inputs * scale_one**3 * jnp.mean(weighted_one * inputs, axis=1, keepdims=True)
        )
        grad_down = grad_down.reshape(experts, units, own_width)
        edge = heads_here * BUCKETS
        table_grad = packed[:edge, :ctx_count].T.reshape(heads, BUCKETS)
        gains = packed[edge:].reshape(-1, width)
        gains = lax.dynamic_slice_in_dim(gains, fsdp_index * own_width, own_width, 1)
        return (
            output,
            grad_tokens[None],
            gains[0],
            grad_qkv.astype(F32),
            grad_proj.astype(F32),
            table_grad,
            gains[1],
            gains[2 : 2 + experts].T,
            grad_up,
            grad_down,
        )
    gate_dots = dots_own[:experts].T
    total_rows = tp_count * length
    grad_out = cotangent[0].astype(F32)
    number = jnp.arange(experts, dtype=jnp.int32)[None, :]
    chosen = (routes[0][:, 0:1] == number) | (routes[0][:, 1:2] == number)
    gates = gates_of(dot(normed_two, router_t, 1, 1), chosen)
    grad_logits = gates * (gate_dots - jnp.sum(gates * gate_dots, axis=1, keepdims=True))
    grad_normed_two = grad_normed_two + jnp.dot(
        grad_logits, router_t.astype(F32), precision=lax.Precision.HIGHEST
    )
    grad_router = lax.dot_general(
        grad_logits,
        normed_two.astype(F32),
        (((0,), (0,)), ((), ())),
        precision=lax.Precision.HIGHEST,
    )
    weighted_two = grad_normed_two * gain_two
    grad_gain_two = jnp.sum(grad_normed_two * middle * scale_two, axis=0)
    grad_middle = (
        grad_out
        + scale_two * weighted_two
        - middle * scale_two**3 * jnp.mean(weighted_two * middle, axis=1, keepdims=True)
    )
    normed_all = normed_all.reshape(total_rows, width)
    grad_pre = grad_pre.reshape(total_rows, hidden)
    gated = gated.reshape(total_rows, hidden)
    grad_all = grad_routes[:, :width]
    grad_up = exchange_sum(dot(grad_pre, normed_all, 0, 0), "fsdp", 1)
    grad_up = jnp.swapaxes(grad_up.reshape(experts, units, own_width), 1, 2)
    grad_down = exchange_sum(dot(gated, grad_all, 0, 0), "fsdp", 1)
    grad_down = grad_down.reshape(experts, units, own_width)

    grad_mid_group = lax.all_gather(grad_middle.astype(BF16), "ctx", axis=0, tiled=True)
    proj_rows = lax.dynamic_slice_in_dim(proj_full, ctx_index * hw, hw, 0)
    grad_attended = dot(grad_mid_group, proj_rows, 1, 1).astype(BF16)
    grad_heads = grad_attended.reshape(length, heads_here, head_size)
    grad_value = jnp.einsum("hqk,qhd->khd", low_probs, grad_heads, preferred_element_type=F32)
    grad_probs = jnp.einsum("qhd,khd->hqk", grad_heads, value, preferred_element_type=F32)
    grad_scores = (
        probs * (grad_probs - jnp.sum(probs * grad_probs, axis=-1, keepdims=True))
    ).astype(BF16)
    grad_query = (
        jnp.einsum("hqk,khd->qhd", grad_scores, key, preferred_element_type=F32) * score_scale
    )
    grad_key = (
        jnp.einsum("hqk,qhd->khd", grad_scores, query, preferred_element_type=F32) * score_scale
    )
    grad_qkv = jnp.concatenate(
        [
            grad_query.astype(BF16).reshape(length, hw),
            grad_key.astype(BF16).reshape(length, hw),
            grad_value.astype(BF16).reshape(length, hw),
        ],
        axis=1,
    )
    grad_normed_one = exchange_sum(dot(grad_qkv, qkv_here, 1, 1), "ctx", 0)

    weight_part = jnp.concatenate(
        [dot(normed_group, grad_qkv, 0, 0), dot(grad_mid_group, attended, 0, 0)], axis=1
    )
    weight_own = exchange_sum(weight_part, "fsdp", 0)
    grad_scores, weight_own = lax.optimization_barrier((grad_scores, weight_own))
    weight_own = exchange_sum(weight_own, "tp", 0).astype(BF16)
    def score_block(i, j):
        return grad_scores[
            :, i * block : (i + 1) * block, j * block : (j + 1) * block
        ].astype(F32)

    near_sum = sum(score_block(i, i) for i in range(blocks))
    next_sum = sum(score_block(i + 1, i) for i in range(blocks - 1))
    far_sum = sum(
        jnp.sum(score_block(i, j), axis=(1, 2)) for i in range(blocks) for j in range(i - 1)
    )
    lows = [0] + BOUNDS
    highs = BOUNDS + [2 * block]
    bucket_sums = [
        jnp.sum(jnp.where((offset >= lo) & (offset < hi), near_sum, 0.0), axis=(1, 2))
        + jnp.sum(
            jnp.where((offset + block >= lo) & (offset + block < hi), next_sum, 0.0), axis=(1, 2)
        )
        for lo, hi in zip(lows, highs)
    ]
    bucket_sums[-1] = bucket_sums[-1] + far_sum
    table_here_grad = jnp.stack(bucket_sums, axis=1)
    table_term = lax.dynamic_update_slice_in_dim(
        jnp.zeros((heads, BUCKETS), F32), table_here_grad, ctx_index * heads_here, 0
    )

    weighted_one = grad_normed_one * gain_one
    grad_gain_one = jnp.sum(grad_normed_one * inputs * scale_one, axis=0)
    grad_tokens = (
        grad_middle
        + scale_one * weighted_one
        - inputs * scale_one**3 * jnp.mean(weighted_one * inputs, axis=1, keepdims=True)
    )
    packed = jnp.concatenate(
        [
            grad_gain_one,
            grad_gain_two,
            grad_router.reshape(-1),
            table_term.reshape(-1),
        ]
    ).reshape(-1, 128)
    packed, weight_own = lax.optimization_barrier((packed, weight_own))
    packed = lax.psum(packed, ("fsdp", "ctx", "tp")).reshape(-1)
    packed, result = lax.optimization_barrier((packed, result))
    output = (middle + result).astype(BF16)[None]
    weight_all = lax.all_gather(weight_own, world, axis=0, tiled=True).astype(F32)
    weight_all = weight_all.reshape(ctx_count, own_width, 4 * hw)
    grad_weight_qkv = jnp.concatenate(
        [
            weight_all[c, :, s * hw : (s + 1) * hw]
            for s in range(3)
            for c in range(ctx_count)
        ],
        axis=1,
    )
    grad_weight_proj = jnp.swapaxes(weight_all[:, :, 3 * hw :], 1, 2).reshape(width, own_width)
    gains = packed[: (2 + experts) * width].reshape(2 + experts, width)
    gains = lax.dynamic_slice_in_dim(gains, fsdp_index * own_width, own_width, 1)
    table_grad = packed[(2 + experts) * width :].reshape(heads, BUCKETS)
    return (
        output,
        grad_tokens[None],
        gains[0],
        grad_weight_qkv,
        grad_weight_proj,
        table_grad,
        gains[1],
        gains[2:].T,
        grad_up,
        grad_down,
    )


def solution(mesh):
    rows = P(("fsdp", "tp"), "ctx", None)
    in_specs = (
        rows,
        P(("fsdp", "tp"), None),
        rows,
        P("fsdp"),
        P("fsdp", None),
        P(None, "fsdp"),
        P(),
        P("fsdp"),
        P("fsdp", None),
        P(None, "fsdp", ("ctx", "tp")),
        P(None, ("ctx", "tp"), "fsdp"),
        rows,
    )
    out_specs = (
        rows,
        rows,
        P("fsdp"),
        P("fsdp", None),
        P(None, "fsdp"),
        P(),
        P("fsdp"),
        P("fsdp", None),
        P(None, "fsdp", ("ctx", "tp")),
        P(None, ("ctx", "tp"), "fsdp"),
    )
    return jax.shard_map(local, mesh=mesh, in_specs=in_specs, out_specs=out_specs, check_vma=False)
```

```python
import functools

import jax
import jax.numpy as jnp
import numpy as np
from jax import lax
from jax.experimental import pallas as pl
from jax.experimental.pallas import tpu as pltpu
from jax.sharding import PartitionSpec as P

BUCKETS = 32
MAX_DISTANCE = 128
EPSILON = 1e-06
MASK_FILL = -1e30
F32 = jnp.float32
BF16 = jnp.bfloat16


def bucket_bounds(buckets, far_reach):
    exact_count = buckets // 2
    bounds = []
    for number in range(1, buckets):
        if number <= exact_count:
            bounds.append(number)
        else:
            exponent = (number - exact_count) / (buckets - exact_count)
            bounds.append(int(np.ceil(exact_count * (far_reach / exact_count) ** exponent)))
    return bounds


BOUNDS = bucket_bounds(BUCKETS, MAX_DISTANCE)


def rms_scale(values):
    return lax.rsqrt(jnp.mean(values * values, axis=-1, keepdims=True) + EPSILON)


def dot(a, b, ca, cb):
    return lax.dot_general(a, b, (((ca,), (cb,)), ((), ())), preferred_element_type=F32)


def gather(shard, axis, dim):
    count = lax.axis_size(axis)
    size = shard.shape[dim]
    me = lax.axis_index(axis)
    pieces = [shard] + [
        lax.ppermute(shard, axis, [(i, (i + step) % count) for i in range(count)])
        for step in range(1, count)
    ]
    if count == 2:
        first = me == 0
        return jnp.concatenate(
            [jnp.where(first, pieces[0], pieces[1]), jnp.where(first, pieces[1], pieces[0])],
            axis=dim,
        )
    shape = list(shard.shape)
    shape[dim] = count * size
    whole = jnp.zeros(shape, shard.dtype)
    for step, piece in enumerate(pieces):
        source = lax.rem(me + count - step, count)
        whole = lax.dynamic_update_slice_in_dim(whole, piece, source * size, dim)
    return whole


def exchange_sum(part, axis, dim, kind=BF16):
    count = lax.axis_size(axis)
    size = part.shape[dim] // count
    me = lax.axis_index(axis)
    total = lax.dynamic_slice_in_dim(part, me * size, size, dim).astype(F32)
    for step in range(1, count):
        target = lax.rem(me + step, count)
        piece = lax.dynamic_slice_in_dim(part, target * size, size, dim).astype(kind)
        total = total + lax.ppermute(
            piece, axis, [(i, (i + step) % count) for i in range(count)]
        ).astype(F32)
    return total


MESH = pl.DeviceIdType.MESH
TILE = 256
SLAB = 32
LANES = 128


def flip(value, bit):
    return value + bit - 2 * bit * lax.rem(lax.div(value, bit), 2)


def xor(value, mask):
    for bit in (1, 2):
        if mask & bit:
            value = flip(value, bit)
    return value


def place():
    return lax.axis_index("fsdp"), lax.axis_index("ctx"), lax.axis_index("tp")


def remote(src, dst, send, recv, target):
    return pltpu.make_async_remote_copy(
        src_ref=src,
        dst_ref=dst,
        send_sem=send,
        recv_sem=recv,
        device_id=target,
        device_id_type=MESH,
    )


def greet(targets):
    barrier = pltpu.get_barrier_semaphore()
    for target in targets:
        pl.semaphore_signal(barrier, inc=1, device_id=target, device_id_type=MESH)
    pl.semaphore_wait(barrier, len(targets))


def tanh_gelu(u):
    first = 0.7978845608028654
    cubic = 0.044715 * first
    square = u * u
    wave = jnp.tanh(u * (first + cubic * square))
    half = 0.5 + 0.5 * wave
    slope = half + (0.5 * u) * (1.0 - wave * wave) * (first + 3.0 * cubic * square)
    return u * half, slope


def gather_copies(spots, source, slot, send, recv, spans=4):
    f, i, t, sibling, across, along = spots

    def one(k, j):
        ends = send.at[k, j], recv.at[k, j]
        if j == 0:
            return remote(source, slot(t, i), *ends, along[k])
        here = slot(xor(t, k), i if j < 3 else flip(i, 2))
        origin = source if (k == 0 and j < 3) else here
        return remote(origin, here, *ends, across if j == 2 else sibling)

    return {(k, j): one(k, j) for k in range(spans) for j in range(4) if (k, j) != (0, 0)}


def neighbours():
    f, i, t = place()
    along = [None] + [(f, i, xor(t, k)) for k in (1, 2, 3)]
    return f, i, t, (f, flip(i, 1), t), (f, flip(i, 2), t), along


class Scatter:
    def __init__(self, spots, buf, part, send, recv):
        f, self.i, t, sibling, across, along = spots
        self.buf, self.part = buf, part
        self.copies = {}
        for k in range(buf["near"].shape[0]):
            for stage in range(4 if k else 3):
                ends = send.at[k, stage], recv.at[k, stage]
                if stage < 2:
                    src = part(k, xor(self.i, 1 if stage == 0 else 3))
                    copy = remote(src, buf["near"].at[k, stage], *ends, sibling)
                elif stage == 2:
                    copy = remote(buf["out"].at[k, 0], buf["far"].at[k, 0], *ends, across)
                else:
                    copy = remote(buf["out"].at[k, 1], buf["far"].at[k, 1], *ends, along[k])
                self.copies[k, stage] = copy

    def first(self, k):
        self.copies[k, 1].start()
        self.copies[k, 0].start()

    def second(self, k):
        b = self.buf
        self.copies[k, 1].wait_recv()
        total = self.part(k, flip(self.i, 2))[...].astype(F32) + b["near"][k, 1].astype(F32)
        b["out"][k, 0] = total.astype(b["out"].dtype)
        self.copies[k, 2].start()

    def third(self, k):
        b = self.buf
        self.copies[k, 0].wait_recv()
        self.copies[k, 2].wait_recv()
        total = (
            self.part(k, self.i)[...].astype(F32)
            + b["near"][k, 0].astype(F32)
            + b["far"][k, 0].astype(F32)
        )
        if k == 0:
            b["sum"][...] = total
        else:
            b["out"][k, 1] = total.astype(b["out"].dtype)
            self.copies[k, 3].start()

    def last(self):
        b = self.buf
        for k in (1, 2, 3):
            self.copies[k, 3].wait_recv()
            b["sum"][...] = b["sum"][...] + b["far"][k, 1].astype(F32)


def gates_of(logits, chosen):
    masked = jnp.where(chosen, logits, MASK_FILL)
    raw = jnp.where(chosen, jnp.exp(masked - jnp.max(masked, axis=1, keepdims=True)), 0.0)
    return raw / jnp.sum(raw, axis=1, keepdims=True)


def experts_kernel(
    forth,
    normed,
    grads,
    up,
    down,
    router,
    wide,
    back_sum,
    forth_sum,
    dots_sum,
    nall,
    gpre,
    gated,
    pre,
    reach,
    gate,
    high,
    low,
    bufs,
    gsend,
    grecv,
    ssend,
    srecv,
    ready=None,
):
    spots = neighbours()
    f, i, t, sibling, across, along = spots
    rows, width = normed.shape
    group = nall.shape[1]

    def block(index):
        return pl.ds(pl.multiple_of(index * rows, rows), rows)

    if ready is None:
        greet([sibling, across] + along[1:])
    gather = gather_copies(
        spots, normed, lambda tt, ii: nall.at[tt, block(ii), :], gsend, grecv
    )
    nall[t, block(i), :] = normed[...]
    gather[0, 2].start()
    gather[0, 1].start()
    gather[1, 0].start()
    gather[2, 0].start()

    pick = wide[pl.ds(0, SLAB), :]

    def compute(k):
        tk = xor(t, k)
        if ready is not None:
            ready(k)

        def tile(m, carry):
            base = pl.multiple_of(m * TILE, TILE)
            piece = pl.ds(base, TILE)
            pre[...] = dot(nall[tk, piece, :], up[...], 1, 1)
            logits = dot(nall[tk, piece, :], router[...], 1, 1)
            reach[...] = dot(grads[tk, piece, pl.ds(0, width)], down[...], 1, 1)
            chosen = grads[tk, piece, pl.ds(width, LANES)].astype(F32) > 0.5
            gates = gates_of(logits, chosen)
            terms = []
            for _ in range(3):
                terms.append(gates.astype(BF16))
                gates = gates - terms[-1].astype(F32)
            gate[...] = dot(jnp.concatenate(terms, axis=1), wide[...], 1, 0)

            def slab(s, inner):
                at = pl.ds(pl.multiple_of(s * SLAB, SLAB), SLAB)
                to = pl.ds(pl.multiple_of(base + s * SLAB, SLAB), SLAB)
                for c in range(pre.shape[1] // LANES):
                    cols = pl.ds(c * LANES, LANES)
                    share = gate[at, cols]
                    act, slope = tanh_gelu(pre[at, cols])
                    act = act.astype(BF16).astype(F32)
                    pull = reach[at, cols]
                    gated[tk, to, cols] = (act * share).astype(BF16)
                    gpre[tk, to, cols] = (pull * share * slope).astype(BF16)
                    product = act * pull
                    coarse = product.astype(BF16)
                    high[at, cols] = coarse
                    low[at, cols] = (product - coarse.astype(F32)).astype(BF16)
                return inner

            lax.fori_loop(0, TILE // SLAB, slab, 0)
            dots = dot(pick, high[...], 1, 1) + dot(pick, low[...], 1, 1)
            for half in range(TILE // rows):
                bufs["dots"]["part"][k, m * (TILE // rows) + half] = dots[
                    :8, half * rows : (half + 1) * rows
                ]
            bufs["back"]["part"][k, piece, :] = dot(gpre[tk, piece, :], up[...], 1, 0).astype(BF16)
            if forth:
                bufs["forth"]["part"][k, piece, :] = dot(
                    gated[tk, piece, :], down[...], 1, 0
                ).astype(BF16)
            return carry

        lax.fori_loop(0, group // TILE, tile, 0)

    bufs["back"]["sum"], bufs["forth"]["sum"], bufs["dots"]["sum"] = back_sum, forth_sum, dots_sum

    def part_of(name):
        part = bufs[name]["part"]
        if name == "dots":
            return lambda k, index: part.at[k, index]
        return lambda k, index: part.at[k, block(index), :]

    streams = {
        name: Scatter(spots, bufs[name], part_of(name), ssend.at[n], srecv.at[n])
        for n, name in enumerate(("back", "dots", "forth") if forth else ("back", "dots"))
    }

    def first(k, which):
        for name in which:
            streams[name].first(k)

    def second(k, which):
        for name in which:
            streams[name].second(k)

    def third(k, which):
        for name in which:
            streams[name].third(k)

    def last(which):
        for name in which:
            streams[name].last()

    early = ("dots", "back")
    gather[0, 2].wait_recv()
    gather[0, 3].start()
    gather[1, 0].wait_recv()
    gather[3, 0].start()
    gather[1, 2].start()
    gather[1, 1].start()
    gather[0, 1].wait_recv()
    gather[0, 3].wait_recv()
    compute(0)
    first(0, early)
    gather[1, 2].wait_recv()
    gather[1, 3].start()
    for k in (2, 3):
        gather[k, 0].wait_recv()
        gather[k, 2].start()
        gather[k, 1].start()
    second(0, early)
    gather[1, 1].wait_recv()
    gather[1, 3].wait_recv()
    compute(1)
    first(1, early)
    for k in (2, 3):
        gather[k, 2].wait_recv()
        gather[k, 3].start()
    third(0, early)
    second(1, early)
    gather[2, 1].wait_recv()
    gather[2, 3].wait_recv()
    compute(2)
    first(2, early)
    third(1, early)
    second(2, early)
    gather[3, 1].wait_recv()
    gather[3, 3].wait_recv()
    compute(3)
    first(3, early)
    third(2, early)
    second(3, early)
    late = ("forth",) if forth else ()
    for k in range(4):
        first(k, late)
    third(3, early)
    for k in (1, 2, 3, 0):
        second(k, late)
    last(early)
    for k in (1, 2, 3, 0):
        third(k, late)
    last(late)
    copies = list(gather.values())
    for stream in streams.values():
        copies += list(stream.copies.values())
    for copy in copies:
        copy.wait_send()


def scatter_scratch(spans, kind, shape, part):
    return {
        "part": pltpu.VMEM((spans,) + part, kind),
        "near": pltpu.VMEM((spans, 2) + shape, kind),
        "out": pltpu.VMEM((spans, 2) + shape, kind),
        "far": pltpu.VMEM((spans, 2) + shape, kind),
    }


def experts_call(forth, normed, grads, up, down, router, wide):
    rows, width = normed.shape
    spans, group, _ = grads.shape
    hidden = up.shape[0]
    vmem = pl.BlockSpec(memory_space=pltpu.VMEM)

    return pl.pallas_call(
        functools.partial(experts_kernel, forth),
        out_shape=(
            jax.ShapeDtypeStruct((rows, width), F32),
            jax.ShapeDtypeStruct((rows, width) if forth else (8, LANES), F32),
            jax.ShapeDtypeStruct((8, rows), F32),
            jax.ShapeDtypeStruct((spans, group, width), BF16),
            jax.ShapeDtypeStruct((spans, group, hidden), BF16),
            jax.ShapeDtypeStruct((spans, group, hidden), BF16),
        ),
        in_specs=[vmem] * 6,
        out_specs=[vmem] * 6,
        scratch_shapes=experts_scratch(forth, spans, rows, group, width, hidden),
        compiler_params=pltpu.CompilerParams(
            collective_id=0, has_side_effects=True, vmem_limit_bytes=56 * 1024 * 1024
        ),
    )(normed, grads, up, down, router, wide)


def front_kernel(
    scale,
    experts,
    tokens,
    cotangent,
    routes,
    seg_across,
    table,
    qkv_part,
    proj_part,
    up_part,
    down_part,
    small_part,
    normed_group,
    qkv,
    probs,
    attended,
    middle,
    normed,
    qkv_full,
    proj_full,
    down_full,
    small_full,
    grads,
    gmiddle,
    gmid_low,
    fixed,
    nall,
    gpre,
    gated,
    back_sum,
    dots_sum,
    inputs,
    up_full,
    bias,
    mixed,
    packed,
    seg_down,
    wide,
    xsend,
    xrecv,
    wsend,
    wrecv,
    csend,
    crecv,
    asend,
    arecv,
    forth_sum,
    *rest,
):
    spots = neighbours()
    f, i, t, sibling, across, along = spots
    peer, diagonal = (1 - f, i, t), (f, xor(i, 3), t)
    rows, width = tokens.shape
    group, own = inputs.shape[0], width // 2
    heads, hw = probs.shape[0], attended.shape[1]
    head, blocks = hw // heads, group // rows

    def block(index):
        return pl.ds(pl.multiple_of(index * rows, rows), rows)

    def half(index):
        return pl.ds(pl.multiple_of(index * own, LANES), own)

    ins = gather_copies(spots, tokens, lambda tt, ii: inputs.at[block(ii), :], xsend, xrecv, 1)
    cots = gather_copies(spots, packed, lambda tt, ii: grads.at[tt, block(ii), :], csend, crecv)

    def give(n, src, dst, target=peer):
        return remote(src, dst, wsend.at[n], wrecv.at[n], target)

    side = half(lax.rem(i, 2))
    other = proj_full.at[side, half(1 - f)]
    quarter = own // 4

    def rows_of(base):
        return pl.ds(pl.multiple_of(base + t * quarter, 16), quarter)

    w_qkv = give(0, qkv_part.at[rows_of(0), :], qkv_full.at[rows_of(f * own), :])
    got = qkv_full.at[rows_of((1 - f) * own), :]
    w_share = [give(5 + k, got, got, along[k]) for k in (1, 2, 3)]
    w_small = give(1, small_part, small_full.at[pl.ds(0, 16), half(f)])
    w_proj = give(2, proj_part.at[side, :], proj_full.at[side, half(f)])
    w_down = give(3, down_part, down_full.at[:, half(f)])
    w_up = give(4, up_part, up_full.at[:, half(f)])
    w_proj_on = give(5, other, other, sibling)
    swaps = [
        remote(attended.at[block(xor(i, j)), :], mixed.at[i], asend.at[j], arecv.at[j], target)
        for j, target in ((1, sibling), (2, across), (3, diagonal))
    ]

    small_full[...] = jnp.zeros_like(small_full)
    lane = lax.broadcasted_iota(jnp.int32, (rows, LANES), 1)
    named = (lane == routes[:, 0:1]) | (lane == routes[:, 1:2])
    packed[:, pl.ds(0, width)] = cotangent[...]
    packed[:, pl.ds(width, LANES)] = jnp.where(named, 1.0, 0.0).astype(BF16)
    greet([sibling, across, diagonal, peer] + along[1:])
    ins[0, 2].start()
    ins[0, 1].start()
    w_small.start()
    w_qkv.start()
    cots[1, 0].start()
    inputs[block(i), :] = tokens[...]
    grads[t, block(i), :] = packed[...]
    qkv_full[half(f), :] = qkv_part[...]
    small_full[pl.ds(0, 16), half(f)] = small_part[...]
    proj_full[:, half(f)] = proj_part[...]
    down_full[:, half(f)] = down_part[...]
    up_full[:, half(f)] = up_part[...]

    for m in range(blocks):
        seg = jnp.broadcast_to(seg_across[:, pl.ds(m * rows, rows)], (rows, rows))
        seg_down[pl.ds(m * rows, rows), :] = jnp.transpose(seg)
    units = wide.shape[1] // experts
    expert = lax.broadcasted_iota(jnp.int32, (LANES, wide.shape[1]), 0)
    unit = lax.broadcasted_iota(jnp.int32, (LANES, wide.shape[1]), 1)
    here = (unit >= expert * units) & (unit < (expert + 1) * units)
    spread = jnp.where(here, 1.0, 0.0).astype(BF16)
    for n in range(3):
        wide[pl.ds(n * LANES, LANES), :] = spread
    apart = lax.broadcasted_iota(jnp.int32, (rows, rows), 0) - lax.broadcasted_iota(
        jnp.int32, (rows, rows), 1
    )
    for h in range(heads):
        for n in range(2):
            value = jnp.full((rows, rows), table[i * heads + h, 0], F32)
            for number, bound in enumerate(BOUNDS, 1):
                value = jnp.where(apart + n * rows >= bound, table[i * heads + h, number], value)
            bias[n, h] = value

    w_qkv.wait_recv()
    for copy in w_share:
        copy.start()
    w_proj.start()
    w_down.start()
    w_up.start()
    ins[0, 2].wait_recv()
    ins[0, 3].start()
    cots[2, 0].start()
    cots[3, 0].start()
    cots[0, 2].start()
    cots[0, 1].start()
    w_small.wait_recv()
    ins[0, 1].wait_recv()
    ins[0, 3].wait_recv()

    def norm_tile(m, carry):
        at = pl.ds(pl.multiple_of(m * 64, 64), 64)
        value = inputs[at, :].astype(F32)
        gain = small_full[pl.ds(4, 1), :].astype(F32)
        normed_group[at, :] = (value * rms_scale(value) * gain).astype(BF16)
        return carry

    lax.fori_loop(0, group // 64, norm_tile, 0)
    for copy in w_share:
        copy.wait_recv()
    for m in range(2):
        at = pl.ds(m * (group // 2), group // 2)
        qkv[at, :] = dot(normed_group[at, :], qkv_full[...], 1, 0).astype(BF16)

    def pass_on(k):
        cots[k, 0].wait_recv()
        cots[k, 2].start()
        cots[k, 1].start()

    def relay(k):
        cots[k, 2].wait_recv()
        cots[k, 3].start()

    pass_on(1)
    relay(0)
    for h in range(heads):
        cols = pl.ds(h * head, head)
        far = table[i * heads + h, BUCKETS - 1]
        for m in range(blocks):
            at, reach = pl.ds(m * rows, rows), (m + 1) * rows
            scores = dot(qkv[at, cols], qkv[pl.ds(0, reach), pl.ds(hw + h * head, head)], 1, 1)
            pieces = []
            for j in range(m + 1):
                allowed = seg_down[at, :] == seg_across[:, pl.ds(j * rows, rows)]
                if j == m:
                    allowed = allowed & (apart >= 0)
                add = bias[m - j, h] if m - j < 2 else far
                score = scores[:, j * rows : (j + 1) * rows] * scale + add
                pieces.append(jnp.where(allowed, score, MASK_FILL))
            scores = jnp.concatenate(pieces, axis=1)
            weights = jnp.exp(scores - jnp.max(scores, axis=1, keepdims=True))
            prob = weights / jnp.sum(weights, axis=1, keepdims=True)
            probs[h, at, pl.ds(0, reach)] = prob
            if reach < group:
                probs[h, at, pl.ds(reach, group - reach)] = jnp.zeros((rows, group - reach), F32)
            attended[at, cols] = dot(
                prob.astype(BF16), qkv[pl.ds(0, reach), pl.ds(2 * hw + h * head, head)], 1, 0
            ).astype(BF16)
        if h < 2:
            pass_on(2 + h)
            relay(1 + h)
    for swap in swaps:
        swap.start()
    mixed[i] = attended[block(i), :]
    w_proj.wait_recv()
    w_proj_on.start()
    relay(3)
    for swap in swaps:
        swap.wait_recv()
    w_proj_on.wait_recv()
    value = tokens[...].astype(F32)
    for j in range(blocks):
        value = value + dot(mixed[j], proj_full[pl.ds(j * hw, hw), :], 1, 0)
    middle[...] = value
    gain = small_full[pl.ds(5, 1), :].astype(F32)
    normed[...] = (value * rms_scale(value) * gain).astype(BF16)

    def ready(k):
        if k == 0:
            w_down.wait_recv()
            w_up.wait_recv()
        else:
            cots[k, 1].wait_recv()
            cots[k, 3].wait_recv()
        if k == 0:
            cots[0, 1].wait_recv()
            cots[0, 3].wait_recv()

    experts_kernel(
        False,
        normed,
        grads,
        up_full,
        down_full,
        small_full,
        wide,
        back_sum,
        forth_sum,
        dots_sum,
        nall,
        gpre,
        gated,
        *rest,
        ready=ready,
    )

    turned = jnp.transpose(
        jnp.concatenate([dots_sum[...], jnp.zeros((rows - 8, rows), F32)], axis=0)
    )
    chosen = packed[:, pl.ds(width, LANES)].astype(F32) > 0.5
    gates = gates_of(dot(normed[...], small_full[...], 1, 1), chosen)
    grad_logits = gates * (turned - jnp.sum(gates * turned, axis=1, keepdims=True))
    sums = [jnp.zeros((1, width), F32) for _ in range(experts + 1)]
    step = 32
    for m in range(rows // step):
        at = pl.ds(m * step, step)
        parts = [grad_logits[m * step : (m + 1) * step, e : e + 1] for e in range(experts)]
        grad = back_sum[at, :]
        seen = normed[at, :].astype(F32)
        for e in range(experts):
            grad = grad + parts[e] * small_full[pl.ds(e, 1), :].astype(F32)
            sums[e + 1] = sums[e + 1] + jnp.sum(parts[e] * seen, axis=0, keepdims=True)
        mid = middle[at, :]
        size = rms_scale(mid)
        weighted = grad * gain
        sums[0] = sums[0] + jnp.sum(grad * mid * size, axis=0, keepdims=True)
        value = (
            packed[at, pl.ds(0, width)].astype(F32)
            + size * weighted
            - mid * size**3 * jnp.mean(weighted * mid, axis=1, keepdims=True)
        )
        gmiddle[at, :] = value
        gmid_low[at, :] = value.astype(BF16)
    tiles = width // LANES
    fixed[...] = jnp.zeros_like(fixed)
    for n, total in enumerate(sums):
        for c in range(tiles):
            fixed[pl.ds((n + 1) * tiles + c, 1), :] = total[:, c * LANES : (c + 1) * LANES]
    copies = list(ins.values()) + list(cots.values()) + swaps
    copies += w_share + [w_qkv, w_small, w_proj, w_down, w_up, w_proj_on]
    for copy in copies:
        copy.wait_send()


def front_call(scale, experts, heads, hw, *operands):
    tokens, seg_across = operands[0], operands[3]
    rows, width = tokens.shape
    group = seg_across.shape[1]
    spans, hidden = 4, operands[7].shape[0]
    vmem = pl.BlockSpec(memory_space=pltpu.VMEM)
    smem = pl.BlockSpec(memory_space=pltpu.SMEM)
    shape = jax.ShapeDtypeStruct
    dma = pltpu.SemaphoreType.DMA
    outs = (
        shape((group, width), BF16),
        shape((group, 3 * hw), BF16),
        shape((heads, group, group), F32),
        shape((group, hw), BF16),
        shape((rows, width), F32),
        shape((rows, width), BF16),
        shape((width, 3 * hw), BF16),
        shape((width, width), BF16),
        shape((hidden, width), BF16),
        shape((LANES, width), BF16),
        shape((spans, group, width + LANES), BF16),
        shape((rows, width), F32),
        shape((rows, width), BF16),
        shape((8 * width // LANES, LANES), F32),
        shape((spans, group, width), BF16),
        shape((spans, group, hidden), BF16),
        shape((spans, group, hidden), BF16),
    )
    return pl.pallas_call(
        functools.partial(front_kernel, scale, experts),
        out_shape=outs,
        in_specs=[smem if n == 4 else vmem for n in range(len(operands))],
        out_specs=[vmem] * len(outs),
        scratch_shapes=[
            pltpu.VMEM((rows, width), F32),
            pltpu.VMEM((8, rows), F32),
            pltpu.VMEM((group, width), BF16),
            pltpu.VMEM((hidden, width), BF16),
            pltpu.VMEM((2, heads, rows, rows), F32),
            pltpu.VMEM((4, rows, hw), BF16),
            pltpu.VMEM((rows, width + LANES), BF16),
            pltpu.VMEM((group, LANES), jnp.int32),
            pltpu.VMEM((3 * LANES, hidden), BF16),
            dma((1, 4)),
            dma((1, 4)),
            dma((9,)),
            dma((9,)),
            dma((4, 4)),
            dma((4, 4)),
            dma((4,)),
            dma((4,)),
            pltpu.VMEM((8, LANES), F32),
        ]
        + experts_scratch(False, spans, rows, group, width, hidden),
        compiler_params=pltpu.CompilerParams(
            collective_id=2, has_side_effects=True, vmem_limit_bytes=60 * 1024 * 1024
        ),
    )(*operands)


def experts_scratch(forth, spans, rows, group, width, hidden):
    streams = {
        "back": scatter_scratch(spans, BF16, (rows, width), (group, width)),
        "dots": scatter_scratch(spans, F32, (8, rows), (4, 8, rows)),
        "forth": (
            scatter_scratch(spans, BF16, (rows, width), (group, width))
            if forth
            else {"sum": pltpu.SMEM((1,), F32)}
        ),
    }
    return [
        pltpu.VMEM((TILE, hidden), F32),
        pltpu.VMEM((TILE, hidden), F32),
        pltpu.VMEM((TILE, hidden), F32),
        pltpu.VMEM((TILE, hidden), BF16),
        pltpu.VMEM((TILE, hidden), BF16),
        streams,
        pltpu.SemaphoreType.DMA((4, 4)),
        pltpu.SemaphoreType.DMA((4, 4)),
        pltpu.SemaphoreType.DMA((3, 4, 4)),
        pltpu.SemaphoreType.DMA((3, 4, 4)),
    ]


def tail_kernel(
    scale,
    gmid_own,
    probs,
    qkv,
    attended,
    normed,
    wqkv,
    wproj,
    gated,
    gpre,
    nall,
    grads,
    down,
    tokens,
    fixed,
    forth_sum,
    gone_sum,
    gup,
    gdown,
    gwq,
    gwp,
    small,
    wall,
    ptmp,
    vtmp,
    wtmp,
    buckets,
    gmid,
    gatt,
    gqkv,
    gscore,
    wide_up,
    wide_down,
    half_send,
    half_recv,
    wsend,
    wrecv,
    wsum,
    zsend,
    zrecv,
    smalls,
    forth_buf,
    gone_buf,
    msend,
    mrecv,
    fsend,
    frecv,
    osend,
    orecv,
    xsend,
    xrecv,
    wgsend,
    wgrecv,
):
    spots = neighbours()
    f, i, t, sibling, across, along = spots
    peer = (1 - f, i, t)
    rows, width = gmid_own.shape
    spans, group, _ = nall.shape
    heads, hw = probs.shape[0], attended.shape[1]
    head = hw // heads
    own = width // 2
    piece = own // spans
    blocks = group // rows

    def block(index):
        return pl.ds(pl.multiple_of(index * rows, rows), rows)

    def half(index):
        return pl.ds(pl.multiple_of(index * own, LANES), own)

    mids = gather_copies(spots, gmid_own, lambda tt, ii: gmid.at[block(ii), :], msend, mrecv, 1)
    forth_buf["sum"], gone_buf["sum"] = forth_sum, gone_sum
    forth = Scatter(
        spots, forth_buf, lambda k, index: forth_buf["part"].at[k, block(index), :], fsend, frecv
    )
    gone = Scatter(
        spots, gone_buf, lambda k, index: gone_buf["part"].at[k, block(index), :], osend, orecv
    )
    halves = [
        remote(half_send[n], half_recv[n], xsend.at[n], xrecv.at[n], peer) for n in range(2)
    ]
    wx = [
        remote(wsend.at[n], wrecv.at[n], xsend.at[2 + n], xrecv.at[2 + n], peer) for n in range(2)
    ]
    wz = [
        {
            k: remote(
                zsend.at[n, pl.ds(pl.multiple_of(xor(t, k) * piece, 16), piece), :],
                zrecv.at[n, k],
                xsend.at[4 + 3 * n + k - 1],
                xrecv.at[4 + 3 * n + k - 1],
                along[k],
            )
            for k in (1, 2, 3)
        }
        for n in range(2)
    ]
    wg = [
        gather_copies(
            spots,
            wall.at[n, t, i],
            lambda tt, ii, n=n: wall.at[n, tt, ii],
            wgsend.at[n],
            wgrecv.at[n],
        )
        for n in range(2)
    ]
    steps = [
        remote(smalls.at[n], smalls.at[3 + n], xsend.at[10 + n], xrecv.at[10 + n], target)
        for n, target in enumerate((sibling, across, peer))
    ]
    rounds = [
        remote(small, smalls.at[5 + k], xsend.at[12 + k], xrecv.at[12 + k], along[k])
        for k in (1, 2, 3)
    ]

    greet([sibling, across, peer] + along[1:])
    gmid[block(i), :] = gmid_own[...]
    mids[0, 2].start()
    mids[0, 1].start()
    apart = lax.broadcasted_iota(jnp.int32, (rows, rows), 0) - lax.broadcasted_iota(
        jnp.int32, (rows, rows), 1
    )
    for n in range(2):
        value = jnp.where(apart + n * rows >= 0, 0, -1)
        for bound in BOUNDS:
            value = value + jnp.where(apart + n * rows >= bound, 1, 0)
        buckets[n] = value

    def forth_part(k):
        tk = xor(t, k)

        def tile(m, carry):
            at = pl.ds(pl.multiple_of(m * TILE, TILE), TILE)
            forth_buf["part"][k, at, :] = dot(gated[tk, at, :], down[...], 1, 0).astype(BF16)
            return carry

        lax.fori_loop(0, group // TILE, tile, 0)
        forth.first(k)

    def up_half(which, out):
        out[...] = jnp.zeros_like(out)

        def step(c, carry):
            out[...] += dot(nall[c, :, half(which)], gpre[c], 0, 0)
            return carry

        lax.fori_loop(0, spans, step, 0)

    def down_half(which, out):
        out[...] = jnp.zeros_like(out)

        def step(c, carry):
            out[...] += dot(gated[c], grads[c, :, half(which)], 0, 0)
            return carry

        lax.fori_loop(0, spans, step, 0)

    forth_part(1)
    forth_part(2)
    mids[0, 2].wait_recv()
    mids[0, 3].start()
    down_half(1 - f, wide_down)
    half_send[0][...] = wide_down[...].astype(BF16)
    halves[0].start()
    forth.second(1)
    forth_part(3)
    forth_part(0)
    forth.second(2)
    mids[0, 1].wait_recv()
    mids[0, 3].wait_recv()

    here = wproj[pl.ds(pl.multiple_of(i * hw, 16), hw), :]
    gatt[...] = dot(gmid[...], here, 1, 1).astype(BF16)
    ptmp[...] = dot(attended[...], gmid[...], 0, 0)
    for h in range(heads):
        cols = pl.ds(h * head, head)
        gqkv[:, pl.ds(2 * hw + h * head, head)] = dot(
            probs[h].astype(BF16), gatt[:, cols], 0, 0
        ).astype(BF16)
    vtmp[...] = dot(normed[...], gqkv[:, pl.ds(2 * hw, hw)], 0, 0)
    low, part = piece // 2, hw // spans
    for side, out in ((1 - f, wsend), (f, wsum)):
        for n in range(spans):
            out[0, pl.ds(n * piece, part), :] = ptmp[pl.ds(n * part, part), half(side)].astype(
                out.dtype
            )
            for e in range(2):
                start = pl.multiple_of(side * own + n * piece + e * low, 16)
                out[0, pl.ds(n * piece + part, low), pl.ds(e * hw, hw)] = vtmp[
                    pl.ds(start, low), :
                ].astype(out.dtype)
    wx[0].start()
    forth.second(3)
    forth.second(0)
    forth.third(1)

    table = small.at[pl.ds(0, heads * BUCKETS), :]
    def reduce_along(n):
        wx[n].wait_recv()
        total = wsum[n] + wrecv[n].astype(F32)
        wsum[n] = total
        zsend[n] = total.astype(BF16)
        for k in (1, 2, 3):
            wz[n][k].start()

    def share(n):
        total = wsum[n, pl.ds(pl.multiple_of(t * piece, 16), piece), :]
        for k in (1, 2, 3):
            wz[n][k].wait_recv()
            total = total + zrecv[n, k].astype(F32)
        wall[n, t, i] = total.astype(BF16)
        wg[n][0, 2].start()
        wg[n][0, 1].start()
        for k in (1, 2, 3):
            wg[n][k, 0].start()

    def onward(n):
        for k in (1, 2, 3):
            wg[n][k, 0].wait_recv()
            wg[n][k, 2].start()
            wg[n][k, 1].start()

    def relay(n):
        for k in range(4):
            wg[n][k, 2].wait_recv()
            wg[n][k, 3].start()

    for h in range(heads):
        cols = pl.ds(h * head, head)
        keys = pl.ds(hw + h * head, head)

        def rowtile(m, carry, h=h, cols=cols, keys=keys):
            at = block(m)
            grad_probs = dot(gatt[at, cols], qkv[:, pl.ds(2 * hw + h * head, head)], 1, 1)
            prob = probs[h, at, :]
            inner = jnp.sum(prob * grad_probs, axis=1, keepdims=True)
            score = (prob * (grad_probs - inner)).astype(BF16)
            gscore[h, at, :] = score
            gqkv[at, cols] = (dot(score, qkv[:, keys], 1, 0) * scale).astype(BF16)
            return carry

        lax.fori_loop(0, blocks, rowtile, 0)
        gqkv[:, keys] = (dot(gscore[h], qkv[:, cols], 0, 0) * scale).astype(BF16)
        if h == 0:
            forth.third(2)
        if h == 1:
            forth.third(3)

    def gone_tile(m, carry):
        at = block(m)
        gone_buf["part"][0, at, :] = dot(gqkv[at, :], wqkv[...], 1, 1).astype(BF16)
        return carry

    lax.fori_loop(0, blocks, gone_tile, 0)
    gone.first(0)
    wtmp[...] = dot(normed[...], gqkv[:, pl.ds(0, 2 * hw)], 0, 0)
    wsend[1] = wtmp[half(1 - f), :].astype(BF16)
    wsum[1] = wtmp[half(f), :]
    wx[1].start()
    gone.second(0)
    up_half(1 - f, wide_up)
    half_send[1][...] = wide_up[...].astype(BF16)
    halves[1].start()
    reduce_along(0)
    forth.third(0)

    def bucket_sums(h):
        near = jnp.zeros((rows, rows), F32)
        after = jnp.zeros((rows, rows), F32)
        far = jnp.zeros((rows, rows), F32)
        for a in range(blocks):
            for b in range(a + 1):
                score = gscore[h, pl.ds(a * rows, rows), pl.ds(b * rows, rows)].astype(F32)
                if a == b:
                    near = near + score
                elif a == b + 1:
                    after = after + score
                else:
                    far = far + score
        sums = []
        for b in range(BUCKETS):
            value = jnp.where(buckets[0] == b, near, 0.0) + jnp.where(
                buckets[1] == b, after, 0.0
            )
            if b == BUCKETS - 1:
                value = value + far
            sums.append(jnp.sum(value, axis=0, keepdims=True))
        sums = jnp.sum(jnp.concatenate(sums, axis=0), axis=1, keepdims=True)
        lane = lax.broadcasted_iota(jnp.int32, (BUCKETS, LANES), 1)
        smalls[0, pl.ds(h * BUCKETS, BUCKETS), :] = jnp.where(lane == i, sums, 0.0)

    for h in range(heads):
        bucket_sums(h)
    gone.third(0)
    value = tokens[...].astype(F32)
    gain = jnp.sum(gone_sum[...] * (value * rms_scale(value)), axis=0, keepdims=True)
    base = heads * BUCKETS
    smalls[0, pl.ds(base, smalls.shape[1] - base), :] = fixed[...]
    for c in range(width // LANES):
        smalls[0, pl.ds(base + c, 1), :] = gain[:, c * LANES : (c + 1) * LANES]
    share(0)
    steps[0].start()
    down_half(f, gdown)
    reduce_along(1)
    up_half(f, wide_up)
    steps[0].wait_recv()
    smalls[1] = smalls[0] + smalls[3]
    steps[1].start()
    onward(0)
    share(1)
    steps[1].wait_recv()
    smalls[2] = smalls[1] + smalls[4]
    steps[2].start()
    relay(0)
    steps[2].wait_recv()
    small[...] = smalls[2] + smalls[5]
    for copy in rounds:
        copy.start()
    onward(1)
    forth.last()
    relay(1)
    for copy in rounds:
        copy.wait()
    small[...] = small[...] + smalls[6] + smalls[7] + smalls[8]
    halves[0].wait_recv()
    gdown[...] = gdown[...] + half_recv[0][...].astype(F32)
    halves[1].wait_recv()
    units = gup.shape[2]
    for e in range(gup.shape[0]):
        cols = pl.ds(e * units, units)
        gup[e] = wide_up[:, cols] + half_recv[1][:, cols].astype(F32)
    for n in range(2):
        for k in range(4):
            wg[n][k, 1].wait_recv()
            wg[n][k, 3].wait_recv()
    for n in range(spans):
        for c in range(blocks):
            gwp[pl.ds(c * hw + n * part, part), :] = wall[0, n, c, pl.ds(0, part), :]
            for e in range(2):
                gwq[pl.ds(n * piece + e * low, low), pl.ds(2 * width + c * hw, hw)] = wall[
                    0, n, c, pl.ds(part, low), pl.ds(e * hw, hw)
                ]
                gwq[pl.ds(n * piece, piece), pl.ds(e * width + c * hw, hw)] = wall[
                    1, n, c, :, pl.ds(e * hw, hw)
                ]
    copies = halves + wx + steps + list(mids.values())
    copies += list(forth.copies.values()) + list(gone.copies.values())
    for n in range(2):
        copies += list(wz[n].values()) + list(wg[n].values())
    for copy in copies:
        copy.wait_send()


def tail_call(scale, experts, *operands):
    gmid, probs, qkv, attended, normed, wqkv, wproj, gated, gpre, nall = operands[:10]
    rows, width = gmid.shape
    spans, group, hidden = gpre.shape
    heads = probs.shape[0]
    hw = attended.shape[1]
    own = width // 2
    piece = own // spans
    extra = 8 * width // LANES
    vmem = pl.BlockSpec(memory_space=pltpu.VMEM)
    shape = jax.ShapeDtypeStruct
    dma = pltpu.SemaphoreType.DMA
    table = heads * BUCKETS + extra
    return pl.pallas_call(
        functools.partial(tail_kernel, scale),
        out_shape=(
            shape((rows, width), F32),
            shape((rows, width), F32),
            shape((experts, own, hidden // experts), F32),
            shape((hidden, own), F32),
            shape((own, 3 * width), BF16),
            shape((width, own), BF16),
            shape((table, LANES), F32),
        ),
        in_specs=[vmem] * len(operands),
        out_specs=[vmem] * 7,
        scratch_shapes=[
            pltpu.VMEM((2, spans, 4, piece, 2 * hw), BF16),
            pltpu.VMEM((hw, width), F32),
            pltpu.VMEM((width, hw), F32),
            pltpu.VMEM((width, 2 * hw), F32),
            pltpu.VMEM((2, rows, rows), jnp.int32),
            pltpu.VMEM((group, width), BF16),
            pltpu.VMEM((group, hw), BF16),
            pltpu.VMEM((group, 3 * hw), BF16),
            pltpu.VMEM((heads, group, group), BF16),
            pltpu.VMEM((own, hidden), F32),
            pltpu.VMEM((hidden, own), F32),
            [pltpu.VMEM((hidden, own), BF16), pltpu.VMEM((own, hidden), BF16)],
            [pltpu.VMEM((hidden, own), BF16), pltpu.VMEM((own, hidden), BF16)],
            pltpu.VMEM((2, own, 2 * hw), BF16),
            pltpu.VMEM((2, own, 2 * hw), BF16),
            pltpu.VMEM((2, own, 2 * hw), F32),
            pltpu.VMEM((2, own, 2 * hw), BF16),
            pltpu.VMEM((2, 4, piece, 2 * hw), BF16),
            pltpu.VMEM((9, table, LANES), F32),
            scatter_scratch(spans, BF16, (rows, width), (group, width)),
            scatter_scratch(1, BF16, (rows, width), (group, width)),
            dma((1, 4)),
            dma((1, 4)),
            dma((spans, 4)),
            dma((spans, 4)),
            dma((1, 4)),
            dma((1, 4)),
            dma((16,)),
            dma((16,)),
            dma((2, 4, 4)),
            dma((2, 4, 4)),
        ],
        compiler_params=pltpu.CompilerParams(
            collective_id=1, has_side_effects=True, vmem_limit_bytes=58 * 1024 * 1024
        ),
    )(*operands)


def local(
    tokens,
    seg_ids,
    routes,
    norm_attn,
    weight_qkv,
    weight_proj,
    rel_table,
    norm_ffn,
    weight_router,
    expert_up,
    expert_down,
    cotangent,
):
    rows = tokens.shape[1]
    width = tokens.shape[2]
    heads = rel_table.shape[0]
    head_size = width // heads
    ctx_count = lax.axis_size("ctx")
    heads_here = heads // ctx_count
    hw = heads_here * head_size
    experts = expert_up.shape[0]
    units = expert_up.shape[2]
    length = seg_ids.shape[1]
    score_scale = head_size ** (-0.5)
    ctx_index = lax.axis_index("ctx")
    fsdp_index = lax.axis_index("fsdp")
    own_width = norm_attn.shape[0]
    world = ("ctx", "tp")

    tp_count = lax.axis_size("tp")
    pair = lax.axis_size("fsdp") == 2
    segment = seg_ids[0]
    inputs = tokens[0].astype(F32)
    scale_one = rms_scale(inputs)
    qkv_part = jnp.concatenate(
        [
            lax.dynamic_slice_in_dim(weight_qkv, s * width + ctx_index * hw, hw, 1)
            for s in range(3)
        ],
        axis=1,
    )
    expert_ids = jnp.arange(LANES, dtype=jnp.int32)[None, :]
    named = (routes[0][:, 0:1] == expert_ids) | (routes[0][:, 1:2] == expert_ids)
    packed_grad = jnp.concatenate([cotangent[0], named.astype(BF16)], axis=1)
    block = MAX_DISTANCE
    offset = (
        lax.broadcasted_iota(jnp.int32, (1, block, block), 1)
        - lax.broadcasted_iota(jnp.int32, (1, block, block), 2)
    )

    hidden = experts * units
    wide = (
        jnp.arange(hidden, dtype=jnp.int32)[None, :] // units
        == jnp.arange(3 * LANES, dtype=jnp.int32)[:, None] % LANES
    ).astype(BF16)
    if pair:
        up_part = jnp.swapaxes(expert_up, 1, 2).reshape(hidden, own_width)
        small_part = jnp.concatenate(
            [
                weight_router.T,
                norm_attn[None],
                norm_ffn[None],
                jnp.zeros((14 - experts, own_width), BF16),
            ],
            axis=0,
        )
        (
            normed_group,
            projected,
            probs,
            attended,
            middle,
            normed_two,
            qkv_here,
            proj_full,
            down,
            small,
            grads_all,
            grad_middle,
            grad_mid_low,
            fixed,
            normed_all,
            grad_pre,
            gated,
        ) = front_call(
            score_scale,
            experts,
            heads_here,
            hw,
            tokens[0],
            cotangent[0],
            routes[0],
            seg_ids,
            rel_table,
            qkv_part,
            weight_proj,
            up_part,
            expert_down.reshape(hidden, own_width),
            small_part,
        )
        gain_one = small[experts].astype(F32)
    else:
        token_group = lax.all_gather(tokens[0], "ctx", axis=0, tiled=True)
        small = jnp.concatenate([norm_attn[None], norm_ffn[None], weight_router.T], axis=0)
        small = gather(small, "fsdp", 1)
        gain_one = small[0].astype(F32)
        gain_two = small[1].astype(F32)
        router_t = small[2:]
        qkv_here = gather(qkv_part, "fsdp", 0)
        proj_full = gather(weight_proj, "fsdp", 1)
        up_t = gather(
            jnp.swapaxes(expert_up, 1, 2).reshape(experts * units, own_width), "fsdp", 1
        )
        down = gather(expert_down.reshape(experts * units, own_width), "fsdp", 1)
        grad_routes = lax.all_gather(packed_grad, ("tp", "ctx"), axis=0, tiled=True)

        table_here = lax.dynamic_slice_in_dim(rel_table, ctx_index * heads_here, heads_here, 0)
        def bias_block(distance):
            value = jnp.broadcast_to(table_here[:, 0][:, None, None], (heads_here, block, block))
            for number, bound in enumerate(BOUNDS, 1):
                value = jnp.where(distance >= bound, table_here[:, number][:, None, None], value)
            return value

        near = bias_block(offset)
        next_near = bias_block(offset + block)
        far = jnp.broadcast_to(table_here[:, BUCKETS - 1][:, None, None], (heads_here, block, block))
        blocks = length // block
        picks = {0: near, 1: next_near}
        bias = jnp.concatenate(
            [
                jnp.concatenate(
                    [picks.get(i - j, far) for j in range(blocks)],
                    axis=2,
                )
                for i in range(blocks)
            ],
            axis=1,
        )
        positions = jnp.arange(length, dtype=jnp.int32)
        allowed = (segment[:, None] == segment[None, :]) & (positions[:, None] >= positions[None, :])
        bias = jnp.where(allowed[None], bias, MASK_FILL)

        inputs_group = token_group.astype(F32)
        normed_group = (inputs_group * rms_scale(inputs_group) * gain_one).astype(BF16)
        projected = dot(normed_group, qkv_here, 1, 0).astype(BF16)
        by_head = projected.reshape(length, 3, heads_here, head_size)
        query, key, value = by_head[:, 0], by_head[:, 1], by_head[:, 2]

        scores = (
            jnp.einsum("qhd,khd->hqk", query, key, preferred_element_type=F32) * score_scale + bias
        )
        peak = jnp.max(scores, axis=-1, keepdims=True)
        weights = jnp.exp(scores - peak)
        probs = weights / jnp.sum(weights, axis=-1, keepdims=True)
        low_probs = probs.astype(BF16)
        attended = (
            jnp.einsum("hqk,khd->qhd", low_probs, value, preferred_element_type=F32)
            .astype(BF16)
            .reshape(length, hw)
        )
        mixed = lax.all_to_all(attended, "ctx", split_axis=0, concat_axis=1, tiled=True)
        mixed, grad_routes, up_t, down = lax.optimization_barrier((mixed, grad_routes, up_t, down))
        middle = inputs + dot(mixed, proj_full, 1, 0)
        scale_two = rms_scale(middle)
        normed_two = (middle * scale_two * gain_two).astype(BF16)

        router_pad = jnp.pad(router_t, ((0, LANES - experts), (0, 0)))
        grad_normed_two, result, dots_own, normed_all, grad_pre, gated = experts_call(
            True,
            normed_two,
            grad_routes.reshape(tp_count, length, width + LANES),
            up_t,
            down,
            router_pad,
            wide,
        )
    if pair:
        result, grad_normed_one, grad_up, grad_down, grad_qkv, grad_proj, packed = tail_call(
            score_scale,
            experts,
            grad_mid_low,
            probs,
            projected,
            attended,
            normed_group,
            qkv_here,
            proj_full,
            gated,
            grad_pre,
            normed_all,
            grads_all,
            down,
            tokens[0],
            fixed,
        )
        output = (middle + result).astype(BF16)[None]
        weighted_one = grad_normed_one * gain_one
        grad_tokens = (
            grad_middle
            + scale_one * weighted_one
            - inputs * scale_one**3 * jnp.mean(weighted_one * inputs, axis=1, keepdims=True)
        )
        grad_down = grad_down.reshape(experts, units, own_width)
        edge = heads_here * BUCKETS
        table_grad = packed[:edge, :ctx_count].T.reshape(heads, BUCKETS)
        gains = packed[edge:].reshape(-1, width)
        gains = lax.dynamic_slice_in_dim(gains, fsdp_index * own_width, own_width, 1)
        return (
            output,
            grad_tokens[None],
            gains[0],
            grad_qkv.astype(F32),
            grad_proj.astype(F32),
            table_grad,
            gains[1],
            gains[2 : 2 + experts].T,
            grad_up,
            grad_down,
        )
    gate_dots = dots_own[:experts].T
    total_rows = tp_count * length
    grad_out = cotangent[0].astype(F32)
    number = jnp.arange(experts, dtype=jnp.int32)[None, :]
    chosen = (routes[0][:, 0:1] == number) | (routes[0][:, 1:2] == number)
    gates = gates_of(dot(normed_two, router_t, 1, 1), chosen)
    grad_logits = gates * (gate_dots - jnp.sum(gates * gate_dots, axis=1, keepdims=True))
    grad_normed_two = grad_normed_two + jnp.dot(
        grad_logits, router_t.astype(F32), precision=lax.Precision.HIGHEST
    )
    grad_router = lax.dot_general(
        grad_logits,
        normed_two.astype(F32),
        (((0,), (0,)), ((), ())),
        precision=lax.Precision.HIGHEST,
    )
    weighted_two = grad_normed_two * gain_two
    grad_gain_two = jnp.sum(grad_normed_two * middle * scale_two, axis=0)
    grad_middle = (
        grad_out
        + scale_two * weighted_two
        - middle * scale_two**3 * jnp.mean(weighted_two * middle, axis=1, keepdims=True)
    )
    normed_all = normed_all.reshape(total_rows, width)
    grad_pre = grad_pre.reshape(total_rows, hidden)
    gated = gated.reshape(total_rows, hidden)
    grad_all = grad_routes[:, :width]
    grad_up = exchange_sum(dot(grad_pre, normed_all, 0, 0), "fsdp", 1)
    grad_up = jnp.swapaxes(grad_up.reshape(experts, units, own_width), 1, 2)
    grad_down = exchange_sum(dot(gated, grad_all, 0, 0), "fsdp", 1)
    grad_down = grad_down.reshape(experts, units, own_width)

    grad_mid_group = lax.all_gather(grad_middle.astype(BF16), "ctx", axis=0, tiled=True)
    proj_rows = lax.dynamic_slice_in_dim(proj_full, ctx_index * hw, hw, 0)
    grad_attended = dot(grad_mid_group, proj_rows, 1, 1).astype(BF16)
    grad_heads = grad_attended.reshape(length, heads_here, head_size)
    grad_value = jnp.einsum("hqk,qhd->khd", low_probs, grad_heads, preferred_element_type=F32)
    grad_probs = jnp.einsum("qhd,khd->hqk", grad_heads, value, preferred_element_type=F32)
    grad_scores = (
        probs * (grad_probs - jnp.sum(probs * grad_probs, axis=-1, keepdims=True))
    ).astype(BF16)
    grad_query = (
        jnp.einsum("hqk,khd->qhd", grad_scores, key, preferred_element_type=F32) * score_scale
    )
    grad_key = (
        jnp.einsum("hqk,qhd->khd", grad_scores, query, preferred_element_type=F32) * score_scale
    )
    grad_qkv = jnp.concatenate(
        [
            grad_query.astype(BF16).reshape(length, hw),
            grad_key.astype(BF16).reshape(length, hw),
            grad_value.astype(BF16).reshape(length, hw),
        ],
        axis=1,
    )
    grad_normed_one = exchange_sum(dot(grad_qkv, qkv_here, 1, 1), "ctx", 0)

    weight_part = jnp.concatenate(
        [dot(normed_group, grad_qkv, 0, 0), dot(grad_mid_group, attended, 0, 0)], axis=1
    )
    weight_own = exchange_sum(weight_part, "fsdp", 0)
    grad_scores, weight_own = lax.optimization_barrier((grad_scores, weight_own))
    weight_own = exchange_sum(weight_own, "tp", 0).astype(BF16)
    def score_block(i, j):
        return grad_scores[
            :, i * block : (i + 1) * block, j * block : (j + 1) * block
        ].astype(F32)

    near_sum = sum(score_block(i, i) for i in range(blocks))
    next_sum = sum(score_block(i + 1, i) for i in range(blocks - 1))
    far_sum = sum(
        jnp.sum(score_block(i, j), axis=(1, 2)) for i in range(blocks) for j in range(i - 1)
    )
    lows = [0] + BOUNDS
    highs = BOUNDS + [2 * block]
    bucket_sums = [
        jnp.sum(jnp.where((offset >= lo) & (offset < hi), near_sum, 0.0), axis=(1, 2))
        + jnp.sum(
            jnp.where((offset + block >= lo) & (offset + block < hi), next_sum, 0.0), axis=(1, 2)
        )
        for lo, hi in zip(lows, highs)
    ]
    bucket_sums[-1] = bucket_sums[-1] + far_sum
    table_here_grad = jnp.stack(bucket_sums, axis=1)
    table_term = lax.dynamic_update_slice_in_dim(
        jnp.zeros((heads, BUCKETS), F32), table_here_grad, ctx_index * heads_here, 0
    )

    weighted_one = grad_normed_one * gain_one
    grad_gain_one = jnp.sum(grad_normed_one * inputs * scale_one, axis=0)
    grad_tokens = (
        grad_middle
        + scale_one * weighted_one
        - inputs * scale_one**3 * jnp.mean(weighted_one * inputs, axis=1, keepdims=True)
    )
    packed = jnp.concatenate(
        [
            grad_gain_one,
            grad_gain_two,
            grad_router.reshape(-1),
            table_term.reshape(-1),
        ]
    ).reshape(-1, 128)
    packed, weight_own = lax.optimization_barrier((packed, weight_own))
    packed = lax.psum(packed, ("fsdp", "ctx", "tp")).reshape(-1)
    packed, result = lax.optimization_barrier((packed, result))
    output = (middle + result).astype(BF16)[None]
    weight_all = lax.all_gather(weight_own, world, axis=0, tiled=True).astype(F32)
    weight_all = weight_all.reshape(ctx_count, own_width, 4 * hw)
    grad_weight_qkv = jnp.concatenate(
        [
            weight_all[c, :, s * hw : (s + 1) * hw]
            for s in range(3)
            for c in range(ctx_count)
        ],
        axis=1,
    )
    grad_weight_proj = jnp.swapaxes(weight_all[:, :, 3 * hw :], 1, 2).reshape(width, own_width)
    gains = packed[: (2 + experts) * width].reshape(2 + experts, width)
    gains = lax.dynamic_slice_in_dim(gains, fsdp_index * own_width, own_width, 1)
    table_grad = packed[(2 + experts) * width :].reshape(heads, BUCKETS)
    return (
        output,
        grad_tokens[None],
        gains[0],
        grad_weight_qkv,
        grad_weight_proj,
        table_grad,
        gains[1],
        gains[2:].T,
        grad_up,
        grad_down,
    )


def solution(mesh):
    rows = P(("fsdp", "tp"), "ctx", None)
    in_specs = (
        rows,
        P(("fsdp", "tp"), None),
        rows,
        P("fsdp"),
        P("fsdp", None),
        P(None, "fsdp"),
        P(),
        P("fsdp"),
        P("fsdp", None),
        P(None, "fsdp", ("ctx", "tp")),
        P(None, ("ctx", "tp"), "fsdp"),
        rows,
    )
    out_specs = (
        rows,
        rows,
        P("fsdp"),
        P("fsdp", None),
        P(None, "fsdp"),
        P(),
        P("fsdp"),
        P("fsdp", None),
        P(None, "fsdp", ("ctx", "tp")),
        P(None, ("ctx", "tp"), "fsdp"),
    )
    return jax.shard_map(local, mesh=mesh, in_specs=in_specs, out_specs=out_specs, check_vma=False)
```
